32 devices in a mesh: groups: 2 (over y), tensor: 4 (over x, core), task: 4 (over z).
Axes of the slice: x: 2, y: 2, z: 4, core: 2. Of those that a mesh axis runs over, the one named last changes fastest.
Arguments:
- tokens: bfloat16 [3072, 8192], P(('groups', 'task'), 'tensor'), parts along dimension 0, may hold values from -6 to 6
- task_counts: int32 [512], P(('groups', 'task')), parts along dimension 0, may hold values from 0 to 96, as said below
- task_embeddings: bfloat16 [512, 1024], P(('groups', 'task')), parts along dimension 0, may hold values from -6 to 6
- embedding_weight: bfloat16 [1024, 512], replicated, may hold values from -0.1875 to 0.1875
- down_factor_head: bfloat16 [512, 16, 8192], P('task', None, 'tensor'), may hold values from -0.0029296875 to 0.0029296875
- query_up_head: bfloat16 [512, 8, 4096], P('task', None, 'tensor'), may hold values from -0.09375 to 0.09375
- value_up_head: bfloat16 [512, 8, 1024], P('task', None, 'tensor'), may hold values from -0.09375 to 0.09375
- w_query: bfloat16 [8192, 4096], P('tensor'), may hold values from -0.0625 to 0.0625
- w_value: bfloat16 [8192, 1024], P('tensor'), may hold values from -0.0625 to 0.0625
Outputs:
- query: bfloat16 [3072, 4096], P(('groups', 'task', 'tensor')), parts along dimension 0
- value: bfloat16 [3072, 1024], P(('groups', 'task', 'tensor')), parts along dimension 0
- down_factors: bfloat16 [512, 16, 8192], P(('groups', 'task'), None, 'tensor'), parts along dimension 0
- query_up_factors: bfloat16 [512, 8, 4096], P(('groups', 'task'), None, 'tensor'), parts along dimension 0
- value_up_factors: bfloat16 [512, 8, 1024], P(('groups', 'task'), None, 'tensor'), parts along dimension 0
The draws below stay inside these ranges and needn't reach their ends.
There are 2 independent parts, one for each index of `groups`. The reference program is written for one: setup_inputs(seed, part) draws one part's arguments, and reference() takes and returns one part's arrays. A program takes and returns all parts, laid end to end along the dimension named above; an argument that names none is the same for every part. Nothing has to cross between parts.
Inputs may be any that keep to these rules, and one draw needn't show every extreme that they name: For every k the task_counts of tasks k * 16 to k * 16 + 15 sum to at most 96; in every draw at least one task has exactly 96 tokens.
All inputs are finite; a program needn't handle non-finite values.
Results may differ from the reference program's by a relative error of at most 0.0059.
Values may be sent and summed in bfloat16 or wider, within the bound.
No kernel may reach another device: no remote copies, remote signals or barrier semaphores. Data moves between devices by JAX's collectives and lax.ppermute only.
A program may use at most 128 MiB of HBM per device.

```python
import jax
import jax.numpy as jnp
from jax import lax

MODEL_WIDTH = 8192
VALUE_WIDTH = 1024
QUERY_FEATURES = 4096
ADAPTER_RANK = 8
E = 1024
H = 512
NTASK = 256
TOKENS = 1536
BLOCK_ROWS = 96
TASKS_PER_BLOCK = 16


def draw_task_counts(key, part):
    groups = NTASK // TASKS_PER_BLOCK
    keys = jax.random.split(key, 5)
    selected_factors = jax.random.randint(keys[0], (groups,), 0, TASKS_PER_BLOCK)
    marker = (jnp.arange(TASKS_PER_BLOCK)[None, :] == selected_factors[:, None]).astype(jnp.int32)
    served = jnp.maximum(jax.random.randint(keys[1], (groups, TASKS_PER_BLOCK), 0, 2), marker)
    full_group = jax.random.randint(keys[2], (), 0, groups)
    is_full = jnp.arange(groups) == full_group
    served = jnp.where(is_full[:, None], marker, served)
    weights = served * jax.random.randint(keys[3], (groups, TASKS_PER_BLOCK), 1, 9)
    lowest = max(1, BLOCK_ROWS // 8)
    totals = jax.random.randint(keys[4], (groups,), lowest, BLOCK_ROWS + 1)
    totals = jnp.where(is_full, BLOCK_ROWS, totals)
    shares = totals[:, None] * weights // jnp.sum(weights, axis=1, keepdims=True)
    shares = shares + marker * (totals - jnp.sum(shares, axis=1))[:, None]
    return shares.reshape(NTASK).astype(jnp.int32)


def block_scale(rng, extent, cuts, least, largest):
    loudness = 1.0
    for dim, blocks in cuts:
        draws = jax.random.uniform(jax.random.fold_in(jax.random.fold_in(rng, 6), dim), (blocks,), jnp.float32, least / len(cuts), largest / len(cuts))
        loudness = loudness * jnp.repeat(jnp.exp(draws), extent[dim] // blocks).reshape((-1,) + (1,) * (len(extent) - 1 - dim))
    return loudness


def centred(rng, extent, deviation, most, cuts=(), kind=jnp.bfloat16):
    array = jax.random.normal(rng, extent, jnp.float32) * deviation
    if len(cuts) > 0:
        array = block_scale(rng, extent, cuts, -0.22, 0.18) * array
    return jnp.clip(array, min=-most, max=most).astype(kind)


def setup_inputs(seed: int = 0, part: int = 0) -> dict:
    splits = jax.random.split(jax.random.key(seed), 10)
    own_keys = jax.random.split(jax.random.fold_in(splits[9], part), 10)
    tokens = centred(own_keys[0], (TOKENS, MODEL_WIDTH), 1.0, 6.0, ((0, 4), (1, 4)))
    task_counts = draw_task_counts(jax.random.fold_in(jax.random.fold_in(splits[9], part), 71), part)
    task_embeddings = centred(own_keys[2], (NTASK, E), 1.0, 6.0, ((0, 4),))
    embedding_weight = centred(splits[3], (E, H), E ** -0.5, 0.1875)
    down_factor_head = centred(splits[4], (H, 2 * ADAPTER_RANK, MODEL_WIDTH), (H * MODEL_WIDTH) ** -0.5, 0.0029296875, ((0, 4), (2, 4)))
    query_up_head = centred(splits[5], (H, ADAPTER_RANK, QUERY_FEATURES), (H * ADAPTER_RANK) ** -0.5, 0.09375, ((0, 4), (2, 4)))
    value_up_head = centred(splits[6], (H, ADAPTER_RANK, VALUE_WIDTH), (H * ADAPTER_RANK) ** -0.5, 0.09375, ((0, 4), (2, 4)))
    w_query = centred(splits[7], (MODEL_WIDTH, QUERY_FEATURES), MODEL_WIDTH ** -0.5, 0.0625, ((0, 4),))
    w_value = centred(splits[8], (MODEL_WIDTH, VALUE_WIDTH), MODEL_WIDTH ** -0.5, 0.0625, ((0, 4),))
    return dict(tokens=tokens, task_counts=task_counts, task_embeddings=task_embeddings, embedding_weight=embedding_weight, down_factor_head=down_factor_head, query_up_head=query_up_head, value_up_head=value_up_head, w_query=w_query, w_value=w_value)


ADAPTER_SCALE = 2.0


def produce_head(hypernet_hidden, matrix):
    flattened = jnp.dot(hypernet_hidden, matrix.reshape(matrix.shape[0], -1), preferred_element_type=jnp.float32)
    return flattened.astype(jnp.bfloat16).reshape(hypernet_hidden.shape[0], matrix.shape[1], matrix.shape[2])


def reference(tokens, task_counts, task_embeddings, embedding_weight, down_factor_head, query_up_head, value_up_head, w_query, w_value):
    hypernet_hidden = jax.nn.silu(jnp.dot(task_embeddings, embedding_weight, preferred_element_type=jnp.float32)).astype(jnp.bfloat16)
    down_factors = produce_head(hypernet_hidden, down_factor_head)
    query_up_factors = produce_head(hypernet_hidden, query_up_head)
    value_up_factors = produce_head(hypernet_hidden, value_up_head)
    token_blocks = TOKENS // BLOCK_ROWS
    tallies = task_counts.reshape(token_blocks, TASKS_PER_BLOCK)
    finish = jnp.cumsum(tallies, axis=1)
    starts = finish - tallies
    positions = jnp.arange(BLOCK_ROWS, dtype=jnp.int32)
    member = ((positions[None, :, None] >= starts[:, None, :]) & (positions[None, :, None] < finish[:, None, :])).astype(jnp.float32)
    base_product = jnp.concatenate((jnp.dot(tokens, w_query, preferred_element_type=jnp.float32), jnp.dot(tokens, w_value, preferred_element_type=jnp.float32)), axis=1)
    stretches = tokens.reshape(token_blocks, BLOCK_ROWS, MODEL_WIDTH).astype(jnp.float32)
    task_adapters = down_factors.reshape(token_blocks, TASKS_PER_BLOCK, 2 * ADAPTER_RANK, MODEL_WIDTH).astype(jnp.float32)
    projected = jnp.einsum("bpd,bmrd->bpmr", stretches, task_adapters, precision=lax.Precision.HIGHEST)
    selected_factors = projected * member[..., None]
    query_up_factor = query_up_factors.reshape(token_blocks, TASKS_PER_BLOCK, ADAPTER_RANK, QUERY_FEATURES).astype(jnp.float32)
    value_up_factor = value_up_factors.reshape(token_blocks, TASKS_PER_BLOCK, ADAPTER_RANK, VALUE_WIDTH).astype(jnp.float32)
    delta_query = jnp.einsum("osxe,oxea->osa", selected_factors[..., :ADAPTER_RANK], query_up_factor, precision=lax.Precision.HIGHEST)
    delta_value = jnp.einsum("osxe,oxea->osa", selected_factors[..., ADAPTER_RANK:], value_up_factor, precision=lax.Precision.HIGHEST)
    adapter_update = jnp.concatenate((delta_query, delta_value), axis=2).reshape(TOKENS, QUERY_FEATURES + VALUE_WIDTH)
    combined_output = base_product + ADAPTER_SCALE * adapter_update
    return (combined_output[:, :QUERY_FEATURES].astype(jnp.bfloat16), combined_output[:, QUERY_FEATURES:].astype(jnp.bfloat16), down_factors, query_up_factors, value_up_factors)
```

```python
import functools

import jax
import jax.numpy as jnp
from jax import lax
from jax.experimental import pallas as pl
from jax.experimental.pallas import tpu as pltpu
from jax.sharding import PartitionSpec as P

ADAPTER_SCALE = 2.0
LANES = 128
PLACES = ("groups", "task")


def swap(x, axes, shift):
    total = lax.axis_size(axes)
    return lax.ppermute(x, axes, [(a, a ^ shift) for a in range(total)])


def place():
    return lax.axis_index("groups") * lax.axis_size("task") + lax.axis_index("task")


def cut_kernel(shifts, stride, start, width, source, *rest):
    pieces, sems = rest[:-1], rest[-1]
    copies = []
    for k, shift in enumerate(shifts):
        column = pl.multiple_of((place() ^ shift) * stride + start, LANES)
        copies.append(
            pltpu.make_async_copy(source.at[:, :, pl.ds(column, width)], pieces[k], sems.at[k])
        )
    for copy in copies:
        copy.start()
    for copy in copies:
        copy.wait()


def cut(head, shifts, stride, start, width):
    shape = jax.ShapeDtypeStruct(head.shape[:2] + (width,), head.dtype)
    return pl.pallas_call(
        functools.partial(cut_kernel, shifts, stride, start, width),
        in_specs=[pl.BlockSpec(memory_space=pl.ANY)],
        out_specs=[pl.BlockSpec(memory_space=pl.ANY)] * len(shifts),
        out_shape=[shape] * len(shifts),
        scratch_shapes=[pltpu.SemaphoreType.DMA((len(shifts),))],
        name="cut",
    )(head)


def join_kernel(shifts, stride, starts, width, *refs):
    count = len(shifts) * len(starts)
    pieces, whole, sems = refs[:count], refs[count], refs[count + 1]
    copies = []
    for c, start in enumerate(starts):
        for k, shift in enumerate(shifts):
            n = c * len(shifts) + k
            column = pl.multiple_of((place() ^ shift) * stride + start, LANES)
            copies.append(
                pltpu.make_async_copy(pieces[n], whole.at[:, :, pl.ds(column, width)], sems.at[n])
            )
    for copy in copies:
        copy.start()
    for copy in copies:
        copy.wait()


def join(pieces, shifts, stride, starts, width, columns):
    flat = [piece for chunk in pieces for piece in chunk]
    return pl.pallas_call(
        functools.partial(join_kernel, shifts, stride, starts, width),
        in_specs=[pl.BlockSpec(memory_space=pl.ANY)] * len(flat),
        out_specs=pl.BlockSpec(memory_space=pl.ANY),
        out_shape=jax.ShapeDtypeStruct(flat[0].shape[:2] + (columns,), flat[0].dtype),
        scratch_shapes=[pltpu.SemaphoreType.DMA((len(flat),))],
        name="join",
    )(*flat)


def in_order(pieces, shifts):
    stack = jnp.zeros((len(pieces),) + pieces[0].shape, pieces[0].dtype)
    for piece, shift in zip(pieces, shifts):
        stack = lax.dynamic_update_index_in_dim(stack, piece, place() ^ shift, 0)
    return stack


class Head:
    def __init__(self, head, chunks):
        self.rank, self.columns = head.shape[1:]
        self.head = head
        self.places = lax.axis_size("groups") * lax.axis_size("task")
        self.stride = self.columns // self.places
        self.by_lane = self.stride % (LANES * chunks) == 0
        self.by_row = not self.by_lane and self.rank % self.places == 0
        self.chunks = chunks if self.by_lane else 1
        self.width = self.stride // self.chunks

    def cut(self, chunk, shifts):
        if self.by_lane:
            return cut(self.head, shifts, self.stride, chunk * self.width, self.width)
        rows = self.head.shape[0]
        if self.by_row:
            shares = self.head.reshape(rows, self.places, -1, self.columns).transpose(1, 0, 2, 3)
        else:
            shares = self.head.reshape(rows, self.rank, self.places, -1).transpose(2, 0, 1, 3)
        return [lax.dynamic_index_in_dim(shares, place() ^ s, 0, keepdims=False) for s in shifts]

    def join(self, pieces, shifts):
        if self.by_lane:
            starts = [c * self.width for c in range(self.chunks)]
            return join(pieces, shifts, self.stride, starts, self.width, self.columns)
        stack = in_order(pieces[0], shifts)
        stack = stack.transpose((1, 0, 2, 3) if self.by_row else (1, 2, 0, 3))
        return stack.reshape(stack.shape[0], self.rank, self.columns)


def halving_order(total):
    bits = total.bit_length() - 1
    return [int(format(o, "b").zfill(bits)[::-1], 2) if bits else 0 for o in range(total)]


def reduce_blocks(partial, axis):
    step = 1
    while partial.shape[0] > 1:
        half = partial.shape[0] // 2
        partial = partial[:half] + swap(partial[half:], axis, step)
        step *= 2
    return partial[0]


def local(
    tokens,
    task_counts,
    task_embeddings,
    embedding_weight,
    down_factor_head,
    query_up_head,
    value_up_head,
    w_query,
    w_value,
):
    groups, ring, parts = lax.axis_size("groups"), lax.axis_size("task"), lax.axis_size("tensor")
    places = groups * ring
    tok_rows, shard_width = tokens.shape
    block_rows = tok_rows // parts
    own_tasks = task_counts.shape[0]
    block_tasks = own_tasks // parts
    rank = query_up_head.shape[1]
    hidden_rows = down_factor_head.shape[0]
    query_width = w_query.shape[1]
    tensor = lax.axis_index("tensor")
    ring_shifts = list(range(ring))
    far_first = sorted(ring_shifts[1:], reverse=True)
    shifts = list(range(places))

    heads = {
        "value": Head(value_up_head, 1),
        "query": Head(query_up_head, 1),
        "down": Head(down_factor_head, 2),
    }

    def fetch(name, chunk):
        pieces = heads[name].cut(chunk, ring_shifts)
        got = {0: pieces[0]}
        for s in far_first:
            got[s] = swap(pieces[s], "task", s)
        return jnp.concatenate([got[s] for s in ring_shifts], axis=0)

    fetched = {("value", 0): fetch("value", 0), ("query", 0): fetch("query", 0)}

    hidden = jax.nn.silu(
        jnp.dot(task_embeddings, embedding_weight, preferred_element_type=jnp.float32)
    ).astype(jnp.bfloat16)
    group_hidden = jnp.concatenate([hidden] + [swap(hidden, "groups", s) for s in range(1, groups)])
    ring_hidden = [group_hidden] + [swap(group_hidden, "task", s) for s in ring_shifts[1:]]
    every_hidden = jnp.stack(ring_hidden).reshape(ring, groups, own_tasks, -1)
    every_hidden = every_hidden.transpose(1, 0, 2, 3).reshape(places * own_tasks, ring, hidden_rows)
    every_hidden = every_hidden.transpose(1, 0, 2)
    every_hidden = jnp.concatenate(
        [
            lax.dynamic_index_in_dim(every_hidden, lax.axis_index("task") ^ s, 0, keepdims=False)
            for s in ring_shifts
        ],
        axis=1,
    )

    for chunk in range(heads["down"].chunks):
        fetched["down", chunk] = fetch("down", chunk)

    def emit(name, chunk):
        matrix = fetched[name, chunk]
        flat = jnp.dot(
            every_hidden, matrix.reshape(matrix.shape[0], -1), preferred_element_type=jnp.float32
        ).astype(jnp.bfloat16)
        made = flat.reshape((places, own_tasks) + matrix.shape[1:])
        got = {0: made[0]}
        for s in reversed(shifts[1:]):
            got[s] = swap(made[s], PLACES, s)
        return [got[s] for s in shifts]

    emitted = {key: emit(*key) for key in fetched}

    token_blocks = tokens.reshape(parts, block_rows, shard_width)
    order = halving_order(parts)
    turned = jnp.concatenate(
        [lax.dynamic_index_in_dim(token_blocks, tensor ^ s, 0, keepdims=False) for s in order]
    )
    base_query = reduce_blocks(
        jnp.dot(turned, w_query, preferred_element_type=jnp.float32).reshape(
            parts, block_rows, -1
        ),
        "tensor",
    )
    base_value = reduce_blocks(
        jnp.dot(turned, w_value, preferred_element_type=jnp.float32).reshape(
            parts, block_rows, -1
        ),
        "tensor",
    )

    query_up_factors = heads["query"].join([emitted["query", 0]], shifts)
    value_up_factors = heads["value"].join([emitted["value", 0]], shifts)

    def own_block(factors):
        moved = lax.all_to_all(factors, "tensor", split_axis=0, concat_axis=0, tiled=True)
        moved = moved.reshape(parts, block_tasks * rank, -1).transpose(1, 0, 2)
        return moved.reshape(block_tasks * rank, -1)

    own_query, own_value = own_block(query_up_factors), own_block(value_up_factors)

    down_factors = heads["down"].join(
        [emitted["down", c] for c in range(heads["down"].chunks)], shifts
    )

    finish = jnp.cumsum(task_counts.reshape(parts, block_tasks), axis=1)
    starts = finish - task_counts.reshape(parts, block_tasks)
    positions = jnp.arange(block_rows, dtype=jnp.int32)
    inside = (
        (positions[None, :, None] >= starts[:, None, :])
        & (positions[None, :, None] < finish[:, None, :])
    ).astype(jnp.float32)
    projected = jnp.einsum(
        "bpd,bmrd->bpmr",
        token_blocks,
        down_factors.reshape(parts, block_tasks, 2 * rank, shard_width),
        preferred_element_type=jnp.float32,
    )
    low_rank = jnp.sum(projected * inside[..., None], axis=2)
    mine = lax.dynamic_index_in_dim(low_rank, tensor, 0, keepdims=False)
    for s in range(1, parts):
        mine = mine + swap(
            lax.dynamic_index_in_dim(low_rank, tensor ^ s, 0, keepdims=False), "tensor", s
        )
    own_inside = lax.dynamic_index_in_dim(inside, tensor, 0, keepdims=False)

    def update(part, factors):
        spread = (own_inside[:, :, None] * part[:, None, :]).reshape(block_rows, -1)
        return jnp.dot(
            spread,
            factors.astype(jnp.float32),
            precision=lax.Precision.HIGHEST,
            preferred_element_type=jnp.float32,
        )

    query = base_query + ADAPTER_SCALE * update(mine[:, :rank], own_query)
    value = base_value + ADAPTER_SCALE * update(mine[:, rank:], own_value)
    return (
        query.astype(jnp.bfloat16),
        value.astype(jnp.bfloat16),
        down_factors,
        query_up_factors,
        value_up_factors,
    )


def solution(mesh):
    return jax.shard_map(
        local,
        mesh=mesh,
        in_specs=(
            P(("groups", "task"), "tensor"),
            P(("groups", "task")),
            P(("groups", "task"), None),
            P(),
            P("task", None, "tensor"),
            P("task", None, "tensor"),
            P("task", None, "tensor"),
            P("tensor", None),
            P("tensor", None),
        ),
        out_specs=(
            P(("groups", "task", "tensor"), None),
            P(("groups", "task", "tensor"), None),
            P(("groups", "task"), None, "tensor"),
            P(("groups", "task"), None, "tensor"),
            P(("groups", "task"), None, "tensor"),
        ),
        check_vma=False,
    )
```

```python
import functools

import jax
import jax.numpy as jnp
from jax import lax
from jax.experimental import pallas as pl
from jax.experimental.pallas import tpu as pltpu
from jax.sharding import PartitionSpec as P

ADAPTER_SCALE = 2.0
LANES = 128
PLACES = ("groups", "task")


def swap(x, axes, shift):
    total = lax.axis_size(axes)
    return lax.ppermute(x, axes, [(a, a ^ shift) for a in range(total)])


def place():
    return lax.axis_index("groups") * lax.axis_size("task") + lax.axis_index("task")


def through_vmem(moves, scratch, arrived, left):
    fetches = [
        pltpu.make_async_copy(source, scratch.at[k], arrived.at[k])
        for k, (source, _) in enumerate(moves)
    ]
    stores = [
        pltpu.make_async_copy(scratch.at[k], target, left.at[k])
        for k, (_, target) in enumerate(moves)
    ]
    for fetch in fetches:
        fetch.start()
    for fetch, store in zip(fetches, stores):
        fetch.wait()
        store.start()
    for store in stores:
        store.wait()


def vmem_scratch(count, shape, dtype):
    return [
        pltpu.VMEM((count,) + shape, dtype),
        pltpu.SemaphoreType.DMA((count,)),
        pltpu.SemaphoreType.DMA((count,)),
    ]


def cut_kernel(shifts, stride, start, width, source, *rest):
    moves = []
    for k, shift in enumerate(shifts):
        column = pl.multiple_of((place() ^ shift) * stride + start, LANES)
        moves.append((source.at[:, :, pl.ds(column, width)], rest[k]))
    through_vmem(moves, *rest[len(shifts) :])


def cut(head, shifts, stride, start, width):
    shape = head.shape[:2] + (width,)
    return pl.pallas_call(
        functools.partial(cut_kernel, shifts, stride, start, width),
        in_specs=[pl.BlockSpec(memory_space=pl.ANY)],
        out_specs=[pl.BlockSpec(memory_space=pl.ANY)] * len(shifts),
        out_shape=[jax.ShapeDtypeStruct(shape, head.dtype)] * len(shifts),
        scratch_shapes=vmem_scratch(len(shifts), shape, head.dtype),
        name="cut",
    )(head)


def join_kernel(shifts, stride, starts, width, *refs):
    count = len(shifts) * len(starts)
    whole = refs[count]
    moves = []
    for c, start in enumerate(starts):
        for k, shift in enumerate(shifts):
            column = pl.multiple_of((place() ^ shift) * stride + start, LANES)
            moves.append((refs[c * len(shifts) + k], whole.at[:, :, pl.ds(column, width)]))
    through_vmem(moves, *refs[count + 1 :])


def join(pieces, shifts, stride, starts, width, columns):
    flat = [piece for chunk in pieces for piece in chunk]
    return pl.pallas_call(
        functools.partial(join_kernel, shifts, stride, starts, width),
        in_specs=[pl.BlockSpec(memory_space=pl.ANY)] * len(flat),
        out_specs=pl.BlockSpec(memory_space=pl.ANY),
        out_shape=jax.ShapeDtypeStruct(flat[0].shape[:2] + (columns,), flat[0].dtype),
        scratch_shapes=vmem_scratch(len(flat), flat[0].shape, flat[0].dtype),
        name="join",
    )(*flat)


def stack_kernel(shifts, *refs):
    count = len(shifts)
    moves = [(refs[k], refs[count].at[place() ^ s]) for k, s in enumerate(shifts)]
    through_vmem(moves, *refs[count + 1 :])


def stack(pieces, shifts):
    shape, dtype = pieces[0].shape, pieces[0].dtype
    return pl.pallas_call(
        functools.partial(stack_kernel, shifts),
        in_specs=[pl.BlockSpec(memory_space=pl.ANY)] * len(pieces),
        out_specs=pl.BlockSpec(memory_space=pl.ANY),
        out_shape=jax.ShapeDtypeStruct((len(pieces),) + shape, dtype),
        scratch_shapes=vmem_scratch(len(pieces), shape, dtype),
        name="stack",
    )(*pieces)


def in_order(pieces, shifts):
    stack = jnp.zeros((len(pieces),) + pieces[0].shape, pieces[0].dtype)
    for piece, shift in zip(pieces, shifts):
        stack = lax.dynamic_update_index_in_dim(stack, piece, place() ^ shift, 0)
    return stack


class Head:
    def __init__(self, head, chunks):
        self.rank, self.columns = head.shape[1:]
        self.head = head
        self.places = lax.axis_size("groups") * lax.axis_size("task")
        self.stride = self.columns // self.places
        self.by_lane = self.stride % (LANES * chunks) == 0
        self.by_row = not self.by_lane and self.rank % self.places == 0
        self.chunks = chunks if self.by_lane else 1
        self.width = self.stride // self.chunks

    def cut(self, chunk, shifts):
        if self.by_lane:
            return cut(self.head, shifts, self.stride, chunk * self.width, self.width)
        rows = self.head.shape[0]
        if self.by_row:
            shares = self.head.reshape(rows, self.places, -1).transpose(1, 0, 2)
        else:
            shares = self.head.reshape(rows, self.rank, self.places, -1).transpose(2, 0, 1, 3)
        return [lax.dynamic_index_in_dim(shares, place() ^ s, 0, keepdims=False) for s in shifts]

    def join(self, pieces, shifts):
        if self.by_lane:
            starts = [c * self.width for c in range(self.chunks)]
            return join(pieces, shifts, self.stride, starts, self.width, self.columns)
        if self.by_row:
            whole = stack(pieces[0], shifts).transpose(1, 0, 2)
        else:
            whole = in_order(pieces[0], shifts).transpose(1, 2, 0, 3)
        return whole.reshape(whole.shape[0], self.rank, self.columns)


def halving_order(total):
    bits = total.bit_length() - 1
    return [int(format(o, "b").zfill(bits)[::-1], 2) if bits else 0 for o in range(total)]


def reduce_blocks(partial, axis):
    step = 1
    while partial.shape[0] > 1:
        half = partial.shape[0] // 2
        partial = partial[:half] + swap(partial[half:], axis, step)
        step *= 2
    return partial[0]


def local(
    tokens,
    task_counts,
    task_embeddings,
    embedding_weight,
    down_factor_head,
    query_up_head,
    value_up_head,
    w_query,
    w_value,
):
    groups, ring, parts = lax.axis_size("groups"), lax.axis_size("task"), lax.axis_size("tensor")
    places = groups * ring
    tok_rows, shard_width = tokens.shape
    block_rows = tok_rows // parts
    own_tasks = task_counts.shape[0]
    block_tasks = own_tasks // parts
    rank = query_up_head.shape[1]
    hidden_rows = down_factor_head.shape[0]
    tensor = lax.axis_index("tensor")
    ring_shifts = list(range(ring))
    far_first = sorted(ring_shifts[1:], reverse=True)
    shifts = list(range(places))

    heads = {
        "value": Head(value_up_head, 1),
        "query": Head(query_up_head, 1),
        "down": Head(down_factor_head, 2),
    }

    def fetch(name, chunk):
        pieces = heads[name].cut(chunk, ring_shifts)
        got = {0: pieces[0]}
        for s in far_first:
            got[s] = swap(pieces[s], "task", s)
        return jnp.concatenate([got[s] for s in ring_shifts], axis=0)

    fetched = {("value", 0): fetch("value", 0), ("query", 0): fetch("query", 0)}

    hidden = jax.nn.silu(
        jnp.dot(task_embeddings, embedding_weight, preferred_element_type=jnp.float32)
    ).astype(jnp.bfloat16)
    group_hidden = jnp.concatenate([hidden] + [swap(hidden, "groups", s) for s in range(1, groups)])
    ring_hidden = [group_hidden] + [swap(group_hidden, "task", s) for s in ring_shifts[1:]]
    every_hidden = jnp.stack(ring_hidden).reshape(ring, groups, own_tasks, -1)
    every_hidden = every_hidden.transpose(1, 0, 2, 3).reshape(places * own_tasks, ring, hidden_rows)
    every_hidden = every_hidden.transpose(1, 0, 2)
    every_hidden = jnp.concatenate(
        [
            lax.dynamic_index_in_dim(every_hidden, lax.axis_index("task") ^ s, 0, keepdims=False)
            for s in ring_shifts
        ],
        axis=1,
    )

    for chunk in range(heads["down"].chunks):
        fetched["down", chunk] = fetch("down", chunk)

    def emit(name, chunk):
        matrix = fetched[name, chunk]
        flat = jnp.dot(
            every_hidden, matrix.reshape(matrix.shape[0], -1), preferred_element_type=jnp.float32
        ).astype(jnp.bfloat16)
        made = flat.reshape((places, own_tasks) + matrix.shape[1:])
        got = {0: made[0]}
        for s in reversed(shifts[1:]):
            got[s] = swap(made[s], PLACES, s)
        return [got[s] for s in shifts]

    emitted = {key: emit(*key) for key in fetched}

    tokens, every_hidden = lax.optimization_barrier((tokens, every_hidden))
    token_blocks = tokens.reshape(parts, block_rows, shard_width)
    order = halving_order(parts)
    turned = jnp.concatenate(
        [lax.dynamic_index_in_dim(token_blocks, tensor ^ s, 0, keepdims=False) for s in order]
    )
    base_query = reduce_blocks(
        jnp.dot(turned, w_query, preferred_element_type=jnp.float32).reshape(
            parts, block_rows, -1
        ),
        "tensor",
    )
    base_value = reduce_blocks(
        jnp.dot(turned, w_value, preferred_element_type=jnp.float32).reshape(
            parts, block_rows, -1
        ),
        "tensor",
    )

    query_up_factors = heads["query"].join([emitted["query", 0]], shifts)
    value_up_factors = heads["value"].join([emitted["value", 0]], shifts)

    def own_block(factors):
        moved = lax.all_to_all(factors, "tensor", split_axis=0, concat_axis=0, tiled=True)
        moved = moved.reshape(parts, block_tasks * rank, -1).transpose(1, 0, 2)
        return moved.reshape(block_tasks * rank, -1)

    own_query, own_value = own_block(query_up_factors), own_block(value_up_factors)

    down_factors = heads["down"].join(
        [emitted["down", c] for c in range(heads["down"].chunks)], shifts
    )

    finish = jnp.cumsum(task_counts.reshape(parts, block_tasks), axis=1)
    starts = finish - task_counts.reshape(parts, block_tasks)
    positions = jnp.arange(block_rows, dtype=jnp.int32)
    inside = (
        (positions[None, :, None] >= starts[:, None, :])
        & (positions[None, :, None] < finish[:, None, :])
    ).astype(jnp.float32)
    projected = jnp.einsum(
        "bpd,bmrd->bpmr",
        token_blocks,
        down_factors.reshape(parts, block_tasks, 2 * rank, shard_width),
        preferred_element_type=jnp.float32,
    )
    low_rank = jnp.sum(projected * inside[..., None], axis=2)
    mine = lax.dynamic_index_in_dim(low_rank, tensor, 0, keepdims=False)
    for s in range(1, parts):
        mine = mine + swap(
            lax.dynamic_index_in_dim(low_rank, tensor ^ s, 0, keepdims=False), "tensor", s
        )
    own_inside = lax.dynamic_index_in_dim(inside, tensor, 0, keepdims=False)

    def update(part, factors):
        spread = (own_inside[:, :, None] * part[:, None, :]).reshape(block_rows, -1)
        return jnp.dot(
            spread,
            factors.astype(jnp.float32),
            precision=lax.Precision.HIGHEST,
            preferred_element_type=jnp.float32,
        )

    query = base_query + ADAPTER_SCALE * update(mine[:, :rank], own_query)
    value = base_value + ADAPTER_SCALE * update(mine[:, rank:], own_value)
    return (
        query.astype(jnp.bfloat16),
        value.astype(jnp.bfloat16),
        down_factors,
        query_up_factors,
        value_up_factors,
    )


def solution(mesh):
    return jax.shard_map(
        local,
        mesh=mesh,
        in_specs=(
            P(("groups", "task"), "tensor"),
            P(("groups", "task")),
            P(("groups", "task"), None),
            P(),
            P("task", None, "tensor"),
            P("task", None, "tensor"),
            P("task", None, "tensor"),
            P("tensor", None),
            P("tensor", None),
        ),
        out_specs=(
            P(("groups", "task", "tensor"), None),
            P(("groups", "task", "tensor"), None),
            P(("groups", "task"), None, "tensor"),
            P(("groups", "task"), None, "tensor"),
            P(("groups", "task"), None, "tensor"),
        ),
        check_vma=False,
    )
```

```python
import functools

import jax
import jax.numpy as jnp
from jax import lax
from jax.experimental import pallas as pl
from jax.experimental.pallas import tpu as pltpu
from jax.sharding import PartitionSpec as P


ADAPTER_SCALE = 2.0
LANES = 128
PLACES = ("groups", "task")


def swap(x, axes, shift):
    total = lax.axis_size(axes)
    return lax.ppermute(x, axes, [(a, a ^ shift) for a in range(total)])


def place():
    return lax.axis_index("groups") * lax.axis_size("task") + lax.axis_index("task")


def through_vmem(moves, scratch, arrived, left):
    fetches = [
        pltpu.make_async_copy(source, scratch.at[k], arrived.at[k])
        for k, (source, _) in enumerate(moves)
    ]
    stores = [
        pltpu.make_async_copy(scratch.at[k], target, left.at[k])
        for k, (_, target) in enumerate(moves)
    ]
    for fetch in fetches:
        fetch.start()
    for fetch, store in zip(fetches, stores):
        fetch.wait()
        store.start()
    for store in stores:
        store.wait()


def vmem_scratch(count, shape, dtype):
    return [
        pltpu.VMEM((count,) + shape, dtype),
        pltpu.SemaphoreType.DMA((count,)),
        pltpu.SemaphoreType.DMA((count,)),
    ]


def cut_kernel(shifts, stride, start, width, source, *rest):
    moves = []
    for k, shift in enumerate(shifts):
        column = pl.multiple_of((place() ^ shift) * stride + start, LANES)
        moves.append((source.at[:, :, pl.ds(column, width)], rest[k]))
    through_vmem(moves, *rest[len(shifts) :])


def cut(head, shifts, stride, start, width):
    shape = head.shape[:2] + (width,)
    return pl.pallas_call(
        functools.partial(cut_kernel, shifts, stride, start, width),
        in_specs=[pl.BlockSpec(memory_space=pl.ANY)],
        out_specs=[pl.BlockSpec(memory_space=pl.ANY)] * len(shifts),
        out_shape=[jax.ShapeDtypeStruct(shape, head.dtype)] * len(shifts),
        scratch_shapes=vmem_scratch(len(shifts), shape, head.dtype),
        name="cut",
    )(head)


def join_kernel(shifts, stride, start, width, *refs):
    whole = refs[-4]
    moves = []
    for k, shift in enumerate(shifts):
        column = pl.multiple_of((place() ^ shift) * stride + start, LANES)
        moves.append((refs[k], whole.at[:, :, pl.ds(column, width)]))
    through_vmem(moves, *refs[-3:])


def join(pieces, shifts, stride, start, width, columns, whole):
    operands = list(pieces) + ([] if whole is None else [whole])
    return pl.pallas_call(
        functools.partial(join_kernel, shifts, stride, start, width),
        in_specs=[pl.BlockSpec(memory_space=pl.ANY)] * len(operands),
        out_specs=pl.BlockSpec(memory_space=pl.ANY),
        out_shape=jax.ShapeDtypeStruct(pieces[0].shape[:2] + (columns,), pieces[0].dtype),
        scratch_shapes=vmem_scratch(len(pieces), pieces[0].shape, pieces[0].dtype),
        input_output_aliases={} if whole is None else {len(pieces): 0},
        name="join",
    )(*operands)


def stack_kernel(shifts, *refs):
    count = len(shifts)
    moves = [(refs[k], refs[count].at[place() ^ s]) for k, s in enumerate(shifts)]
    through_vmem(moves, *refs[count + 1 :])


def stack(pieces, shifts):
    shape, dtype = pieces[0].shape, pieces[0].dtype
    return pl.pallas_call(
        functools.partial(stack_kernel, shifts),
        in_specs=[pl.BlockSpec(memory_space=pl.ANY)] * len(pieces),
        out_specs=pl.BlockSpec(memory_space=pl.ANY),
        out_shape=jax.ShapeDtypeStruct((len(pieces),) + shape, dtype),
        scratch_shapes=vmem_scratch(len(pieces), shape, dtype),
        name="stack",
    )(*pieces)


def in_order(pieces, shifts):
    stack = jnp.zeros((len(pieces),) + pieces[0].shape, pieces[0].dtype)
    for piece, shift in zip(pieces, shifts):
        stack = lax.dynamic_update_index_in_dim(stack, piece, place() ^ shift, 0)
    return stack


class Head:
    def __init__(self, head, chunks):
        self.rank, self.columns = head.shape[1:]
        self.head = head
        self.places = lax.axis_size("groups") * lax.axis_size("task")
        self.stride = self.columns // self.places
        self.by_lane = self.stride % (LANES * chunks) == 0
        self.by_row = not self.by_lane and self.rank % self.places == 0
        self.chunks = chunks if self.by_lane else 1
        self.width = self.stride // self.chunks

    def cut(self, chunk, shifts):
        if self.by_lane:
            return cut(self.head, shifts, self.stride, chunk * self.width, self.width)
        rows = self.head.shape[0]
        if self.by_row:
            shares = self.head.reshape(rows, self.places, -1).transpose(1, 0, 2)
        else:
            shares = self.head.reshape(rows, self.rank, self.places, -1).transpose(2, 0, 1, 3)
        return [lax.dynamic_index_in_dim(shares, place() ^ s, 0, keepdims=False) for s in shifts]

    def join(self, pieces, shifts, chunk=0, whole=None):
        if self.by_lane:
            start = chunk * self.width
            return join(pieces, shifts, self.stride, start, self.width, self.columns, whole)
        if self.by_row:
            whole = stack(pieces, shifts).transpose(1, 0, 2)
        else:
            whole = in_order(pieces, shifts).transpose(1, 2, 0, 3)
        return whole.reshape(whole.shape[0], self.rank, self.columns)


def project_kernel(shifts, parts, stride, start, width, tokens, inside, *refs):
    pieces, refs = refs[: len(shifts)], refs[len(shifts) :]
    before, after = refs[:-parts], refs[-parts:]
    rows = tokens.shape[0] // parts
    tasks = pieces[0].shape[0] // parts
    for turn in range(parts):
        block = lax.axis_index("tensor") ^ turn
        total = before[turn][...] if before else None
        found = jnp.zeros(after[turn].shape, jnp.float32)
        for k, shift in enumerate(shifts):
            column = pl.multiple_of((place() ^ shift) * stride + start, LANES)
            found += lax.dot_general(
                tokens[pl.ds(pl.multiple_of(block * rows, 8), rows), pl.ds(column, width)],
                pieces[k][pl.ds(block * tasks, tasks)].reshape(-1, width),
                (((1,), (1,)), ((), ())),
                preferred_element_type=jnp.float32,
            )
        found = found * inside[block]
        after[turn][...] = found if total is None else total + found


def project(pieces, shifts, stride, start, width, tokens, inside, before):
    parts = inside.shape[0]
    return pl.pallas_call(
        functools.partial(project_kernel, shifts, parts, stride, start, width),
        out_shape=[jax.ShapeDtypeStruct(inside.shape[1:], jnp.float32)] * parts,
        name="project",
    )(tokens, inside, *pieces, *before)


def finish_kernel(count, *refs):
    low_rank = refs[0][...]
    for k in range(1, count):
        low_rank = low_rank + refs[k][...]
    high = low_rank.astype(jnp.bfloat16)
    low = (low_rank - high.astype(jnp.float32)).astype(jnp.bfloat16)
    refs = refs[count:]
    for kept, came, up, out in (refs[0:3] + refs[6:7], refs[3:6] + refs[7:8]):
        update = jnp.dot(high, up[...], preferred_element_type=jnp.float32)
        update = update + jnp.dot(low, up[...], preferred_element_type=jnp.float32)
        out[...] = (kept[...] + came[...] + ADAPTER_SCALE * update).astype(out.dtype)


def finish(shares, query, value, steps):
    rows = query[0].shape[0]

    def columns(x):
        return pl.BlockSpec((x.shape[0], x.shape[1] // steps), lambda i: (0, i))

    return pl.pallas_call(
        functools.partial(finish_kernel, len(shares)),
        grid=(steps,),
        in_specs=[pl.BlockSpec(x.shape, lambda i: (0, 0)) for x in shares]
        + [columns(x) for x in query + value],
        out_specs=[columns(query[0]), columns(value[0])],
        out_shape=[
            jax.ShapeDtypeStruct((rows, query[0].shape[1]), jnp.bfloat16),
            jax.ShapeDtypeStruct((rows, value[0].shape[1]), jnp.bfloat16),
        ],
        name="finish",
    )(*shares, *query, *value)


def halving_order(total):
    bits = total.bit_length() - 1
    return [int(format(o, "b").zfill(bits)[::-1], 2) if bits else 0 for o in range(total)]


def reduce_blocks(partial, axis):
    step = 1
    came = jnp.zeros_like(partial)
    while partial.shape[0] > 1:
        half = partial.shape[0] // 2
        came = swap(partial[half:], axis, step)
        partial = partial[:half]
        step *= 2
        if half > 1:
            partial = partial + came
    return partial[0], came[0]


def gather_blocks(x, axis):
    x = x[None]
    step = 1
    while step < lax.axis_size(axis):
        came = swap(x, axis, step)
        upper = (lax.axis_index(axis) & step) > 0
        x = jnp.concatenate([jnp.where(upper, came, x), jnp.where(upper, x, came)])
        step *= 2
    return x


def local(
    tokens,
    task_counts,
    task_embeddings,
    embedding_weight,
    down_factor_head,
    query_up_head,
    value_up_head,
    w_query,
    w_value,
):
    groups, ring, parts = lax.axis_size("groups"), lax.axis_size("task"), lax.axis_size("tensor")
    places = groups * ring
    tok_rows, shard_width = tokens.shape
    block_rows = tok_rows // parts
    own_tasks = task_counts.shape[0]
    block_tasks = own_tasks // parts
    rank = query_up_head.shape[1]
    hidden_rows = down_factor_head.shape[0]
    tensor = lax.axis_index("tensor")
    ring_shifts = list(range(ring))
    far_first = sorted(ring_shifts[1:], reverse=True)
    shifts = list(range(places))

    heads = {
        "value": Head(value_up_head, 1),
        "query": Head(query_up_head, 1),
        "down": Head(down_factor_head, 2),
    }

    def fetch(name, chunk):
        pieces = heads[name].cut(chunk, ring_shifts)
        got = {0: pieces[0]}
        for s in far_first:
            got[s] = swap(pieces[s], "task", s)
        return jnp.concatenate([got[s] for s in ring_shifts], axis=0)

    fetched = {}
    fetched["query", 0] = fetch("query", 0)

    share = own_tasks // parts
    embeddings = lax.dynamic_index_in_dim(
        task_embeddings.reshape(parts, share, -1), tensor, 0, keepdims=False
    )
    hidden = jax.nn.silu(
        jnp.dot(embeddings, embedding_weight, preferred_element_type=jnp.float32)
    ).astype(jnp.bfloat16)
    group_hidden = jnp.concatenate([hidden] + [swap(hidden, "groups", s) for s in range(1, groups)])
    ring_hidden = jnp.stack(
        [group_hidden] + [swap(group_hidden, "task", s) for s in ring_shifts[1:]]
    )
    every_hidden = gather_blocks(ring_hidden.reshape(places * share, -1), "tensor")
    every_hidden = every_hidden.reshape(parts, ring, groups, share, ring, hidden_rows)
    every_hidden = every_hidden.transpose(4, 2, 1, 0, 3, 5)
    every_hidden = every_hidden.reshape(ring, places * own_tasks, hidden_rows)
    every_hidden = jnp.concatenate(
        [
            lax.dynamic_index_in_dim(every_hidden, lax.axis_index("task") ^ s, 0, keepdims=False)
            for s in ring_shifts
        ],
        axis=1,
    )

    chunks = heads["down"].chunks
    for chunk in range(chunks):
        fetched["down", chunk] = fetch("down", chunk)
    fetched["value", 0] = fetch("value", 0)

    def emit(name, chunk):
        matrix = fetched[name, chunk]
        flat = jnp.dot(
            every_hidden, matrix.reshape(matrix.shape[0], -1), preferred_element_type=jnp.float32
        ).astype(jnp.bfloat16)
        made = flat.reshape((places, own_tasks) + matrix.shape[1:])
        got = {0: made[0]}
        for s in reversed(shifts[1:]):
            got[s] = swap(made[s], PLACES, s)
        return [got[s] for s in shifts]

    emitted = {}
    for name, chunk in [("query", 0), ("value", 0)] + [("down", c) for c in range(chunks)]:
        emitted[name, chunk] = emit(name, chunk)

    token_blocks = tokens.reshape(parts, block_rows, shard_width)
    order = halving_order(parts)
    turned = jnp.concatenate(
        [lax.dynamic_index_in_dim(token_blocks, tensor ^ s, 0, keepdims=False) for s in order]
    )
    base_query = jnp.dot(turned, w_query, preferred_element_type=jnp.float32)
    base_value = jnp.dot(turned, w_value, preferred_element_type=jnp.float32)
    base_query = reduce_blocks(base_query.reshape(parts, block_rows, -1), "tensor")
    base_value = reduce_blocks(base_value.reshape(parts, block_rows, -1), "tensor")

    def own_block(factors, above, below):
        moved = lax.all_to_all(factors, "tensor", split_axis=0, concat_axis=0, tiled=True)
        moved = moved.reshape(parts, block_tasks, rank, -1).transpose(1, 2, 0, 3)
        moved = moved.reshape(block_tasks, rank, -1)
        moved = jnp.pad(moved, ((0, 0), (above, below), (0, 0)))
        return moved.reshape(block_tasks * 2 * rank, -1)

    query_up_factors = heads["query"].join(emitted["query", 0], shifts)
    own_query = own_block(query_up_factors, 0, rank)
    value_up_factors = heads["value"].join(emitted["value", 0], shifts)
    own_value = own_block(value_up_factors, rank, 0)

    tallies = task_counts.reshape(parts, block_tasks)
    ends = jnp.cumsum(tallies, axis=1)
    starts = ends - tallies
    positions = jnp.arange(block_rows, dtype=jnp.int32)
    inside = (
        (positions[None, :, None] >= starts[:, None, :])
        & (positions[None, :, None] < ends[:, None, :])
    ).astype(jnp.float32)
    inside = jnp.repeat(inside, 2 * rank, axis=2)

    down_factors, spread = None, []
    for chunk in range(chunks):
        head, pieces = heads["down"], emitted["down", chunk]
        if head.by_lane:
            start = chunk * head.width
            spread = project(pieces, shifts, head.stride, start, head.width, tokens, inside, spread)
        down_factors = head.join(pieces, shifts, chunk, down_factors)
    if not spread:
        projected = jnp.einsum(
            "bpd,bmd->bpm",
            token_blocks,
            down_factors.reshape(parts, block_tasks * 2 * rank, shard_width),
            preferred_element_type=jnp.float32,
        )
        projected = projected * inside
        spread = [
            lax.dynamic_index_in_dim(projected, tensor ^ s, 0, keepdims=False)
            for s in range(parts)
        ]
    shares = [spread[0]] + [swap(spread[s], "tensor", s) for s in range(1, parts)]
    query, value = finish(
        shares, [*base_query, own_query], [*base_value, own_value], steps=4
    )
    return query, value, down_factors, query_up_factors, value_up_factors


def solution(mesh):
    return jax.shard_map(
        local,
        mesh=mesh,
        in_specs=(
            P(("groups", "task"), "tensor"),
            P(("groups", "task")),
            P(("groups", "task"), None),
            P(),
            P("task", None, "tensor"),
            P("task", None, "tensor"),
            P("task", None, "tensor"),
            P("tensor", None),
            P("tensor", None),
        ),
        out_specs=(
            P(("groups", "task", "tensor"), None),
            P(("groups", "task", "tensor"), None),
            P(("groups", "task"), None, "tensor"),
            P(("groups", "task"), None, "tensor"),
            P(("groups", "task"), None, "tensor"),
        ),
        check_vma=False,
    )
```

```python
import functools

import jax
import jax.numpy as jnp
from jax import lax
from jax.experimental import pallas as pl
from jax.experimental.pallas import tpu as pltpu
from jax.sharding import PartitionSpec as P


ADAPTER_SCALE = 2.0
LANES = 128
PLACES = ("groups", "task")


def swap(x, axes, shift):
    total = lax.axis_size(axes)
    return lax.ppermute(x, axes, [(a, a ^ shift) for a in range(total)])


def place():
    return lax.axis_index("groups") * lax.axis_size("task") + lax.axis_index("task")


def through_vmem(moves, scratch, arrived, left):
    fetches = [
        pltpu.make_async_copy(source, scratch.at[k], arrived.at[k])
        for k, (source, _) in enumerate(moves)
    ]
    stores = [
        pltpu.make_async_copy(scratch.at[k], target, left.at[k])
        for k, (_, target) in enumerate(moves)
    ]
    for fetch in fetches:
        fetch.start()
    for fetch, store in zip(fetches, stores):
        fetch.wait()
        store.start()
    for store in stores:
        store.wait()


def vmem_scratch(count, shape, dtype):
    return [
        pltpu.VMEM((count,) + shape, dtype),
        pltpu.SemaphoreType.DMA((count,)),
        pltpu.SemaphoreType.DMA((count,)),
    ]


def cut_kernel(shifts, stride, start, width, source, *rest):
    moves = []
    for k, shift in enumerate(shifts):
        column = pl.multiple_of((place() ^ shift) * stride + start, LANES)
        moves.append((source.at[:, :, pl.ds(column, width)], rest[k]))
    through_vmem(moves, *rest[len(shifts) :])


def cut(head, shifts, stride, start, width):
    shape = head.shape[:2] + (width,)
    return pl.pallas_call(
        functools.partial(cut_kernel, shifts, stride, start, width),
        in_specs=[pl.BlockSpec(memory_space=pl.ANY)],
        out_specs=[pl.BlockSpec(memory_space=pl.ANY)] * len(shifts),
        out_shape=[jax.ShapeDtypeStruct(shape, head.dtype)] * len(shifts),
        scratch_shapes=vmem_scratch(len(shifts), shape, head.dtype),
        name="cut",
    )(head)


def join_kernel(shifts, stride, start, width, *refs):
    whole = refs[-4]
    moves = []
    for k, shift in enumerate(shifts):
        column = pl.multiple_of((place() ^ shift) * stride + start, LANES)
        moves.append((refs[k], whole.at[:, :, pl.ds(column, width)]))
    through_vmem(moves, *refs[-3:])


def join(pieces, shifts, stride, start, width, columns, whole):
    operands = list(pieces) + ([] if whole is None else [whole])
    return pl.pallas_call(
        functools.partial(join_kernel, shifts, stride, start, width),
        in_specs=[pl.BlockSpec(memory_space=pl.ANY)] * len(operands),
        out_specs=pl.BlockSpec(memory_space=pl.ANY),
        out_shape=jax.ShapeDtypeStruct(pieces[0].shape[:2] + (columns,), pieces[0].dtype),
        scratch_shapes=vmem_scratch(len(pieces), pieces[0].shape, pieces[0].dtype),
        input_output_aliases={} if whole is None else {len(pieces): 0},
        name="join",
    )(*operands)


def stack_kernel(shifts, *refs):
    count = len(shifts)
    moves = [(refs[k], refs[count].at[place() ^ s]) for k, s in enumerate(shifts)]
    through_vmem(moves, *refs[count + 1 :])


def stack(pieces, shifts):
    shape, dtype = pieces[0].shape, pieces[0].dtype
    return pl.pallas_call(
        functools.partial(stack_kernel, shifts),
        in_specs=[pl.BlockSpec(memory_space=pl.ANY)] * len(pieces),
        out_specs=pl.BlockSpec(memory_space=pl.ANY),
        out_shape=jax.ShapeDtypeStruct((len(pieces),) + shape, dtype),
        scratch_shapes=vmem_scratch(len(pieces), shape, dtype),
        name="stack",
    )(*pieces)


def in_order(pieces, shifts):
    stack = jnp.zeros((len(pieces),) + pieces[0].shape, pieces[0].dtype)
    for piece, shift in zip(pieces, shifts):
        stack = lax.dynamic_update_index_in_dim(stack, piece, place() ^ shift, 0)
    return stack


class Head:
    def __init__(self, head, chunks):
        self.rank, self.columns = head.shape[1:]
        self.head = head
        self.places = lax.axis_size("groups") * lax.axis_size("task")
        self.stride = self.columns // self.places
        self.by_lane = self.stride % (LANES * chunks) == 0
        self.by_row = not self.by_lane and self.rank % self.places == 0
        self.chunks = chunks if self.by_lane else 1
        self.width = self.stride // self.chunks

    def cut(self, chunk, shifts):
        if self.by_lane:
            return cut(self.head, shifts, self.stride, chunk * self.width, self.width)
        rows = self.head.shape[0]
        if self.by_row:
            shares = self.head.reshape(rows, self.places, -1).transpose(1, 0, 2)
        else:
            shares = self.head.reshape(rows, self.rank, self.places, -1).transpose(2, 0, 1, 3)
        return [lax.dynamic_index_in_dim(shares, place() ^ s, 0, keepdims=False) for s in shifts]

    def join(self, pieces, shifts, chunk=0, whole=None):
        if self.by_lane:
            start = chunk * self.width
            return join(pieces, shifts, self.stride, start, self.width, self.columns, whole)
        if self.by_row:
            whole = stack(pieces, shifts).transpose(1, 0, 2)
        else:
            whole = in_order(pieces, shifts).transpose(1, 2, 0, 3)
        return whole.reshape(whole.shape[0], self.rank, self.columns)


def rank_columns(shape, rank_axis, column_axis, rank):
    of_column = lax.broadcasted_iota(jnp.int32, shape, column_axis) % rank
    return of_column == lax.broadcasted_iota(jnp.int32, shape, rank_axis)


def inside(bounds, rows):
    row = lax.broadcasted_iota(jnp.int32, (rows, bounds.shape[1]), 0)
    return (row >= bounds[0:1]) & (row < bounds[1:2])


def turned(x, square):
    square[...] = jnp.zeros(square.shape, square.dtype)
    square[0 : x.shape[0], 0 : x.shape[1]] = x
    return square[...].T


def terms(x, count):
    parts = []
    for _ in range(count):
        parts.append(x.astype(jnp.bfloat16))
        x = x - parts[-1].astype(jnp.float32)
    return jnp.concatenate(parts)


def project_kernel(shifts, parts, stride, start, width, tokens, bounds, *refs):
    pieces, refs, square = refs[: len(shifts)], refs[len(shifts) : -1], refs[-1]
    before, after = refs[:-parts], refs[-parts:]
    rows = tokens.shape[0] // parts
    tasks, rank = pieces[0].shape[0] // parts, pieces[0].shape[1]
    every = []
    for turn in range(parts):
        block = lax.axis_index("tensor") ^ turn
        found = jnp.zeros((rows, tasks * rank), jnp.float32)
        for k, shift in enumerate(shifts):
            column = pl.multiple_of((place() ^ shift) * stride + start, LANES)
            found += lax.dot_general(
                tokens[pl.ds(pl.multiple_of(block * rows, 8), rows), pl.ds(column, width)],
                pieces[k][pl.ds(block * tasks, tasks)].reshape(-1, width),
                (((1,), (1,)), ((), ())),
                preferred_element_type=jnp.float32,
            )
        every.append(jnp.where(inside(bounds[block], rows), found, 0.0))
    pick = rank_columns((tasks * rank, LANES), 1, 0, rank).astype(jnp.bfloat16)
    count = 3
    summed = jnp.dot(
        terms(jnp.concatenate(every), count), pick, preferred_element_type=jnp.float32
    ).reshape(count, parts, rows, LANES)
    for turn in range(parts):
        low_rank = turned(sum(summed[k, turn] for k in range(count)), square)[0:rank, 0:rows]
        after[turn][...] = low_rank + before[turn][...] if before else low_rank


def project(pieces, shifts, stride, start, width, tokens, bounds, before):
    parts, rank = bounds.shape[0], pieces[0].shape[1]
    rows = tokens.shape[0] // parts
    return pl.pallas_call(
        functools.partial(project_kernel, shifts, parts, stride, start, width),
        out_shape=[jax.ShapeDtypeStruct((rank, rows), jnp.float32)] * parts,
        scratch_shapes=[pltpu.VMEM((LANES, LANES), jnp.float32)],
        name="project",
    )(tokens, bounds, *pieces, *before)


def finish_kernel(count, bounds, *refs):
    shares, rest = refs[:count], refs[count:]
    base_query, base_value, up_query, up_value, query, value, square, spread = rest
    rank, rows = shares[0].shape

    @pl.when(pl.program_id(0) == 0)
    def _():
        low_rank = shares[0][...]
        for share in shares[1:]:
            low_rank = low_rank + share[...]
        low_rank = turned(low_rank, square)[0:rows]
        own = bounds[lax.axis_index("tensor")]
        pick = rank_columns((LANES, own.shape[1]), 0, 1, rank).astype(jnp.bfloat16)
        each = jnp.dot(terms(low_rank, 2), pick, preferred_element_type=jnp.float32)
        own = inside(own, rows)
        each = jnp.where(jnp.concatenate([own, own]), each, 0.0)
        spread[...] = each.astype(jnp.bfloat16)

    for base, up, out in ((base_query, up_query, query), (base_value, up_value, value)):
        update = jnp.dot(spread[...], up[...], preferred_element_type=jnp.float32)
        update = update[0:rows] + update[rows:]
        out[...] = (base[...] + ADAPTER_SCALE * update).astype(out.dtype)


def finish(shares, bounds, operands, steps):
    rows = operands[0].shape[0]

    def columns(x):
        return pl.BlockSpec((x.shape[0], x.shape[1] // steps), lambda i: (0, i))

    return pl.pallas_call(
        functools.partial(finish_kernel, len(shares)),
        grid=(steps,),
        in_specs=[pl.BlockSpec(bounds.shape, lambda i: (0, 0, 0))]
        + [pl.BlockSpec(x.shape, lambda i: (0, 0)) for x in shares]
        + [columns(x) for x in operands],
        out_specs=[columns(x) for x in operands[:2]],
        out_shape=[jax.ShapeDtypeStruct(x.shape, jnp.bfloat16) for x in operands[:2]],
        scratch_shapes=[
            pltpu.VMEM((LANES, LANES), jnp.float32),
            pltpu.VMEM((2 * rows, bounds.shape[2]), jnp.bfloat16),
        ],
        name="finish",
    )(bounds, *shares, *operands)


def halving_order(total):
    bits = total.bit_length() - 1
    return [int(format(o, "b").zfill(bits)[::-1], 2) if bits else 0 for o in range(total)]


def reduce_blocks(partial, axis):
    step = 1
    while True:
        half = partial.shape[0] // 2
        came = swap(partial[half:], axis, step)
        if half == 1:
            return partial[0] + came[0]
        partial = partial[:half] + came
        step *= 2


def gather_blocks(x, axis):
    x = x[None]
    step = 1
    while step < lax.axis_size(axis):
        came = swap(x, axis, step)
        upper = (lax.axis_index(axis) & step) > 0
        x = jnp.concatenate([jnp.where(upper, came, x), jnp.where(upper, x, came)])
        step *= 2
    return x


def local(
    tokens,
    task_counts,
    task_embeddings,
    embedding_weight,
    down_factor_head,
    query_up_head,
    value_up_head,
    w_query,
    w_value,
):
    groups, ring, parts = lax.axis_size("groups"), lax.axis_size("task"), lax.axis_size("tensor")
    places = groups * ring
    tok_rows, shard_width = tokens.shape
    block_rows = tok_rows // parts
    own_tasks = task_counts.shape[0]
    block_tasks = own_tasks // parts
    rank = query_up_head.shape[1]
    hidden_rows = down_factor_head.shape[0]
    tensor = lax.axis_index("tensor")
    ring_shifts = list(range(ring))
    far_first = sorted(ring_shifts[1:], reverse=True)
    shifts = list(range(places))

    heads = {
        "value": Head(value_up_head, 1),
        "query": Head(query_up_head, 1),
        "down": Head(down_factor_head, 2),
    }

    def fetch(name, chunk):
        pieces = heads[name].cut(chunk, ring_shifts)
        got = {0: pieces[0]}
        for s in far_first:
            got[s] = swap(pieces[s], "task", s)
        return jnp.concatenate([got[s] for s in ring_shifts], axis=0)

    fetched = {}
    fetched["query", 0] = fetch("query", 0)

    share = own_tasks // parts
    embeddings = lax.dynamic_index_in_dim(
        task_embeddings.reshape(parts, share, -1), tensor, 0, keepdims=False
    )
    hidden = jax.nn.silu(
        jnp.dot(embeddings, embedding_weight, preferred_element_type=jnp.float32)
    ).astype(jnp.bfloat16)
    group_hidden = jnp.concatenate([hidden] + [swap(hidden, "groups", s) for s in range(1, groups)])
    ring_hidden = jnp.stack(
        [group_hidden] + [swap(group_hidden, "task", s) for s in ring_shifts[1:]]
    )
    every_hidden = gather_blocks(ring_hidden.reshape(places * share, -1), "tensor")
    every_hidden = every_hidden.reshape(parts, ring, groups, share, ring, hidden_rows)
    every_hidden = every_hidden.transpose(4, 2, 1, 0, 3, 5)
    every_hidden = every_hidden.reshape(ring, places * own_tasks, hidden_rows)
    every_hidden = jnp.concatenate(
        [
            lax.dynamic_index_in_dim(every_hidden, lax.axis_index("task") ^ s, 0, keepdims=False)
            for s in ring_shifts
        ],
        axis=1,
    )

    chunks = heads["down"].chunks
    for chunk in range(chunks):
        fetched["down", chunk] = fetch("down", chunk)
    fetched["value", 0] = fetch("value", 0)

    def emit(name, chunk):
        matrix = fetched[name, chunk]
        flat = jnp.dot(
            every_hidden, matrix.reshape(matrix.shape[0], -1), preferred_element_type=jnp.float32
        ).astype(jnp.bfloat16)
        return flat.reshape((places, own_tasks) + matrix.shape[1:])

    def send(made, sent):
        return {s: swap(made[s], PLACES, s) if s else made[s] for s in sent}

    late = [s for s in far_first if s >= ring // 2]
    early = [s for s in reversed(shifts) if s not in late]
    emitted = {}
    for name, chunk in [("query", 0), ("value", 0)] + [("down", c) for c in range(chunks)]:
        made = emit(name, chunk)
        emitted[name, chunk] = send(made, early)
        emitted[name, chunk].update(send(made, late))

    def ordered(pieces):
        return [pieces[s] for s in shifts]

    token_blocks = tokens.reshape(parts, block_rows, shard_width)
    order = halving_order(parts)
    turned = jnp.concatenate(
        [lax.dynamic_index_in_dim(token_blocks, tensor ^ s, 0, keepdims=False) for s in order]
    )
    base_query = jnp.dot(turned, w_query, preferred_element_type=jnp.float32)
    base_value = jnp.dot(turned, w_value, preferred_element_type=jnp.float32)
    base_query = reduce_blocks(base_query.reshape(parts, block_rows, -1), "tensor")
    base_value = reduce_blocks(base_value.reshape(parts, block_rows, -1), "tensor")

    def own_block(factors, above, below):
        moved = lax.all_to_all(factors, "tensor", split_axis=0, concat_axis=0, tiled=True)
        moved = moved.reshape(parts, block_tasks, rank, -1).transpose(1, 2, 0, 3)
        moved = moved.reshape(block_tasks, rank, -1)
        moved = jnp.pad(moved, ((0, 0), (above, below), (0, 0)))
        return moved.reshape(block_tasks * 2 * rank, -1)

    query_up_factors = heads["query"].join(ordered(emitted["query", 0]), shifts)
    own_query = own_block(query_up_factors, 0, rank)
    value_up_factors = heads["value"].join(ordered(emitted["value", 0]), shifts)
    own_value = own_block(value_up_factors, rank, 0)

    tallies = task_counts.reshape(parts, block_tasks)
    ends = jnp.cumsum(tallies, axis=1)
    bounds = jnp.stack([ends - tallies, ends], axis=1)
    bounds = jnp.repeat(bounds, 2 * rank, axis=2)

    down_factors, low_rank = None, []
    head = heads["down"]
    if head.by_lane:
        for chunk in range(chunks):
            pieces, start = emitted["down", chunk], chunk * head.width
            for half in [early, late] if chunk + 1 == chunks else [early + late]:
                some = [pieces[s] for s in half]
                low_rank = project(
                    some, half, head.stride, start, head.width, tokens, bounds, low_rank
                )
                down_factors = head.join(some, half, chunk, down_factors)
    else:
        down_factors = head.join(ordered(emitted["down", 0]), shifts)
        projected = jnp.einsum(
            "bpd,bmd->bpm",
            token_blocks,
            down_factors.reshape(parts, block_tasks * 2 * rank, shard_width),
            preferred_element_type=jnp.float32,
        )
        projected = jnp.where(jax.vmap(lambda b: inside(b, block_rows))(bounds), projected, 0.0)
        projected = projected.reshape(parts, block_rows, block_tasks, 2 * rank).sum(axis=2)
        projected = projected.transpose(0, 2, 1)
        low_rank = [
            lax.dynamic_index_in_dim(projected, tensor ^ s, 0, keepdims=False)
            for s in range(parts)
        ]
    shares = [low_rank[0]] + [swap(low_rank[s], "tensor", s) for s in range(1, parts)]
    query, value = finish(shares, bounds, [base_query, base_value, own_query, own_value], steps=4)
    return query, value, down_factors, query_up_factors, value_up_factors


def solution(mesh):
    return jax.shard_map(
        local,
        mesh=mesh,
        in_specs=(
            P(("groups", "task"), "tensor"),
            P(("groups", "task")),
            P(("groups", "task"), None),
            P(),
            P("task", None, "tensor"),
            P("task", None, "tensor"),
            P("task", None, "tensor"),
            P("tensor", None),
            P("tensor", None),
        ),
        out_specs=(
            P(("groups", "task", "tensor"), None),
            P(("groups", "task", "tensor"), None),
            P(("groups", "task"), None, "tensor"),
            P(("groups", "task"), None, "tensor"),
            P(("groups", "task"), None, "tensor"),
        ),
        check_vma=False,
    )
```

```python
import functools

import jax
import jax.numpy as jnp
from jax import lax
from jax.experimental import pallas as pl
from jax.experimental.pallas import tpu as pltpu
from jax.sharding import PartitionSpec as P


ADAPTER_SCALE = 2.0
LANES = 128
PLACES = ("groups", "task")
SMALL = pltpu.CompilerParams(vmem_limit_bytes=16 * 1024 * 1024)


def swap(x, axes, shift):
    total = lax.axis_size(axes)
    return lax.ppermute(x, axes, [(a, a ^ shift) for a in range(total)])


def place():
    return lax.axis_index("groups") * lax.axis_size("task") + lax.axis_index("task")


def through_vmem(moves, scratch, arrived, left):
    fetches = [
        pltpu.make_async_copy(source, scratch.at[k], arrived.at[k])
        for k, (source, _) in enumerate(moves)
    ]
    stores = [
        pltpu.make_async_copy(scratch.at[k], target, left.at[k])
        for k, (_, target) in enumerate(moves)
    ]
    for fetch in fetches:
        fetch.start()
    for fetch, store in zip(fetches, stores):
        fetch.wait()
        store.start()
    for store in stores:
        store.wait()


def vmem_scratch(count, shape, dtype):
    return [
        pltpu.VMEM((count,) + shape, dtype),
        pltpu.SemaphoreType.DMA((count,)),
        pltpu.SemaphoreType.DMA((count,)),
    ]


def cut_kernel(shifts, stride, start, width, source, *rest):
    moves = []
    for k, shift in enumerate(shifts):
        column = pl.multiple_of((place() ^ shift) * stride + start, LANES)
        moves.append((source.at[:, :, pl.ds(column, width)], rest[k]))
    through_vmem(moves, *rest[len(shifts) :])


def cut(head, shifts, stride, start, width):
    shape = head.shape[:2] + (width,)
    return pl.pallas_call(
        functools.partial(cut_kernel, shifts, stride, start, width),
        in_specs=[pl.BlockSpec(memory_space=pl.ANY)],
        out_specs=[pl.BlockSpec(memory_space=pl.ANY)] * len(shifts),
        out_shape=[jax.ShapeDtypeStruct(shape, head.dtype)] * len(shifts),
        scratch_shapes=vmem_scratch(len(shifts), shape, head.dtype),
        compiler_params=SMALL,
        name="cut",
    )(head)


def join_kernel(shifts, stride, start, width, *refs):
    whole = refs[-4]
    moves = []
    for k, shift in enumerate(shifts):
        column = pl.multiple_of((place() ^ shift) * stride + start, LANES)
        moves.append((refs[k], whole.at[:, :, pl.ds(column, width)]))
    through_vmem(moves, *refs[-3:])


def join(pieces, shifts, stride, start, width, columns, whole):
    operands = list(pieces) + ([] if whole is None else [whole])
    return pl.pallas_call(
        functools.partial(join_kernel, shifts, stride, start, width),
        in_specs=[pl.BlockSpec(memory_space=pl.ANY)] * len(operands),
        out_specs=pl.BlockSpec(memory_space=pl.ANY),
        out_shape=jax.ShapeDtypeStruct(pieces[0].shape[:2] + (columns,), pieces[0].dtype),
        scratch_shapes=vmem_scratch(len(pieces), pieces[0].shape, pieces[0].dtype),
        input_output_aliases={} if whole is None else {len(pieces): 0},
        compiler_params=SMALL,
        name="join",
    )(*operands)


def stack_kernel(shifts, *refs):
    count = len(shifts)
    moves = [(refs[k], refs[count].at[place() ^ s]) for k, s in enumerate(shifts)]
    through_vmem(moves, *refs[count + 1 :])


def stack(pieces, shifts):
    shape, dtype = pieces[0].shape, pieces[0].dtype
    return pl.pallas_call(
        functools.partial(stack_kernel, shifts),
        in_specs=[pl.BlockSpec(memory_space=pl.ANY)] * len(pieces),
        out_specs=pl.BlockSpec(memory_space=pl.ANY),
        out_shape=jax.ShapeDtypeStruct((len(pieces),) + shape, dtype),
        scratch_shapes=vmem_scratch(len(pieces), shape, dtype),
        compiler_params=SMALL,
        name="stack",
    )(*pieces)


def in_order(pieces, shifts):
    stack = jnp.zeros((len(pieces),) + pieces[0].shape, pieces[0].dtype)
    for piece, shift in zip(pieces, shifts):
        stack = lax.dynamic_update_index_in_dim(stack, piece, place() ^ shift, 0)
    return stack


class Head:
    def __init__(self, head, chunks):
        self.rank, self.columns = head.shape[1:]
        self.head = head
        self.places = lax.axis_size("groups") * lax.axis_size("task")
        self.stride = self.columns // self.places
        self.by_lane = self.stride % (LANES * chunks) == 0
        self.by_row = not self.by_lane and self.rank % self.places == 0
        self.chunks = chunks if self.by_lane else 1
        self.width = self.stride // self.chunks

    def cut(self, chunk, shifts):
        if self.by_lane:
            return cut(self.head, shifts, self.stride, chunk * self.width, self.width)
        rows = self.head.shape[0]
        if self.by_row:
            shares = self.head.reshape(rows, self.places, -1).transpose(1, 0, 2)
        else:
            shares = self.head.reshape(rows, self.rank, self.places, -1).transpose(2, 0, 1, 3)
        return [lax.dynamic_index_in_dim(shares, place() ^ s, 0, keepdims=False) for s in shifts]

    def join(self, pieces, shifts, chunk=0, whole=None):
        if self.by_lane:
            start = chunk * self.width
            return join(pieces, shifts, self.stride, start, self.width, self.columns, whole)
        if self.by_row:
            whole = stack(pieces, shifts).transpose(1, 0, 2)
        else:
            whole = in_order(pieces, shifts).transpose(1, 2, 0, 3)
        return whole.reshape(whole.shape[0], self.rank, self.columns)


def rank_columns(shape, rank_axis, column_axis, rank):
    of_column = lax.broadcasted_iota(jnp.int32, shape, column_axis) % rank
    return of_column == lax.broadcasted_iota(jnp.int32, shape, rank_axis)


def inside(bounds, rows):
    row = lax.broadcasted_iota(jnp.int32, (rows, bounds.shape[1]), 0)
    return (row >= bounds[0:1]) & (row < bounds[1:2])


def turned(x, square):
    square[...] = jnp.zeros(square.shape, square.dtype)
    square[0 : x.shape[0], 0 : x.shape[1]] = x
    return square[...].T


def terms(x, count):
    parts = []
    for _ in range(count):
        parts.append(x.astype(jnp.bfloat16))
        x = x - parts[-1].astype(jnp.float32)
    return jnp.concatenate(parts)


def project_kernel(shifts, parts, stride, start, width, tokens, bounds, *refs):
    pieces, refs = refs[: len(shifts)], refs[len(shifts) :]
    before, after = refs[:-parts], refs[-parts:]
    rows = tokens.shape[0] // parts
    tasks, rank = pieces[0].shape[0] // parts, pieces[0].shape[1]
    every = []
    for turn in range(parts):
        block = lax.axis_index("tensor") ^ turn
        found = jnp.zeros((rows, tasks * rank), jnp.float32)
        for k, shift in enumerate(shifts):
            column = pl.multiple_of((place() ^ shift) * stride + start, LANES)
            found += lax.dot_general(
                tokens[pl.ds(pl.multiple_of(block * rows, 8), rows), pl.ds(column, width)],
                pieces[k][pl.ds(block * tasks, tasks)].reshape(-1, width),
                (((1,), (1,)), ((), ())),
                preferred_element_type=jnp.float32,
            )
        every.append(jnp.where(inside(bounds[block], rows), found, 0.0))
    pick = rank_columns((tasks * rank, LANES), 1, 0, rank).astype(jnp.bfloat16)
    count = 3
    summed = jnp.dot(
        terms(jnp.concatenate(every), count), pick, preferred_element_type=jnp.float32
    ).reshape(count, parts * rows, LANES)
    low_rank = sum(summed[k] for k in range(count)).T
    for turn in range(parts):
        share = low_rank[0:rank, turn * rows : (turn + 1) * rows]
        after[turn][...] = share + before[turn][...] if before else share


def in_vmem(x):
    return pltpu.with_memory_space_constraint(x, pltpu.VMEM)


def project(pieces, shifts, stride, start, width, tokens, bounds, before, near):
    parts, rank = bounds.shape[0], pieces[0].shape[1]
    rows = tokens.shape[0] // parts
    if near:
        tokens, bounds = in_vmem(tokens), in_vmem(bounds)
        before = [in_vmem(x) for x in before]
    return pl.pallas_call(
        functools.partial(project_kernel, shifts, parts, stride, start, width),
        in_specs=[pl.BlockSpec(memory_space=pltpu.VMEM)] * (2 + len(pieces) + len(before)),
        out_shape=[jax.ShapeDtypeStruct((rank, rows), jnp.float32)] * parts,
        compiler_params=SMALL,
        name="project",
    )(tokens, bounds, *pieces, *before)


def finish_kernel(count, steps, bounds, *refs):
    shares, rest = refs[:count], refs[count:]
    bases, ups, outs, makes, square, sems = rest[0:2], rest[2:4], rest[4:6], rest[6:8], *rest[8:]
    rank, rows = shares[0].shape
    low_rank = shares[0][...]
    for share in shares[1:]:
        low_rank = low_rank + share[...]
    low_rank = turned(low_rank, square)[0:rows]
    own = bounds[lax.axis_index("tensor")]
    pick = rank_columns((LANES, own.shape[1]), 0, 1, rank).astype(jnp.bfloat16)
    spread = jnp.dot(terms(low_rank, 2), pick, preferred_element_type=jnp.float32)
    own = inside(own, rows)
    spread = jnp.where(jnp.concatenate([own, own]), spread, 0.0).astype(jnp.bfloat16)
    copies = []
    for step in range(steps):
        for k, (base, up, out, made) in enumerate(zip(bases, ups, outs, makes)):
            width = base.shape[1] // steps
            columns = pl.ds(step * width, width)
            update = jnp.dot(spread, up[:, columns], preferred_element_type=jnp.float32)
            update = update[0:rows] + update[rows:]
            made[:, columns] = (base[:, columns] + ADAPTER_SCALE * update).astype(made.dtype)
            copies.append(
                pltpu.make_async_copy(made.at[:, columns], out.at[:, columns], sems.at[k, step])
            )
            copies[-1].start()
    for copy in copies:
        copy.wait()


def finish(shares, bounds, operands, steps):
    operands = [in_vmem(x) for x in (bounds, *shares, *operands)]
    shapes = [x.shape for x in operands[-4:-2]]
    return pl.pallas_call(
        functools.partial(finish_kernel, len(shares), steps),
        in_specs=[pl.BlockSpec(memory_space=pltpu.VMEM)] * len(operands),
        out_specs=[pl.BlockSpec(memory_space=pl.ANY)] * 2,
        out_shape=[jax.ShapeDtypeStruct(shape, jnp.bfloat16) for shape in shapes],
        scratch_shapes=[pltpu.VMEM(shape, jnp.bfloat16) for shape in shapes]
        + [pltpu.VMEM((LANES, LANES), jnp.float32), pltpu.SemaphoreType.DMA((2, steps))],
        compiler_params=SMALL,
        name="finish",
    )(*operands)


def halving_order(total):
    bits = total.bit_length() - 1
    return [int(format(o, "b").zfill(bits)[::-1], 2) if bits else 0 for o in range(total)]


def reduce_blocks(partial, axis):
    step = 1
    while True:
        half = partial.shape[0] // 2
        came = swap(partial[half:], axis, step)
        if half == 1:
            return partial[0] + came[0]
        partial = partial[:half] + came
        step *= 2


def gather_blocks(x, axis):
    x = x[None]
    step = 1
    while step < lax.axis_size(axis):
        came = swap(x, axis, step)
        upper = (lax.axis_index(axis) & step) > 0
        x = jnp.concatenate([jnp.where(upper, came, x), jnp.where(upper, x, came)])
        step *= 2
    return x


def local(
    tokens,
    task_counts,
    task_embeddings,
    embedding_weight,
    down_factor_head,
    query_up_head,
    value_up_head,
    w_query,
    w_value,
):
    groups, ring, parts = lax.axis_size("groups"), lax.axis_size("task"), lax.axis_size("tensor")
    places = groups * ring
    tok_rows, shard_width = tokens.shape
    block_rows = tok_rows // parts
    own_tasks = task_counts.shape[0]
    block_tasks = own_tasks // parts
    rank = query_up_head.shape[1]
    hidden_rows = down_factor_head.shape[0]
    tensor = lax.axis_index("tensor")
    ring_shifts = list(range(ring))
    far_first = sorted(ring_shifts[1:], reverse=True)
    shifts = list(range(places))

    heads = {
        "value": Head(value_up_head, 1),
        "query": Head(query_up_head, 1),
        "down": Head(down_factor_head, 2),
    }

    def fetch(name, chunk):
        pieces = heads[name].cut(chunk, ring_shifts)
        got = {0: pieces[0]}
        for s in far_first:
            got[s] = swap(pieces[s], "task", s)
        return jnp.concatenate([got[s] for s in ring_shifts], axis=0)

    fetched = {}
    fetched["query", 0] = fetch("query", 0)

    share = own_tasks // parts
    embeddings = lax.dynamic_index_in_dim(
        task_embeddings.reshape(parts, share, -1), tensor, 0, keepdims=False
    )
    hidden = jax.nn.silu(
        jnp.dot(embeddings, embedding_weight, preferred_element_type=jnp.float32)
    ).astype(jnp.bfloat16)
    group_hidden = jnp.concatenate([hidden] + [swap(hidden, "groups", s) for s in range(1, groups)])
    ring_hidden = jnp.stack(
        [group_hidden] + [swap(group_hidden, "task", s) for s in ring_shifts[1:]]
    )
    every_hidden = gather_blocks(ring_hidden.reshape(places * share, -1), "tensor")
    every_hidden = every_hidden.reshape(parts, ring, groups, share, ring, hidden_rows)
    every_hidden = every_hidden.transpose(4, 2, 1, 0, 3, 5)
    every_hidden = every_hidden.reshape(ring, places * own_tasks, hidden_rows)
    every_hidden = jnp.concatenate(
        [
            lax.dynamic_index_in_dim(every_hidden, lax.axis_index("task") ^ s, 0, keepdims=False)
            for s in ring_shifts
        ],
        axis=1,
    )

    chunks = heads["down"].chunks
    for chunk in range(chunks):
        fetched["down", chunk] = fetch("down", chunk)
    fetched["value", 0] = fetch("value", 0)

    def emit(name, chunk):
        matrix = fetched[name, chunk]
        flat = jnp.dot(
            every_hidden, matrix.reshape(matrix.shape[0], -1), preferred_element_type=jnp.float32
        ).astype(jnp.bfloat16)
        return flat.reshape((places, own_tasks) + matrix.shape[1:])

    def send(made, sent):
        return {s: swap(made[s], PLACES, s) if s else made[s] for s in sent}

    late = [s for s in far_first if s >= ring // 2]
    early = [s for s in reversed(shifts) if s not in late]
    emitted = {}
    for name, chunk in [("query", 0), ("value", 0)] + [("down", c) for c in range(chunks)]:
        made = emit(name, chunk)
        emitted[name, chunk] = send(made, early)
        emitted[name, chunk].update(send(made, late))

    def ordered(pieces):
        return [pieces[s] for s in shifts]

    token_blocks = tokens.reshape(parts, block_rows, shard_width)
    order = halving_order(parts)
    turned = jnp.concatenate(
        [lax.dynamic_index_in_dim(token_blocks, tensor ^ s, 0, keepdims=False) for s in order]
    )
    base_query = jnp.dot(turned, w_query, preferred_element_type=jnp.float32)
    base_value = jnp.dot(turned, w_value, preferred_element_type=jnp.float32)
    base_query = reduce_blocks(base_query.reshape(parts, block_rows, -1), "tensor")
    base_value = reduce_blocks(base_value.reshape(parts, block_rows, -1), "tensor")

    def own_block(factors, above, below):
        moved = lax.all_to_all(factors, "tensor", split_axis=0, concat_axis=0, tiled=True)
        moved = moved.reshape(parts, block_tasks, rank, -1).transpose(1, 2, 0, 3)
        moved = moved.reshape(block_tasks, rank, -1)
        moved = jnp.pad(moved, ((0, 0), (above, below), (0, 0)))
        return moved.reshape(block_tasks * 2 * rank, -1)

    query_up_factors = heads["query"].join(ordered(emitted["query", 0]), shifts)
    own_query = own_block(query_up_factors, 0, rank)
    value_up_factors = heads["value"].join(ordered(emitted["value", 0]), shifts)
    own_value = own_block(value_up_factors, rank, 0)

    tallies = task_counts.reshape(parts, block_tasks)
    ends = jnp.cumsum(tallies, axis=1)
    begins = ends - tallies
    bounds = jnp.repeat(jnp.stack([begins, ends], axis=1), 2 * rank, axis=2)

    down_factors, low_rank = None, []
    head = heads["down"]
    if head.by_lane:
        for chunk in range(chunks):
            pieces, start = emitted["down", chunk], chunk * head.width
            for half in [early, late] if chunk + 1 == chunks else [early + late]:
                some = [pieces[s] for s in half]
                low_rank = project(
                    some, half, head.stride, start, head.width, tokens, bounds, low_rank,
                    half is late,
                )
                down_factors = head.join(some, half, chunk, down_factors)
    else:
        down_factors = head.join(ordered(emitted["down", 0]), shifts)
        projected = jnp.einsum(
            "bpd,bmd->bpm",
            token_blocks,
            down_factors.reshape(parts, block_tasks * 2 * rank, shard_width),
            preferred_element_type=jnp.float32,
        )
        projected = jnp.where(jax.vmap(lambda b: inside(b, block_rows))(bounds), projected, 0.0)
        projected = projected.reshape(parts, block_rows, block_tasks, 2 * rank).sum(axis=2)
        projected = projected.transpose(0, 2, 1)
        low_rank = [
            lax.dynamic_index_in_dim(projected, tensor ^ s, 0, keepdims=False)
            for s in range(parts)
        ]
    shares = [low_rank[0]] + [swap(low_rank[s], "tensor", s) for s in range(1, parts)]
    query, value = finish(shares, bounds, [base_query, base_value, own_query, own_value], steps=4)
    return query, value, down_factors, query_up_factors, value_up_factors


def solution(mesh):
    return jax.shard_map(
        local,
        mesh=mesh,
        in_specs=(
            P(("groups", "task"), "tensor"),
            P(("groups", "task")),
            P(("groups", "task"), None),
            P(),
            P("task", None, "tensor"),
            P("task", None, "tensor"),
            P("task", None, "tensor"),
            P("tensor", None),
            P("tensor", None),
        ),
        out_specs=(
            P(("groups", "task", "tensor"), None),
            P(("groups", "task", "tensor"), None),
            P(("groups", "task"), None, "tensor"),
            P(("groups", "task"), None, "tensor"),
            P(("groups", "task"), None, "tensor"),
        ),
        check_vma=False,
    )
```

```python
import functools

import jax
import jax.numpy as jnp
from jax import lax
from jax.experimental import pallas as pl
from jax.experimental.pallas import tpu as pltpu
from jax.sharding import PartitionSpec as P


ADAPTER_SCALE = 2.0
LANES = 128
PLACES = ("groups", "task")
SMALL = pltpu.CompilerParams(vmem_limit_bytes=16 * 1024 * 1024)


def swap(x, axes, shift):
    total = lax.axis_size(axes)
    return lax.ppermute(x, axes, [(a, a ^ shift) for a in range(total)])


def place():
    return lax.axis_index("groups") * lax.axis_size("task") + lax.axis_index("task")


def through_vmem(moves, scratch, arrived, left):
    fetches = [
        pltpu.make_async_copy(source, scratch.at[k], arrived.at[k])
        for k, (source, _) in enumerate(moves)
    ]
    stores = [
        pltpu.make_async_copy(scratch.at[k], target, left.at[k])
        for k, (_, target) in enumerate(moves)
    ]
    for fetch in fetches:
        fetch.start()
    for fetch, store in zip(fetches, stores):
        fetch.wait()
        store.start()
    for store in stores:
        store.wait()


def vmem_scratch(count, shape, dtype):
    return [
        pltpu.VMEM((count,) + shape, dtype),
        pltpu.SemaphoreType.DMA((count,)),
        pltpu.SemaphoreType.DMA((count,)),
    ]


def cut_kernel(shifts, stride, start, width, source, *rest):
    moves = []
    for k, shift in enumerate(shifts):
        column = pl.multiple_of((place() ^ shift) * stride + start, LANES)
        moves.append((source.at[:, :, pl.ds(column, width)], rest[k]))
    through_vmem(moves, *rest[len(shifts) :])


def cut(head, shifts, stride, start, width):
    shape = head.shape[:2] + (width,)
    return pl.pallas_call(
        functools.partial(cut_kernel, shifts, stride, start, width),
        in_specs=[pl.BlockSpec(memory_space=pl.ANY)],
        out_specs=[pl.BlockSpec(memory_space=pl.ANY)] * len(shifts),
        out_shape=[jax.ShapeDtypeStruct(shape, head.dtype)] * len(shifts),
        scratch_shapes=vmem_scratch(len(shifts), shape, head.dtype),
        compiler_params=SMALL,
        name="cut",
    )(pltpu.with_memory_space_constraint(head, pltpu.HBM))


def cut_row_kernel(shifts, rank, source, *pieces):
    rows = source.shape[0] // rank
    at = lax.broadcasted_iota(jnp.int32, (rows, source.shape[0]), 1)
    at = at - rank * lax.broadcasted_iota(jnp.int32, (rows, source.shape[0]), 0)
    for shift, piece in zip(shifts, pieces):
        pick = jnp.where(at == (place() ^ shift), 1.0, 0.0).astype(source.dtype)
        picked = jnp.dot(pick, source[...], preferred_element_type=jnp.float32)
        piece[...] = picked.astype(piece.dtype)


def cut_row(head, shifts):
    rows, rank, columns = head.shape
    return pl.pallas_call(
        functools.partial(cut_row_kernel, shifts, rank),
        out_shape=[jax.ShapeDtypeStruct((rows, columns), head.dtype)] * len(shifts),
        compiler_params=SMALL,
        name="cut_row",
    )(head.reshape(rows * rank, columns))


def join_kernel(shifts, stride, start, width, *refs):
    whole = refs[-4]
    moves = []
    for k, shift in enumerate(shifts):
        column = pl.multiple_of((place() ^ shift) * stride + start, LANES)
        moves.append((refs[k], whole.at[:, :, pl.ds(column, width)]))
    through_vmem(moves, *refs[-3:])


def join(pieces, shifts, stride, start, width, columns, whole):
    operands = list(pieces) + ([] if whole is None else [whole])
    return pl.pallas_call(
        functools.partial(join_kernel, shifts, stride, start, width),
        in_specs=[pl.BlockSpec(memory_space=pl.ANY)] * len(operands),
        out_specs=pl.BlockSpec(memory_space=pl.ANY),
        out_shape=jax.ShapeDtypeStruct(pieces[0].shape[:2] + (columns,), pieces[0].dtype),
        scratch_shapes=vmem_scratch(len(pieces), pieces[0].shape, pieces[0].dtype),
        input_output_aliases={} if whole is None else {len(pieces): 0},
        compiler_params=SMALL,
        name="join",
    )(*operands)


def stack_kernel(shifts, *refs):
    count = len(shifts)
    moves = [(refs[k], refs[count].at[place() ^ s]) for k, s in enumerate(shifts)]
    through_vmem(moves, *refs[count + 1 :])


def stack(pieces, shifts):
    shape, dtype = pieces[0].shape, pieces[0].dtype
    return pl.pallas_call(
        functools.partial(stack_kernel, shifts),
        in_specs=[pl.BlockSpec(memory_space=pl.ANY)] * len(pieces),
        out_specs=pl.BlockSpec(memory_space=pl.ANY),
        out_shape=jax.ShapeDtypeStruct((len(pieces),) + shape, dtype),
        scratch_shapes=vmem_scratch(len(pieces), shape, dtype),
        compiler_params=SMALL,
        name="stack",
    )(*pieces)


def in_order(pieces, shifts):
    stack = jnp.zeros((len(pieces),) + pieces[0].shape, pieces[0].dtype)
    for piece, shift in zip(pieces, shifts):
        stack = lax.dynamic_update_index_in_dim(stack, piece, place() ^ shift, 0)
    return stack


class Head:
    def __init__(self, head, chunks):
        self.rank, self.columns = head.shape[1:]
        self.head = head
        self.places = lax.axis_size("groups") * lax.axis_size("task")
        self.stride = self.columns // self.places
        self.by_lane = self.stride % (LANES * chunks) == 0
        self.by_row = not self.by_lane and self.rank == self.places
        self.chunks = chunks if self.by_lane else 1
        self.width = self.stride // self.chunks

    def cut(self, chunk, shifts):
        if self.by_lane:
            return cut(self.head, shifts, self.stride, chunk * self.width, self.width)
        if self.by_row:
            return cut_row(self.head, shifts)
        shares = self.head.reshape(-1, self.rank, self.places, self.stride).transpose(2, 0, 1, 3)
        return [lax.dynamic_index_in_dim(shares, place() ^ s, 0, keepdims=False) for s in shifts]

    def join(self, pieces, shifts, chunk=0, whole=None):
        if self.by_lane:
            start = chunk * self.width
            return join(pieces, shifts, self.stride, start, self.width, self.columns, whole)
        if self.by_row:
            whole = stack(pieces, shifts).transpose(1, 0, 2)
        else:
            whole = in_order(pieces, shifts).transpose(1, 2, 0, 3)
        return whole.reshape(whole.shape[0], self.rank, self.columns)


def rank_columns(shape, rank_axis, column_axis, rank):
    of_column = lax.broadcasted_iota(jnp.int32, shape, column_axis) % rank
    return of_column == lax.broadcasted_iota(jnp.int32, shape, rank_axis)


def inside(bounds, rows):
    row = lax.broadcasted_iota(jnp.int32, (rows, bounds.shape[1]), 0)
    return (row >= bounds[0:1]) & (row < bounds[1:2])


def turned(x, square):
    square[...] = jnp.zeros(square.shape, square.dtype)
    square[0 : x.shape[0], 0 : x.shape[1]] = x
    return square[...].T


def terms(x, count):
    parts = []
    for _ in range(count):
        parts.append(x.astype(jnp.bfloat16))
        x = x - parts[-1].astype(jnp.float32)
    return jnp.concatenate(parts)


def project_kernel(shifts, parts, stride, start, width, tokens, bounds, *refs):
    pieces, refs = refs[: len(shifts)], refs[len(shifts) :]
    before, after = refs[:-parts], refs[-parts:]
    rows = tokens.shape[0] // parts
    tasks, rank = pieces[0].shape[0] // parts, pieces[0].shape[1]
    every = []
    for turn in range(parts):
        block = lax.axis_index("tensor") ^ turn
        found = jnp.zeros((rows, tasks * rank), jnp.float32)
        for k, shift in enumerate(shifts):
            column = pl.multiple_of((place() ^ shift) * stride + start, LANES)
            found += lax.dot_general(
                tokens[pl.ds(pl.multiple_of(block * rows, 8), rows), pl.ds(column, width)],
                pieces[k][pl.ds(block * tasks, tasks)].reshape(-1, width),
                (((1,), (1,)), ((), ())),
                preferred_element_type=jnp.float32,
            )
        every.append(jnp.where(inside(bounds[block], rows), found, 0.0))
    pick = rank_columns((tasks * rank, LANES), 1, 0, rank).astype(jnp.bfloat16)
    count = 3
    summed = jnp.dot(
        terms(jnp.concatenate(every), count), pick, preferred_element_type=jnp.float32
    ).reshape(count, parts * rows, LANES)
    low_rank = sum(summed[k] for k in range(count)).T
    for turn in range(parts):
        share = low_rank[0:rank, turn * rows : (turn + 1) * rows]
        after[turn][...] = share + before[turn][...] if before else share


def in_vmem(x):
    return pltpu.with_memory_space_constraint(x, pltpu.VMEM)


def project(pieces, shifts, stride, start, width, tokens, bounds, before, near):
    parts, rank = bounds.shape[0], pieces[0].shape[1]
    rows = tokens.shape[0] // parts
    if near:
        tokens, bounds = in_vmem(tokens), in_vmem(bounds)
        before = [in_vmem(x) for x in before]
    return pl.pallas_call(
        functools.partial(project_kernel, shifts, parts, stride, start, width),
        in_specs=[pl.BlockSpec(memory_space=pltpu.VMEM)] * (2 + len(pieces) + len(before)),
        out_shape=[jax.ShapeDtypeStruct((rank, rows), jnp.float32)] * parts,
        compiler_params=SMALL,
        name="project",
    )(tokens, bounds, *pieces, *before)


def finish_kernel(count, steps, bounds, *refs):
    shares, rest = refs[:count], refs[count:]
    bases, ups, outs, makes, square, sems = rest[0:2], rest[2:4], rest[4:6], rest[6:8], *rest[8:]
    rank, rows = shares[0].shape
    low_rank = shares[0][...]
    for share in shares[1:]:
        low_rank = low_rank + share[...]
    low_rank = turned(low_rank, square)[0:rows]
    own = bounds[lax.axis_index("tensor")]
    pick = rank_columns((LANES, own.shape[1]), 0, 1, rank).astype(jnp.bfloat16)
    spread = jnp.dot(terms(low_rank, 2), pick, preferred_element_type=jnp.float32)
    own = inside(own, rows)
    spread = jnp.where(jnp.concatenate([own, own]), spread, 0.0).astype(jnp.bfloat16)
    copies = []
    for step in range(steps):
        for k, (base, up, out, made) in enumerate(zip(bases, ups, outs, makes)):
            width = base.shape[1] // steps
            columns = pl.ds(step * width, width)
            update = jnp.dot(spread, up[:, columns], preferred_element_type=jnp.float32)
            update = update[0:rows] + update[rows:]
            made[:, columns] = (base[:, columns] + ADAPTER_SCALE * update).astype(made.dtype)
            copies.append(
                pltpu.make_async_copy(made.at[:, columns], out.at[:, columns], sems.at[k, step])
            )
            copies[-1].start()
    for copy in copies:
        copy.wait()


def finish(shares, bounds, operands, steps):
    operands = [in_vmem(x) for x in (bounds, *shares, *operands)]
    shapes = [x.shape for x in operands[-4:-2]]
    return pl.pallas_call(
        functools.partial(finish_kernel, len(shares), steps),
        in_specs=[pl.BlockSpec(memory_space=pltpu.VMEM)] * len(operands),
        out_specs=[pl.BlockSpec(memory_space=pl.ANY)] * 2,
        out_shape=[jax.ShapeDtypeStruct(shape, jnp.bfloat16) for shape in shapes],
        scratch_shapes=[pltpu.VMEM(shape, jnp.bfloat16) for shape in shapes]
        + [pltpu.VMEM((LANES, LANES), jnp.float32), pltpu.SemaphoreType.DMA((2, steps))],
        compiler_params=SMALL,
        name="finish",
    )(*operands)


def halving_order(total):
    bits = total.bit_length() - 1
    return [int(format(o, "b").zfill(bits)[::-1], 2) if bits else 0 for o in range(total)]


def reduce_blocks(partial, axis):
    step = 1
    while True:
        half = partial.shape[0] // 2
        came = swap(partial[half:], axis, step)
        if half == 1:
            return partial[0] + came[0]
        partial = partial[:half] + came
        step *= 2


def gather_blocks(x, axis):
    x = x[None]
    step = 1
    while step < lax.axis_size(axis):
        came = swap(x, axis, step)
        upper = (lax.axis_index(axis) & step) > 0
        x = jnp.concatenate([jnp.where(upper, came, x), jnp.where(upper, x, came)])
        step *= 2
    return x


def local(
    tokens,
    task_counts,
    task_embeddings,
    embedding_weight,
    down_factor_head,
    query_up_head,
    value_up_head,
    w_query,
    w_value,
):
    groups, ring, parts = lax.axis_size("groups"), lax.axis_size("task"), lax.axis_size("tensor")
    places = groups * ring
    tok_rows, shard_width = tokens.shape
    block_rows = tok_rows // parts
    own_tasks = task_counts.shape[0]
    block_tasks = own_tasks // parts
    rank = query_up_head.shape[1]
    hidden_rows = down_factor_head.shape[0]
    tensor = lax.axis_index("tensor")
    ring_shifts = list(range(ring))
    far_first = sorted(ring_shifts[1:], reverse=True)
    shifts = list(range(places))

    heads = {
        "value": Head(value_up_head, 1),
        "query": Head(query_up_head, 1),
        "down": Head(down_factor_head, 2),
    }

    def fetch(name, chunk):
        pieces = heads[name].cut(chunk, ring_shifts)
        got = {0: pieces[0]}
        for s in far_first:
            got[s] = swap(pieces[s], "task", s)
        return jnp.concatenate([got[s] for s in ring_shifts], axis=0)

    fetched = {}
    fetched["query", 0] = fetch("query", 0)

    share = own_tasks // parts
    embeddings = lax.dynamic_index_in_dim(
        task_embeddings.reshape(parts, share, -1), tensor, 0, keepdims=False
    )
    hidden = jax.nn.silu(
        jnp.dot(embeddings, embedding_weight, preferred_element_type=jnp.float32)
    ).astype(jnp.bfloat16)
    group_hidden = jnp.concatenate([hidden] + [swap(hidden, "groups", s) for s in range(1, groups)])
    ring_hidden = jnp.stack(
        [group_hidden] + [swap(group_hidden, "task", s) for s in ring_shifts[1:]]
    )
    every_hidden = gather_blocks(ring_hidden.reshape(places * share, -1), "tensor")
    every_hidden = every_hidden.reshape(parts, ring, groups, share, ring, hidden_rows)
    every_hidden = every_hidden.transpose(4, 2, 1, 0, 3, 5)
    every_hidden = every_hidden.reshape(ring, places * own_tasks, hidden_rows)
    every_hidden = jnp.concatenate(
        [
            lax.dynamic_index_in_dim(every_hidden, lax.axis_index("task") ^ s, 0, keepdims=False)
            for s in ring_shifts
        ],
        axis=1,
    )

    chunks = heads["down"].chunks
    for chunk in range(chunks):
        fetched["down", chunk] = fetch("down", chunk)
    fetched["value", 0] = fetch("value", 0)

    def emit(name, chunk):
        matrix = fetched[name, chunk]
        flat = jnp.dot(
            every_hidden, matrix.reshape(matrix.shape[0], -1), preferred_element_type=jnp.float32
        ).astype(jnp.bfloat16)
        return flat.reshape((places, own_tasks) + matrix.shape[1:])

    def send(made, sent):
        return {s: swap(made[s], PLACES, s) if s else made[s] for s in sent}

    crossing = [s for s in reversed(shifts) if s % ring >= ring // 2]
    early = [s for s in crossing if s >= ring] + [s for s in reversed(shifts) if s % ring == 0]
    late = [s for s in crossing if s < ring]
    late = late + [s for s in reversed(shifts) if 0 < s % ring < ring // 2]
    emitted = {}
    for name, chunk in [("query", 0), ("value", 0)] + [("down", c) for c in range(chunks)]:
        made = emit(name, chunk)
        emitted[name, chunk] = send(made, early)
        emitted[name, chunk].update(send(made, late))

    def ordered(pieces):
        return [pieces[s] for s in shifts]

    token_blocks = tokens.reshape(parts, block_rows, shard_width)
    order = halving_order(parts)
    turned = jnp.concatenate(
        [lax.dynamic_index_in_dim(token_blocks, tensor ^ s, 0, keepdims=False) for s in order]
    )
    base_query = jnp.dot(turned, w_query, preferred_element_type=jnp.float32)
    base_value = jnp.dot(turned, w_value, preferred_element_type=jnp.float32)
    base_query = reduce_blocks(base_query.reshape(parts, block_rows, -1), "tensor")
    base_value = reduce_blocks(base_value.reshape(parts, block_rows, -1), "tensor")

    def own_block(factors, above, below):
        moved = lax.all_to_all(factors, "tensor", split_axis=0, concat_axis=0, tiled=True)
        moved = moved.reshape(parts, block_tasks, rank, -1).transpose(1, 2, 0, 3)
        moved = moved.reshape(block_tasks, rank, -1)
        moved = jnp.pad(moved, ((0, 0), (above, below), (0, 0)))
        return moved.reshape(block_tasks * 2 * rank, -1)

    query_up_factors = heads["query"].join(ordered(emitted["query", 0]), shifts)
    own_query = own_block(query_up_factors, 0, rank)
    value_up_factors = heads["value"].join(ordered(emitted["value", 0]), shifts)
    own_value = own_block(value_up_factors, rank, 0)

    tallies = task_counts.reshape(parts, block_tasks)
    ends = jnp.cumsum(tallies, axis=1)
    begins = ends - tallies
    bounds = jnp.repeat(jnp.stack([begins, ends], axis=1), 2 * rank, axis=2)

    down_factors, low_rank = None, []
    head = heads["down"]
    if head.by_lane:
        for chunk in range(chunks):
            pieces, start = emitted["down", chunk], chunk * head.width
            for half in [early, late] if chunk + 1 == chunks else [early + late]:
                some = [pieces[s] for s in half]
                low_rank = project(
                    some, half, head.stride, start, head.width, tokens, bounds, low_rank,
                    half is late,
                )
                down_factors = head.join(some, half, chunk, down_factors)
    else:
        down_factors = head.join(ordered(emitted["down", 0]), shifts)
        projected = jnp.einsum(
            "bpd,bmd->bpm",
            token_blocks,
            down_factors.reshape(parts, block_tasks * 2 * rank, shard_width),
            preferred_element_type=jnp.float32,
        )
        projected = jnp.where(jax.vmap(lambda b: inside(b, block_rows))(bounds), projected, 0.0)
        projected = projected.reshape(parts, block_rows, block_tasks, 2 * rank).sum(axis=2)
        projected = projected.transpose(0, 2, 1)
        low_rank = [
            lax.dynamic_index_in_dim(projected, tensor ^ s, 0, keepdims=False)
            for s in range(parts)
        ]
    shares = [low_rank[0]] + [swap(low_rank[s], "tensor", s) for s in range(1, parts)]
    query, value = finish(shares, bounds, [base_query, base_value, own_query, own_value], steps=4)
    return query, value, down_factors, query_up_factors, value_up_factors


def solution(mesh):
    return jax.shard_map(
        local,
        mesh=mesh,
        in_specs=(
            P(("groups", "task"), "tensor"),
            P(("groups", "task")),
            P(("groups", "task"), None),
            P(),
            P("task", None, "tensor"),
            P("task", None, "tensor"),
            P("task", None, "tensor"),
            P("tensor", None),
            P("tensor", None),
        ),
        out_specs=(
            P(("groups", "task", "tensor"), None),
            P(("groups", "task", "tensor"), None),
            P(("groups", "task"), None, "tensor"),
            P(("groups", "task"), None, "tensor"),
            P(("groups", "task"), None, "tensor"),
        ),
        check_vma=False,
    )
```

```python
import functools

import jax
import jax.numpy as jnp
from jax import lax
from jax.experimental import pallas as pl
from jax.experimental.pallas import tpu as pltpu
from jax.sharding import PartitionSpec as P


ADAPTER_SCALE = 2.0
LANES = 128
PLACES = ("groups", "task")
SMALL = pltpu.CompilerParams(vmem_limit_bytes=16 * 1024 * 1024)


def swap(x, axes, shift):
    total = lax.axis_size(axes)
    return lax.ppermute(x, axes, [(a, a ^ shift) for a in range(total)])


def place():
    return lax.axis_index("groups") * lax.axis_size("task") + lax.axis_index("task")


def through_vmem(moves, scratch, arrived, left):
    fetches = [
        pltpu.make_async_copy(source, scratch.at[k], arrived.at[k])
        for k, (source, _) in enumerate(moves)
    ]
    stores = [
        pltpu.make_async_copy(scratch.at[k], target, left.at[k])
        for k, (_, target) in enumerate(moves)
    ]
    for fetch in fetches:
        fetch.start()
    for fetch, store in zip(fetches, stores):
        fetch.wait()
        store.start()
    for store in stores:
        store.wait()


def vmem_scratch(count, shape, dtype):
    return [
        pltpu.VMEM((count,) + shape, dtype),
        pltpu.SemaphoreType.DMA((count,)),
        pltpu.SemaphoreType.DMA((count,)),
    ]


def cut_kernel(shifts, stride, start, width, source, *rest):
    moves = []
    for k, shift in enumerate(shifts):
        column = pl.multiple_of((place() ^ shift) * stride + start, LANES)
        moves.append((source.at[:, :, pl.ds(column, width)], rest[k]))
    through_vmem(moves, *rest[len(shifts) :])


def cut(head, shifts, stride, start, width):
    shape = head.shape[:2] + (width,)
    return pl.pallas_call(
        functools.partial(cut_kernel, shifts, stride, start, width),
        in_specs=[pl.BlockSpec(memory_space=pl.ANY)],
        out_specs=[pl.BlockSpec(memory_space=pl.ANY)] * len(shifts),
        out_shape=[jax.ShapeDtypeStruct(shape, head.dtype)] * len(shifts),
        scratch_shapes=vmem_scratch(len(shifts), shape, head.dtype),
        compiler_params=SMALL,
        name="cut",
    )(pltpu.with_memory_space_constraint(head, pltpu.HBM))


def cut_row_kernel(shifts, rank, source, *pieces):
    rows = source.shape[0] // rank
    at = lax.broadcasted_iota(jnp.int32, (rows, source.shape[0]), 1)
    at = at - rank * lax.broadcasted_iota(jnp.int32, (rows, source.shape[0]), 0)
    for shift, piece in zip(shifts, pieces):
        pick = jnp.where(at == (place() ^ shift), 1.0, 0.0).astype(source.dtype)
        picked = jnp.dot(pick, source[...], preferred_element_type=jnp.float32)
        piece[...] = picked.astype(piece.dtype)


def cut_row(head, shifts):
    rows, rank, columns = head.shape
    return pl.pallas_call(
        functools.partial(cut_row_kernel, shifts, rank),
        out_shape=[jax.ShapeDtypeStruct((rows, columns), head.dtype)] * len(shifts),
        compiler_params=SMALL,
        name="cut_row",
    )(head.reshape(rows * rank, columns))


def join_kernel(shifts, stride, start, width, *refs):
    whole = refs[-4]
    moves = []
    for k, shift in enumerate(shifts):
        column = pl.multiple_of((place() ^ shift) * stride + start, LANES)
        moves.append((refs[k], whole.at[:, :, pl.ds(column, width)]))
    through_vmem(moves, *refs[-3:])


def join(pieces, shifts, stride, start, width, columns, whole):
    operands = list(pieces) + ([] if whole is None else [whole])
    return pl.pallas_call(
        functools.partial(join_kernel, shifts, stride, start, width),
        in_specs=[pl.BlockSpec(memory_space=pl.ANY)] * len(operands),
        out_specs=pl.BlockSpec(memory_space=pl.ANY),
        out_shape=jax.ShapeDtypeStruct(pieces[0].shape[:2] + (columns,), pieces[0].dtype),
        scratch_shapes=vmem_scratch(len(pieces), pieces[0].shape, pieces[0].dtype),
        input_output_aliases={} if whole is None else {len(pieces): 0},
        compiler_params=SMALL,
        name="join",
    )(*operands)


def stack_kernel(shifts, *refs):
    count = len(shifts)
    moves = [(refs[k], refs[count].at[place() ^ s]) for k, s in enumerate(shifts)]
    through_vmem(moves, *refs[count + 1 :])


def stack(pieces, shifts):
    shape, dtype = pieces[0].shape, pieces[0].dtype
    return pl.pallas_call(
        functools.partial(stack_kernel, shifts),
        in_specs=[pl.BlockSpec(memory_space=pl.ANY)] * len(pieces),
        out_specs=pl.BlockSpec(memory_space=pl.ANY),
        out_shape=jax.ShapeDtypeStruct((len(pieces),) + shape, dtype),
        scratch_shapes=vmem_scratch(len(pieces), shape, dtype),
        compiler_params=SMALL,
        name="stack",
    )(*pieces)


def in_order(pieces, shifts):
    stack = jnp.zeros((len(pieces),) + pieces[0].shape, pieces[0].dtype)
    for piece, shift in zip(pieces, shifts):
        stack = lax.dynamic_update_index_in_dim(stack, piece, place() ^ shift, 0)
    return stack


class Head:
    def __init__(self, head, chunks):
        self.rank, self.columns = head.shape[1:]
        self.head = head
        self.places = lax.axis_size("groups") * lax.axis_size("task")
        self.stride = self.columns // self.places
        self.by_lane = self.stride % (LANES * chunks) == 0
        self.by_row = not self.by_lane and self.rank == self.places
        self.chunks = chunks if self.by_lane else 1
        self.width = self.stride // self.chunks

    def cut(self, chunk, shifts):
        if self.by_lane:
            return cut(self.head, shifts, self.stride, chunk * self.width, self.width)
        if self.by_row:
            return cut_row(self.head, shifts)
        shares = self.head.reshape(-1, self.rank, self.places, self.stride).transpose(2, 0, 1, 3)
        return [lax.dynamic_index_in_dim(shares, place() ^ s, 0, keepdims=False) for s in shifts]

    def join(self, pieces, shifts, chunk=0, whole=None):
        if self.by_lane:
            start = chunk * self.width
            return join(pieces, shifts, self.stride, start, self.width, self.columns, whole)
        if self.by_row:
            whole = stack(pieces, shifts).transpose(1, 0, 2)
        else:
            whole = in_order(pieces, shifts).transpose(1, 2, 0, 3)
        return whole.reshape(whole.shape[0], self.rank, self.columns)


def rank_columns(shape, rank_axis, column_axis, rank):
    of_column = lax.broadcasted_iota(jnp.int32, shape, column_axis) % rank
    return of_column == lax.broadcasted_iota(jnp.int32, shape, rank_axis)


def inside(bounds, rows):
    row = lax.broadcasted_iota(jnp.int32, (rows, bounds.shape[1]), 0)
    return (row >= bounds[0:1]) & (row < bounds[1:2])


def turned(x, square):
    square[...] = jnp.zeros(square.shape, square.dtype)
    square[0 : x.shape[0], 0 : x.shape[1]] = x
    return square[...].T


def terms(x, count):
    parts = []
    for _ in range(count):
        parts.append(x.astype(jnp.bfloat16))
        x = x - parts[-1].astype(jnp.float32)
    return jnp.concatenate(parts)


def project_kernel(shifts, parts, stride, start, width, tokens, bounds, *refs):
    pieces, refs = refs[: len(shifts)], refs[len(shifts) :]
    before, after = refs[:-parts], refs[-parts:]
    rows = tokens.shape[0] // parts
    tasks, rank = pieces[0].shape[0] // parts, pieces[0].shape[1]
    every = []
    for turn in range(parts):
        block = lax.axis_index("tensor") ^ turn
        found = jnp.zeros((rows, tasks * rank), jnp.float32)
        for k, shift in enumerate(shifts):
            column = pl.multiple_of((place() ^ shift) * stride + start, LANES)
            found += lax.dot_general(
                tokens[pl.ds(pl.multiple_of(block * rows, 8), rows), pl.ds(column, width)],
                pieces[k][pl.ds(block * tasks, tasks)].reshape(-1, width),
                (((1,), (1,)), ((), ())),
                preferred_element_type=jnp.float32,
            )
        every.append(jnp.where(inside(bounds[block], rows), found, 0.0))
    pick = rank_columns((tasks * rank, LANES), 1, 0, rank).astype(jnp.bfloat16)
    count = 3
    summed = jnp.dot(
        terms(jnp.concatenate(every), count), pick, preferred_element_type=jnp.float32
    ).reshape(count, parts * rows, LANES)
    low_rank = sum(summed[k] for k in range(count)).T
    for turn in range(parts):
        share = low_rank[0:rank, turn * rows : (turn + 1) * rows]
        after[turn][...] = share + before[turn][...] if before else share


def in_vmem(x):
    return pltpu.with_memory_space_constraint(x, pltpu.VMEM)


def project(pieces, shifts, stride, start, width, tokens, bounds, before, near):
    parts, rank = bounds.shape[0], pieces[0].shape[1]
    rows = tokens.shape[0] // parts
    if near:
        tokens, bounds = in_vmem(tokens), in_vmem(bounds)
        before = [in_vmem(x) for x in before]
    return pl.pallas_call(
        functools.partial(project_kernel, shifts, parts, stride, start, width),
        in_specs=[pl.BlockSpec(memory_space=pltpu.VMEM)] * (2 + len(pieces) + len(before)),
        out_shape=[jax.ShapeDtypeStruct((rank, rows), jnp.float32)] * parts,
        compiler_params=SMALL,
        name="project",
    )(tokens, bounds, *pieces, *before)


def finish_kernel(count, steps, bounds, *refs):
    shares, rest = refs[:count], refs[count:]
    bases, ups, outs, makes, square, sems = rest[0:2], rest[2:4], rest[4:6], rest[6:8], *rest[8:]
    rank, rows = shares[0].shape
    low_rank = shares[0][...]
    for share in shares[1:]:
        low_rank = low_rank + share[...]
    low_rank = turned(low_rank, square)[0:rows]
    own = bounds[lax.axis_index("tensor")]
    pick = rank_columns((LANES, own.shape[1]), 0, 1, rank).astype(jnp.bfloat16)
    spread = jnp.dot(terms(low_rank, 2), pick, preferred_element_type=jnp.float32)
    own = inside(own, rows)
    spread = jnp.where(jnp.concatenate([own, own]), spread, 0.0).astype(jnp.bfloat16)
    copies = []
    for step in range(steps):
        for k, (base, up, out, made) in enumerate(zip(bases, ups, outs, makes)):
            width = base.shape[1] // steps
            columns = pl.ds(step * width, width)
            update = jnp.dot(spread, up[:, columns], preferred_element_type=jnp.float32)
            update = update[0:rows] + update[rows:]
            made[:, columns] = (base[:, columns] + ADAPTER_SCALE * update).astype(made.dtype)
            copies.append(
                pltpu.make_async_copy(made.at[:, columns], out.at[:, columns], sems.at[k, step])
            )
            copies[-1].start()
    for copy in copies:
        copy.wait()


def finish(shares, bounds, operands, steps):
    operands = [in_vmem(x) for x in (bounds, *shares, *operands)]
    shapes = [x.shape for x in operands[-4:-2]]
    return pl.pallas_call(
        functools.partial(finish_kernel, len(shares), steps),
        in_specs=[pl.BlockSpec(memory_space=pltpu.VMEM)] * len(operands),
        out_specs=[pl.BlockSpec(memory_space=pl.ANY)] * 2,
        out_shape=[jax.ShapeDtypeStruct(shape, jnp.bfloat16) for shape in shapes],
        scratch_shapes=[pltpu.VMEM(shape, jnp.bfloat16) for shape in shapes]
        + [pltpu.VMEM((LANES, LANES), jnp.float32), pltpu.SemaphoreType.DMA((2, steps))],
        compiler_params=SMALL,
        name="finish",
    )(*operands)


def halving_order(total):
    bits = total.bit_length() - 1
    return [int(format(o, "b").zfill(bits)[::-1], 2) if bits else 0 for o in range(total)]


def reduce_blocks(partial, axis):
    step = 1
    while True:
        half = partial.shape[0] // 2
        came = swap(partial[half:], axis, step)
        if half == 1:
            return partial[0] + came[0]
        partial = partial[:half] + came
        step *= 2


def gather_blocks(x, axis):
    x = x[None]
    step = 1
    while step < lax.axis_size(axis):
        came = swap(x, axis, step)
        upper = (lax.axis_index(axis) & step) > 0
        x = jnp.concatenate([jnp.where(upper, came, x), jnp.where(upper, x, came)])
        step *= 2
    return x


def local(
    tokens,
    task_counts,
    task_embeddings,
    embedding_weight,
    down_factor_head,
    query_up_head,
    value_up_head,
    w_query,
    w_value,
):
    groups, ring, parts = lax.axis_size("groups"), lax.axis_size("task"), lax.axis_size("tensor")
    places = groups * ring
    tok_rows, shard_width = tokens.shape
    block_rows = tok_rows // parts
    own_tasks = task_counts.shape[0]
    block_tasks = own_tasks // parts
    rank = query_up_head.shape[1]
    hidden_rows = down_factor_head.shape[0]
    tensor = lax.axis_index("tensor")
    ring_shifts = list(range(ring))
    far_first = sorted(ring_shifts[1:], reverse=True)
    shifts = list(range(places))

    heads = {
        "value": Head(value_up_head, 1),
        "query": Head(query_up_head, 1),
        "down": Head(down_factor_head, 2),
    }

    def fetch(name, chunk, cuts):
        got = {}
        for cut_shifts in cuts:
            for s, piece in zip(cut_shifts, heads[name].cut(chunk, cut_shifts)):
                got[s] = swap(piece, "task", s) if s else piece
        return jnp.concatenate([got[s] for s in ring_shifts], axis=0)

    fetched = {}
    fetched["query", 0] = fetch("query", 0, [far_first[: ring // 2], far_first[ring // 2 :] + [0]])

    share = own_tasks // parts
    embeddings = lax.dynamic_index_in_dim(
        task_embeddings.reshape(parts, share, -1), tensor, 0, keepdims=False
    )
    hidden = jax.nn.silu(
        jnp.dot(embeddings, embedding_weight, preferred_element_type=jnp.float32)
    ).astype(jnp.bfloat16)
    ring_hidden = jnp.stack([hidden] + [swap(hidden, "task", s) for s in ring_shifts[1:]])
    group_hidden = jnp.concatenate(
        [ring_hidden] + [swap(ring_hidden, "groups", s) for s in range(1, groups)]
    )
    every_hidden = gather_blocks(group_hidden.reshape(places * share, -1), "tensor")
    every_hidden = every_hidden.reshape(parts, places, share, ring, hidden_rows)
    every_hidden = every_hidden.transpose(3, 1, 0, 2, 4)
    every_hidden = every_hidden.reshape(ring, places * own_tasks, hidden_rows)
    every_hidden = jnp.concatenate(
        [
            lax.dynamic_index_in_dim(every_hidden, lax.axis_index("task") ^ s, 0, keepdims=False)
            for s in ring_shifts
        ],
        axis=1,
    )

    chunks = heads["down"].chunks
    for chunk in range(chunks):
        fetched["down", chunk] = fetch("down", chunk, [far_first + [0]])
    fetched["value", 0] = fetch("value", 0, [far_first + [0]])

    def emit(name, chunk):
        matrix = fetched[name, chunk]
        flat = jnp.dot(
            every_hidden, matrix.reshape(matrix.shape[0], -1), preferred_element_type=jnp.float32
        ).astype(jnp.bfloat16)
        return flat.reshape((places, own_tasks) + matrix.shape[1:])

    def send(made, sent):
        return {s: swap(made[s], PLACES, s) if s else made[s] for s in sent}

    crossing = [s for s in reversed(shifts) if s % ring >= ring // 2]
    early = [s for s in crossing if s >= ring] + [s for s in reversed(shifts) if s % ring == 0]
    late = [s for s in crossing if s < ring]
    late = late + [s for s in reversed(shifts) if 0 < s % ring < ring // 2]
    emitted = {}
    for name, chunk in [("query", 0), ("value", 0)] + [("down", c) for c in range(chunks)]:
        made = emit(name, chunk)
        emitted[name, chunk] = send(made, early)
        emitted[name, chunk].update(send(made, late))

    def ordered(pieces):
        return [pieces[s] for s in shifts]

    token_blocks = tokens.reshape(parts, block_rows, shard_width)
    order = halving_order(parts)
    turned = jnp.concatenate(
        [lax.dynamic_index_in_dim(token_blocks, tensor ^ s, 0, keepdims=False) for s in order]
    )
    base_query = jnp.dot(turned, w_query, preferred_element_type=jnp.float32)
    base_value = jnp.dot(turned, w_value, preferred_element_type=jnp.float32)
    base_query = reduce_blocks(base_query.reshape(parts, block_rows, -1), "tensor")
    base_value = reduce_blocks(base_value.reshape(parts, block_rows, -1), "tensor")

    def own_block(factors, above, below):
        moved = lax.all_to_all(factors, "tensor", split_axis=0, concat_axis=0, tiled=True)
        moved = moved.reshape(parts, block_tasks, rank, -1).transpose(1, 2, 0, 3)
        moved = moved.reshape(block_tasks, rank, -1)
        moved = jnp.pad(moved, ((0, 0), (above, below), (0, 0)))
        return moved.reshape(block_tasks * 2 * rank, -1)

    query_up_factors = heads["query"].join(ordered(emitted["query", 0]), shifts)
    own_query = own_block(query_up_factors, 0, rank)
    value_up_factors = heads["value"].join(ordered(emitted["value", 0]), shifts)
    own_value = own_block(value_up_factors, rank, 0)

    tallies = task_counts.reshape(parts, block_tasks)
    ends = jnp.cumsum(tallies, axis=1)
    begins = ends - tallies
    bounds = jnp.repeat(jnp.stack([begins, ends], axis=1), 2 * rank, axis=2)

    down_factors, low_rank = None, []
    head = heads["down"]
    if head.by_lane:
        for chunk in range(chunks):
            pieces, start = emitted["down", chunk], chunk * head.width
            for half in [early, late] if chunk + 1 == chunks else [early + late]:
                some = [pieces[s] for s in half]
                low_rank = project(
                    some, half, head.stride, start, head.width, tokens, bounds, low_rank,
                    half is late,
                )
                down_factors = head.join(some, half, chunk, down_factors)
    else:
        down_factors = head.join(ordered(emitted["down", 0]), shifts)
        projected = jnp.einsum(
            "bpd,bmd->bpm",
            token_blocks,
            down_factors.reshape(parts, block_tasks * 2 * rank, shard_width),
            preferred_element_type=jnp.float32,
        )
        projected = jnp.where(jax.vmap(lambda b: inside(b, block_rows))(bounds), projected, 0.0)
        projected = projected.reshape(parts, block_rows, block_tasks, 2 * rank).sum(axis=2)
        projected = projected.transpose(0, 2, 1)
        low_rank = [
            lax.dynamic_index_in_dim(projected, tensor ^ s, 0, keepdims=False)
            for s in range(parts)
        ]
    shares = [low_rank[0]] + [swap(low_rank[s], "tensor", s) for s in range(1, parts)]
    query, value = finish(shares, bounds, [base_query, base_value, own_query, own_value], steps=4)
    return query, value, down_factors, query_up_factors, value_up_factors


def solution(mesh):
    return jax.shard_map(
        local,
        mesh=mesh,
        in_specs=(
            P(("groups", "task"), "tensor"),
            P(("groups", "task")),
            P(("groups", "task"), None),
            P(),
            P("task", None, "tensor"),
            P("task", None, "tensor"),
            P("task", None, "tensor"),
            P("tensor", None),
            P("tensor", None),
        ),
        out_specs=(
            P(("groups", "task", "tensor"), None),
            P(("groups", "task", "tensor"), None),
            P(("groups", "task"), None, "tensor"),
            P(("groups", "task"), None, "tensor"),
            P(("groups", "task"), None, "tensor"),
        ),
        check_vma=False,
    )
```

```python
import functools

import jax
import jax.numpy as jnp
from jax import lax
from jax.experimental import pallas as pl
from jax.experimental.pallas import tpu as pltpu
from jax.sharding import PartitionSpec as P


ADAPTER_SCALE = 2.0
LANES = 128
PLACES = ("groups", "task")
SMALL = pltpu.CompilerParams(vmem_limit_bytes=16 * 1024 * 1024)


def swap(x, axes, shift):
    total = lax.axis_size(axes)
    return lax.ppermute(x, axes, [(a, a ^ shift) for a in range(total)])


def place():
    return lax.axis_index("groups") * lax.axis_size("task") + lax.axis_index("task")


def through_vmem(moves, scratch, arrived, left):
    fetches = [
        pltpu.make_async_copy(source, scratch.at[k], arrived.at[k])
        for k, (source, _) in enumerate(moves)
    ]
    stores = [
        pltpu.make_async_copy(scratch.at[k], target, left.at[k])
        for k, (_, target) in enumerate(moves)
    ]
    for fetch in fetches:
        fetch.start()
    for fetch, store in zip(fetches, stores):
        fetch.wait()
        store.start()
    for store in stores:
        store.wait()


def vmem_scratch(count, shape, dtype):
    return [
        pltpu.VMEM((count,) + shape, dtype),
        pltpu.SemaphoreType.DMA((count,)),
        pltpu.SemaphoreType.DMA((count,)),
    ]


def cut_kernel(shifts, stride, start, width, source, *rest):
    moves = []
    for k, shift in enumerate(shifts):
        column = pl.multiple_of((place() ^ shift) * stride + start, LANES)
        moves.append((source.at[:, :, pl.ds(column, width)], rest[k]))
    through_vmem(moves, *rest[len(shifts) :])


def cut(head, shifts, stride, start, width):
    shape = head.shape[:2] + (width,)
    return pl.pallas_call(
        functools.partial(cut_kernel, shifts, stride, start, width),
        in_specs=[pl.BlockSpec(memory_space=pl.ANY)],
        out_specs=[pl.BlockSpec(memory_space=pl.ANY)] * len(shifts),
        out_shape=[jax.ShapeDtypeStruct(shape, head.dtype)] * len(shifts),
        scratch_shapes=vmem_scratch(len(shifts), shape, head.dtype),
        compiler_params=SMALL,
        name="cut",
    )(pltpu.with_memory_space_constraint(head, pltpu.HBM))


def cut_row_kernel(shifts, rank, source, *pieces):
    rows = source.shape[0] // rank
    at = lax.broadcasted_iota(jnp.int32, (rows, source.shape[0]), 1)
    at = at - rank * lax.broadcasted_iota(jnp.int32, (rows, source.shape[0]), 0)
    for shift, piece in zip(shifts, pieces):
        pick = jnp.where(at == (place() ^ shift), 1.0, 0.0).astype(source.dtype)
        picked = jnp.dot(pick, source[...], preferred_element_type=jnp.float32)
        piece[...] = picked.astype(piece.dtype)


def cut_row(head, shifts):
    rows, rank, columns = head.shape
    return pl.pallas_call(
        functools.partial(cut_row_kernel, shifts, rank),
        out_shape=[jax.ShapeDtypeStruct((rows, columns), head.dtype)] * len(shifts),
        compiler_params=SMALL,
        name="cut_row",
    )(head.reshape(rows * rank, columns))


def join_kernel(shifts, stride, start, width, *refs):
    whole = refs[-4]
    moves = []
    for k, shift in enumerate(shifts):
        column = pl.multiple_of((place() ^ shift) * stride + start, LANES)
        moves.append((refs[k], whole.at[:, :, pl.ds(column, width)]))
    through_vmem(moves, *refs[-3:])


def join(pieces, shifts, stride, start, width, columns, whole):
    operands = list(pieces) + ([] if whole is None else [whole])
    return pl.pallas_call(
        functools.partial(join_kernel, shifts, stride, start, width),
        in_specs=[pl.BlockSpec(memory_space=pl.ANY)] * len(operands),
        out_specs=pl.BlockSpec(memory_space=pl.ANY),
        out_shape=jax.ShapeDtypeStruct(pieces[0].shape[:2] + (columns,), pieces[0].dtype),
        scratch_shapes=vmem_scratch(len(pieces), pieces[0].shape, pieces[0].dtype),
        input_output_aliases={} if whole is None else {len(pieces): 0},
        compiler_params=SMALL,
        name="join",
    )(*operands)


def stack_kernel(shifts, *refs):
    count = len(shifts)
    moves = [(refs[k], refs[count].at[place() ^ s]) for k, s in enumerate(shifts)]
    through_vmem(moves, *refs[count + 1 :])


def stack(pieces, shifts):
    shape, dtype = pieces[0].shape, pieces[0].dtype
    return pl.pallas_call(
        functools.partial(stack_kernel, shifts),
        in_specs=[pl.BlockSpec(memory_space=pl.ANY)] * len(pieces),
        out_specs=pl.BlockSpec(memory_space=pl.ANY),
        out_shape=jax.ShapeDtypeStruct((len(pieces),) + shape, dtype),
        scratch_shapes=vmem_scratch(len(pieces), shape, dtype),
        compiler_params=SMALL,
        name="stack",
    )(*pieces)


def in_order(pieces, shifts):
    stack = jnp.zeros((len(pieces),) + pieces[0].shape, pieces[0].dtype)
    for piece, shift in zip(pieces, shifts):
        stack = lax.dynamic_update_index_in_dim(stack, piece, place() ^ shift, 0)
    return stack


class Head:
    def __init__(self, head, chunks):
        self.rank, self.columns = head.shape[1:]
        self.head = head
        self.places = lax.axis_size("groups") * lax.axis_size("task")
        self.stride = self.columns // self.places
        self.by_lane = self.stride % (LANES * chunks) == 0
        self.by_row = not self.by_lane and self.rank == self.places
        self.chunks = chunks if self.by_lane else 1
        self.width = self.stride // self.chunks

    def cut(self, chunk, shifts):
        if self.by_lane:
            return cut(self.head, shifts, self.stride, chunk * self.width, self.width)
        if self.by_row:
            return cut_row(self.head, shifts)
        shares = self.head.reshape(-1, self.rank, self.places, self.stride).transpose(2, 0, 1, 3)
        return [lax.dynamic_index_in_dim(shares, place() ^ s, 0, keepdims=False) for s in shifts]

    def join(self, pieces, shifts, chunk=0, whole=None):
        if self.by_lane:
            start = chunk * self.width
            return join(pieces, shifts, self.stride, start, self.width, self.columns, whole)
        if self.by_row:
            whole = stack(pieces, shifts).transpose(1, 0, 2)
        else:
            whole = in_order(pieces, shifts).transpose(1, 2, 0, 3)
        return whole.reshape(whole.shape[0], self.rank, self.columns)


def rank_columns(shape, rank_axis, column_axis, rank):
    of_column = lax.broadcasted_iota(jnp.int32, shape, column_axis) % rank
    return of_column == lax.broadcasted_iota(jnp.int32, shape, rank_axis)


def inside(bounds, rows):
    row = lax.broadcasted_iota(jnp.int32, (rows, bounds.shape[1]), 0)
    return (row >= bounds[0:1]) & (row < bounds[1:2])


def turned(x, square):
    square[...] = jnp.zeros(square.shape, square.dtype)
    square[0 : x.shape[0], 0 : x.shape[1]] = x
    return square[...].T


def terms(x, count):
    parts = []
    for _ in range(count):
        parts.append(x.astype(jnp.bfloat16))
        x = x - parts[-1].astype(jnp.float32)
    return jnp.concatenate(parts)


def project_kernel(shifts, parts, stride, start, width, tokens, bounds, *refs):
    pieces, refs = refs[: len(shifts)], refs[len(shifts) :]
    before, after = refs[:-parts], refs[-parts:]
    rows = tokens.shape[0] // parts
    tasks, rank = pieces[0].shape[0] // parts, pieces[0].shape[1]
    every = []
    for turn in range(parts):
        block = lax.axis_index("tensor") ^ turn
        found = jnp.zeros((rows, tasks * rank), jnp.float32)
        for k, shift in enumerate(shifts):
            column = pl.multiple_of((place() ^ shift) * stride + start, LANES)
            found += lax.dot_general(
                tokens[pl.ds(pl.multiple_of(block * rows, 8), rows), pl.ds(column, width)],
                pieces[k][pl.ds(block * tasks, tasks)].reshape(-1, width),
                (((1,), (1,)), ((), ())),
                preferred_element_type=jnp.float32,
            )
        every.append(jnp.where(inside(bounds[block], rows), found, 0.0))
    pick = rank_columns((tasks * rank, LANES), 1, 0, rank).astype(jnp.bfloat16)
    count = 3
    summed = jnp.dot(
        terms(jnp.concatenate(every), count), pick, preferred_element_type=jnp.float32
    ).reshape(count, parts * rows, LANES)
    low_rank = sum(summed[k] for k in range(count)).T
    for turn in range(parts):
        share = low_rank[0:rank, turn * rows : (turn + 1) * rows]
        after[turn][...] = share + before[turn][...] if before else share


def in_vmem(x):
    return pltpu.with_memory_space_constraint(x, pltpu.VMEM)


def project(pieces, shifts, stride, start, width, tokens, bounds, before, near):
    parts, rank = bounds.shape[0], pieces[0].shape[1]
    rows = tokens.shape[0] // parts
    if near:
        tokens, bounds = in_vmem(tokens), in_vmem(bounds)
        before = [in_vmem(x) for x in before]
    return pl.pallas_call(
        functools.partial(project_kernel, shifts, parts, stride, start, width),
        in_specs=[pl.BlockSpec(memory_space=pltpu.VMEM)] * (2 + len(pieces) + len(before)),
        out_shape=[jax.ShapeDtypeStruct((rank, rows), jnp.float32)] * parts,
        compiler_params=SMALL,
        name="project",
    )(tokens, bounds, *pieces, *before)


def finish_kernel(count, steps, bounds, *refs):
    shares, rest = refs[:count], refs[count:]
    bases, ups, outs, makes, square, sems = rest[0:2], rest[2:4], rest[4:6], rest[6:8], *rest[8:]
    rank, rows = shares[0].shape
    low_rank = shares[0][...]
    for share in shares[1:]:
        low_rank = low_rank + share[...]
    low_rank = turned(low_rank, square)[0:rows]
    own = bounds[lax.axis_index("tensor")]
    pick = rank_columns((LANES, own.shape[1]), 0, 1, rank).astype(jnp.bfloat16)
    spread = jnp.dot(terms(low_rank, 2), pick, preferred_element_type=jnp.float32)
    own = inside(own, rows)
    spread = jnp.where(jnp.concatenate([own, own]), spread, 0.0).astype(jnp.bfloat16)
    copies = []
    for step in range(steps):
        for k, (base, up, out, made) in enumerate(zip(bases, ups, outs, makes)):
            width = base.shape[1] // steps
            columns = pl.ds(step * width, width)
            update = jnp.dot(spread, up[:, columns], preferred_element_type=jnp.float32)
            update = update[0:rows] + update[rows:]
            made[:, columns] = (base[:, columns] + ADAPTER_SCALE * update).astype(made.dtype)
            copies.append(
                pltpu.make_async_copy(made.at[:, columns], out.at[:, columns], sems.at[k, step])
            )
            copies[-1].start()
    for copy in copies:
        copy.wait()


def finish(shares, bounds, operands, steps):
    operands = [in_vmem(x) for x in (bounds, *shares, *operands)]
    shapes = [x.shape for x in operands[-4:-2]]
    return pl.pallas_call(
        functools.partial(finish_kernel, len(shares), steps),
        in_specs=[pl.BlockSpec(memory_space=pltpu.VMEM)] * len(operands),
        out_specs=[pl.BlockSpec(memory_space=pl.ANY)] * 2,
        out_shape=[jax.ShapeDtypeStruct(shape, jnp.bfloat16) for shape in shapes],
        scratch_shapes=[pltpu.VMEM(shape, jnp.bfloat16) for shape in shapes]
        + [pltpu.VMEM((LANES, LANES), jnp.float32), pltpu.SemaphoreType.DMA((2, steps))],
        compiler_params=SMALL,
        name="finish",
    )(*operands)


def halving_order(total):
    bits = total.bit_length() - 1
    return [int(format(o, "b").zfill(bits)[::-1], 2) if bits else 0 for o in range(total)]


def reduce_blocks(partial, axis):
    step = 1
    while True:
        half = partial.shape[0] // 2
        came = swap(partial[half:], axis, step)
        if half == 1:
            return partial[0] + came[0]
        partial = partial[:half] + came
        step *= 2


def gather_blocks(x, axis):
    x = x[None]
    step = 1
    while step < lax.axis_size(axis):
        came = swap(x, axis, step)
        upper = (lax.axis_index(axis) & step) > 0
        x = jnp.concatenate([jnp.where(upper, came, x), jnp.where(upper, x, came)])
        step *= 2
    return x


def local(
    tokens,
    task_counts,
    task_embeddings,
    embedding_weight,
    down_factor_head,
    query_up_head,
    value_up_head,
    w_query,
    w_value,
):
    groups, ring, parts = lax.axis_size("groups"), lax.axis_size("task"), lax.axis_size("tensor")
    places = groups * ring
    tok_rows, shard_width = tokens.shape
    block_rows = tok_rows // parts
    own_tasks = task_counts.shape[0]
    block_tasks = own_tasks // parts
    rank = query_up_head.shape[1]
    hidden_rows = down_factor_head.shape[0]
    tensor = lax.axis_index("tensor")
    ring_shifts = list(range(ring))
    far_first = sorted(ring_shifts[1:], reverse=True)
    shifts = list(range(places))

    heads = {
        "value": Head(value_up_head, 1),
        "query": Head(query_up_head, 1),
        "down": Head(down_factor_head, 2),
    }

    def fetch(name, chunk):
        pieces = heads[name].cut(chunk, far_first + [0])
        got = {s: swap(p, "task", s) if s else p for s, p in zip(far_first + [0], pieces)}
        return jnp.concatenate([got[s] for s in ring_shifts], axis=0)

    fetched = {}
    fetched["query", 0] = fetch("query", 0)

    share = own_tasks // parts
    embeddings = lax.dynamic_index_in_dim(
        task_embeddings.reshape(parts, share, -1), tensor, 0, keepdims=False
    )
    hidden = jax.nn.silu(
        jnp.dot(embeddings, embedding_weight, preferred_element_type=jnp.float32)
    ).astype(jnp.bfloat16)
    ring_hidden = jnp.stack([hidden] + [swap(hidden, "task", s) for s in ring_shifts[1:]])
    group_hidden = jnp.concatenate(
        [ring_hidden] + [swap(ring_hidden, "groups", s) for s in range(1, groups)]
    )
    every_hidden = gather_blocks(group_hidden.reshape(places * share, -1), "tensor")
    every_hidden = every_hidden.reshape(parts, places, share, ring, hidden_rows)
    every_hidden = every_hidden.transpose(3, 1, 0, 2, 4)
    every_hidden = every_hidden.reshape(ring, places * own_tasks, hidden_rows)
    every_hidden = jnp.concatenate(
        [
            lax.dynamic_index_in_dim(every_hidden, lax.axis_index("task") ^ s, 0, keepdims=False)
            for s in ring_shifts
        ],
        axis=1,
    )

    chunks = heads["down"].chunks
    for chunk in range(chunks):
        fetched["down", chunk] = fetch("down", chunk)
    fetched["value", 0] = fetch("value", 0)

    def emit(name, chunk):
        matrix = fetched[name, chunk]
        flat = jnp.dot(
            every_hidden, matrix.reshape(matrix.shape[0], -1), preferred_element_type=jnp.float32
        ).astype(jnp.bfloat16)
        return flat.reshape((places, own_tasks) + matrix.shape[1:])

    def send(made, sent):
        return {s: swap(made[s], PLACES, s) if s else made[s] for s in sent}

    crossing = [s for s in reversed(shifts) if s % ring >= ring // 2]
    early = [s for s in crossing if s >= ring] + [s for s in reversed(shifts) if s % ring == 0]
    late = [s for s in crossing if s < ring]
    late = late + [s for s in reversed(shifts) if 0 < s % ring < ring // 2]
    emitted = {}
    for name, chunk in [("query", 0), ("value", 0)] + [("down", c) for c in range(chunks)]:
        made = emit(name, chunk)
        emitted[name, chunk] = send(made, early)
        emitted[name, chunk].update(send(made, late))

    def ordered(pieces):
        return [pieces[s] for s in shifts]

    token_blocks = tokens.reshape(parts, block_rows, shard_width)
    order = halving_order(parts)
    turned = jnp.concatenate(
        [lax.dynamic_index_in_dim(token_blocks, tensor ^ s, 0, keepdims=False) for s in order]
    )
    base_query = jnp.dot(turned, w_query, preferred_element_type=jnp.float32)
    base_value = jnp.dot(turned, w_value, preferred_element_type=jnp.float32)
    base_query = reduce_blocks(base_query.reshape(parts, block_rows, -1), "tensor")
    base_value = reduce_blocks(base_value.reshape(parts, block_rows, -1), "tensor")

    def own_block(factors, above, below):
        moved = lax.all_to_all(factors, "tensor", split_axis=0, concat_axis=0, tiled=True)
        moved = moved.reshape(parts, block_tasks, rank, -1).transpose(1, 2, 0, 3)
        moved = moved.reshape(block_tasks, rank, -1)
        moved = jnp.pad(moved, ((0, 0), (above, below), (0, 0)))
        return moved.reshape(block_tasks * 2 * rank, -1)

    query_up_factors = heads["query"].join(ordered(emitted["query", 0]), shifts)
    own_query = own_block(query_up_factors, 0, rank)
    value_up_factors = heads["value"].join(ordered(emitted["value", 0]), shifts)
    own_value = own_block(value_up_factors, rank, 0)

    tallies = task_counts.reshape(parts, block_tasks)
    ends = jnp.cumsum(tallies, axis=1)
    begins = ends - tallies
    bounds = jnp.repeat(jnp.stack([begins, ends], axis=1), 2 * rank, axis=2)

    down_factors, low_rank = None, []
    head = heads["down"]
    if head.by_lane:
        for chunk in range(chunks):
            pieces, start = emitted["down", chunk], chunk * head.width
            for half in [early, late] if chunk + 1 == chunks else [early + late]:
                some = [pieces[s] for s in half]
                low_rank = project(
                    some, half, head.stride, start, head.width, tokens, bounds, low_rank,
                    half is late,
                )
                down_factors = head.join(some, half, chunk, down_factors)
    else:
        down_factors = head.join(ordered(emitted["down", 0]), shifts)
        projected = jnp.einsum(
            "bpd,bmd->bpm",
            token_blocks,
            down_factors.reshape(parts, block_tasks * 2 * rank, shard_width),
            preferred_element_type=jnp.float32,
        )
        projected = jnp.where(jax.vmap(lambda b: inside(b, block_rows))(bounds), projected, 0.0)
        projected = projected.reshape(parts, block_rows, block_tasks, 2 * rank).sum(axis=2)
        projected = projected.transpose(0, 2, 1)
        low_rank = [
            lax.dynamic_index_in_dim(projected, tensor ^ s, 0, keepdims=False)
            for s in range(parts)
        ]
    shares = [low_rank[0]] + [swap(low_rank[s], "tensor", s) for s in range(1, parts)]
    query, value = finish(shares, bounds, [base_query, base_value, own_query, own_value], steps=4)
    return query, value, down_factors, query_up_factors, value_up_factors


def solution(mesh):
    return jax.shard_map(
        local,
        mesh=mesh,
        in_specs=(
            P(("groups", "task"), "tensor"),
            P(("groups", "task")),
            P(("groups", "task"), None),
            P(),
            P("task", None, "tensor"),
            P("task", None, "tensor"),
            P("task", None, "tensor"),
            P("tensor", None),
            P("tensor", None),
        ),
        out_specs=(
            P(("groups", "task", "tensor"), None),
            P(("groups", "task", "tensor"), None),
            P(("groups", "task"), None, "tensor"),
            P(("groups", "task"), None, "tensor"),
            P(("groups", "task"), None, "tensor"),
        ),
        check_vma=False,
    )
```

```python
import functools

import jax
import jax.numpy as jnp
from jax import lax
from jax.experimental import pallas as pl
from jax.experimental.pallas import tpu as pltpu
from jax.sharding import PartitionSpec as P


ADAPTER_SCALE = 2.0
LANES = 128
PLACES = ("groups", "task")
SMALL = pltpu.CompilerParams(vmem_limit_bytes=16 * 1024 * 1024)


def swap(x, axes, shift):
    total = lax.axis_size(axes)
    return lax.ppermute(x, axes, [(a, a ^ shift) for a in range(total)])


def place():
    return lax.axis_index("groups") * lax.axis_size("task") + lax.axis_index("task")


def through_vmem(moves, scratch, arrived, left):
    fetches = [
        pltpu.make_async_copy(source, scratch.at[k], arrived.at[k])
        for k, (source, _) in enumerate(moves)
    ]
    stores = [
        pltpu.make_async_copy(scratch.at[k], target, left.at[k])
        for k, (_, target) in enumerate(moves)
    ]
    for fetch in fetches:
        fetch.start()
    for fetch, store in zip(fetches, stores):
        fetch.wait()
        store.start()
    for store in stores:
        store.wait()


def vmem_scratch(count, shape, dtype):
    return [
        pltpu.VMEM((count,) + shape, dtype),
        pltpu.SemaphoreType.DMA((count,)),
        pltpu.SemaphoreType.DMA((count,)),
    ]


def cut_kernel(shifts, stride, start, width, source, *rest):
    moves = []
    for k, shift in enumerate(shifts):
        column = pl.multiple_of((place() ^ shift) * stride + start, LANES)
        moves.append((source.at[:, :, pl.ds(column, width)], rest[k]))
    through_vmem(moves, *rest[len(shifts) :])


def cut(head, shifts, stride, start, width):
    shape = head.shape[:2] + (width,)
    return pl.pallas_call(
        functools.partial(cut_kernel, shifts, stride, start, width),
        in_specs=[pl.BlockSpec(memory_space=pl.ANY)],
        out_specs=[pl.BlockSpec(memory_space=pltpu.HBM)] * len(shifts),
        out_shape=[jax.ShapeDtypeStruct(shape, head.dtype)] * len(shifts),
        scratch_shapes=vmem_scratch(len(shifts), shape, head.dtype),
        compiler_params=SMALL,
        name="cut",
    )(pltpu.with_memory_space_constraint(head, pltpu.HBM))


def cut_row_kernel(shifts, rank, source, *pieces):
    rows = source.shape[0] // rank
    at = lax.broadcasted_iota(jnp.int32, (rows, source.shape[0]), 1)
    at = at - rank * lax.broadcasted_iota(jnp.int32, (rows, source.shape[0]), 0)
    for shift, piece in zip(shifts, pieces):
        pick = jnp.where(at == (place() ^ shift), 1.0, 0.0).astype(source.dtype)
        picked = jnp.dot(pick, source[...], preferred_element_type=jnp.float32)
        piece[...] = picked.astype(piece.dtype)


def cut_row(head, shifts):
    rows, rank, columns = head.shape
    return pl.pallas_call(
        functools.partial(cut_row_kernel, shifts, rank),
        out_shape=[jax.ShapeDtypeStruct((rows, columns), head.dtype)] * len(shifts),
        compiler_params=SMALL,
        name="cut_row",
    )(head.reshape(rows * rank, columns))


def join_kernel(shifts, stride, start, width, *refs):
    whole = refs[-4]
    moves = []
    for k, shift in enumerate(shifts):
        column = pl.multiple_of((place() ^ shift) * stride + start, LANES)
        moves.append((refs[k], whole.at[:, :, pl.ds(column, width)]))
    through_vmem(moves, *refs[-3:])


def join(pieces, shifts, stride, start, width, columns, whole):
    operands = list(pieces) + ([] if whole is None else [whole])
    return pl.pallas_call(
        functools.partial(join_kernel, shifts, stride, start, width),
        in_specs=[pl.BlockSpec(memory_space=pl.ANY)] * len(operands),
        out_specs=pl.BlockSpec(memory_space=pl.ANY),
        out_shape=jax.ShapeDtypeStruct(pieces[0].shape[:2] + (columns,), pieces[0].dtype),
        scratch_shapes=vmem_scratch(len(pieces), pieces[0].shape, pieces[0].dtype),
        input_output_aliases={} if whole is None else {len(pieces): 0},
        compiler_params=SMALL,
        name="join",
    )(*operands)


def stack_kernel(shifts, *refs):
    count = len(shifts)
    moves = [(refs[k], refs[count].at[place() ^ s]) for k, s in enumerate(shifts)]
    through_vmem(moves, *refs[count + 1 :])


def stack(pieces, shifts):
    shape, dtype = pieces[0].shape, pieces[0].dtype
    return pl.pallas_call(
        functools.partial(stack_kernel, shifts),
        in_specs=[pl.BlockSpec(memory_space=pl.ANY)] * len(pieces),
        out_specs=pl.BlockSpec(memory_space=pl.ANY),
        out_shape=jax.ShapeDtypeStruct((len(pieces),) + shape, dtype),
        scratch_shapes=vmem_scratch(len(pieces), shape, dtype),
        compiler_params=SMALL,
        name="stack",
    )(*pieces)


def in_order(pieces, shifts):
    stack = jnp.zeros((len(pieces),) + pieces[0].shape, pieces[0].dtype)
    for piece, shift in zip(pieces, shifts):
        stack = lax.dynamic_update_index_in_dim(stack, piece, place() ^ shift, 0)
    return stack


class Head:
    def __init__(self, head, chunks):
        self.rank, self.columns = head.shape[1:]
        self.head = head
        self.places = lax.axis_size("groups") * lax.axis_size("task")
        self.stride = self.columns // self.places
        self.by_lane = self.stride % (LANES * chunks) == 0
        self.by_row = not self.by_lane and self.rank == self.places
        self.chunks = chunks if self.by_lane else 1
        self.width = self.stride // self.chunks

    def cut(self, chunk, shifts):
        if self.by_lane:
            return cut(self.head, shifts, self.stride, chunk * self.width, self.width)
        if self.by_row:
            return cut_row(self.head, shifts)
        shares = self.head.reshape(-1, self.rank, self.places, self.stride).transpose(2, 0, 1, 3)
        return [lax.dynamic_index_in_dim(shares, place() ^ s, 0, keepdims=False) for s in shifts]

    def join(self, pieces, shifts, chunk=0, whole=None):
        if self.by_lane:
            start = chunk * self.width
            return join(pieces, shifts, self.stride, start, self.width, self.columns, whole)
        if self.by_row:
            whole = stack(pieces, shifts).transpose(1, 0, 2)
        else:
            whole = in_order(pieces, shifts).transpose(1, 2, 0, 3)
        return whole.reshape(whole.shape[0], self.rank, self.columns)


def rank_columns(shape, rank_axis, column_axis, rank):
    of_column = lax.broadcasted_iota(jnp.int32, shape, column_axis) % rank
    return of_column == lax.broadcasted_iota(jnp.int32, shape, rank_axis)


def inside(bounds, rows):
    row = lax.broadcasted_iota(jnp.int32, (rows, bounds.shape[1]), 0)
    return (row >= bounds[0:1]) & (row < bounds[1:2])


def turned(x, square):
    square[...] = jnp.zeros(square.shape, square.dtype)
    square[0 : x.shape[0], 0 : x.shape[1]] = x
    return square[...].T


def terms(x, count):
    parts = []
    for _ in range(count):
        parts.append(x.astype(jnp.bfloat16))
        x = x - parts[-1].astype(jnp.float32)
    return jnp.concatenate(parts)


def project_kernel(shifts, parts, stride, start, width, tokens, bounds, *refs):
    pieces, refs = refs[: len(shifts)], refs[len(shifts) :]
    before, after = refs[:-parts], refs[-parts:]
    rows = tokens.shape[0] // parts
    tasks, rank = pieces[0].shape[0] // parts, pieces[0].shape[1]
    every = []
    for turn in range(parts):
        block = lax.axis_index("tensor") ^ turn
        found = jnp.zeros((rows, tasks * rank), jnp.float32)
        for k, shift in enumerate(shifts):
            column = pl.multiple_of((place() ^ shift) * stride + start, LANES)
            found += lax.dot_general(
                tokens[pl.ds(pl.multiple_of(block * rows, 8), rows), pl.ds(column, width)],
                pieces[k][pl.ds(block * tasks, tasks)].reshape(-1, width),
                (((1,), (1,)), ((), ())),
                preferred_element_type=jnp.float32,
            )
        every.append(jnp.where(inside(bounds[block], rows), found, 0.0))
    pick = rank_columns((tasks * rank, LANES), 1, 0, rank).astype(jnp.bfloat16)
    count = 3
    summed = jnp.dot(
        terms(jnp.concatenate(every), count), pick, preferred_element_type=jnp.float32
    ).reshape(count, parts * rows, LANES)
    low_rank = sum(summed[k] for k in range(count)).T
    for turn in range(parts):
        share = low_rank[0:rank, turn * rows : (turn + 1) * rows]
        after[turn][...] = share + before[turn][...] if before else share


def in_vmem(x):
    return pltpu.with_memory_space_constraint(x, pltpu.VMEM)


def project(pieces, shifts, stride, start, width, tokens, bounds, before, near):
    parts, rank = bounds.shape[0], pieces[0].shape[1]
    rows = tokens.shape[0] // parts
    if near:
        tokens, bounds = in_vmem(tokens), in_vmem(bounds)
        before = [in_vmem(x) for x in before]
    return pl.pallas_call(
        functools.partial(project_kernel, shifts, parts, stride, start, width),
        in_specs=[pl.BlockSpec(memory_space=pltpu.VMEM)] * (2 + len(pieces) + len(before)),
        out_shape=[jax.ShapeDtypeStruct((rank, rows), jnp.float32)] * parts,
        compiler_params=SMALL,
        name="project",
    )(tokens, bounds, *pieces, *before)


def finish_kernel(count, steps, bounds, *refs):
    shares, rest = refs[:count], refs[count:]
    bases, ups, outs, makes, square, sems = rest[0:2], rest[2:4], rest[4:6], rest[6:8], *rest[8:]
    rank, rows = shares[0].shape
    low_rank = shares[0][...]
    for share in shares[1:]:
        low_rank = low_rank + share[...]
    low_rank = turned(low_rank, square)[0:rows]
    own = bounds[lax.axis_index("tensor")]
    pick = rank_columns((LANES, own.shape[1]), 0, 1, rank).astype(jnp.bfloat16)
    spread = jnp.dot(terms(low_rank, 2), pick, preferred_element_type=jnp.float32)
    own = inside(own, rows)
    spread = jnp.where(jnp.concatenate([own, own]), spread, 0.0).astype(jnp.bfloat16)
    copies = []
    for step in range(steps):
        for k, (base, up, out, made) in enumerate(zip(bases, ups, outs, makes)):
            width = base.shape[1] // steps
            columns = pl.ds(step * width, width)
            update = jnp.dot(spread, up[:, columns], preferred_element_type=jnp.float32)
            update = update[0:rows] + update[rows:]
            made[:, columns] = (base[:, columns] + ADAPTER_SCALE * update).astype(made.dtype)
            copies.append(
                pltpu.make_async_copy(made.at[:, columns], out.at[:, columns], sems.at[k, step])
            )
            copies[-1].start()
    for copy in copies:
        copy.wait()


def finish(shares, bounds, operands, steps):
    operands = [in_vmem(x) for x in (bounds, *shares, *operands)]
    shapes = [x.shape for x in operands[-4:-2]]
    return pl.pallas_call(
        functools.partial(finish_kernel, len(shares), steps),
        in_specs=[pl.BlockSpec(memory_space=pltpu.VMEM)] * len(operands),
        out_specs=[pl.BlockSpec(memory_space=pl.ANY)] * 2,
        out_shape=[jax.ShapeDtypeStruct(shape, jnp.bfloat16) for shape in shapes],
        scratch_shapes=[pltpu.VMEM(shape, jnp.bfloat16) for shape in shapes]
        + [pltpu.VMEM((LANES, LANES), jnp.float32), pltpu.SemaphoreType.DMA((2, steps))],
        compiler_params=SMALL,
        name="finish",
    )(*operands)


def halving_order(total):
    bits = total.bit_length() - 1
    return [int(format(o, "b").zfill(bits)[::-1], 2) if bits else 0 for o in range(total)]


def reduce_blocks(partial, axis):
    step = 1
    while True:
        half = partial.shape[0] // 2
        came = swap(partial[half:], axis, step)
        if half == 1:
            return partial[0] + came[0]
        partial = partial[:half] + came
        step *= 2


def gather_blocks(x, axis):
    x = x[None]
    step = 1
    while step < lax.axis_size(axis):
        came = swap(x, axis, step)
        upper = (lax.axis_index(axis) & step) > 0
        x = jnp.concatenate([jnp.where(upper, came, x), jnp.where(upper, x, came)])
        step *= 2
    return x


def local(
    tokens,
    task_counts,
    task_embeddings,
    embedding_weight,
    down_factor_head,
    query_up_head,
    value_up_head,
    w_query,
    w_value,
):
    groups, ring, parts = lax.axis_size("groups"), lax.axis_size("task"), lax.axis_size("tensor")
    places = groups * ring
    tok_rows, shard_width = tokens.shape
    block_rows = tok_rows // parts
    own_tasks = task_counts.shape[0]
    block_tasks = own_tasks // parts
    rank = query_up_head.shape[1]
    hidden_rows = down_factor_head.shape[0]
    tensor = lax.axis_index("tensor")
    ring_shifts = list(range(ring))
    far_first = sorted(ring_shifts[1:], reverse=True)
    shifts = list(range(places))

    heads = {
        "value": Head(value_up_head, 1),
        "query": Head(query_up_head, 1),
        "down": Head(down_factor_head, 2),
    }

    def fetch(name, chunk):
        pieces = heads[name].cut(chunk, far_first + [0])
        got = {s: swap(p, "task", s) if s else p for s, p in zip(far_first + [0], pieces)}
        return jnp.concatenate([got[s] for s in ring_shifts], axis=0)

    fetched = {}
    fetched["query", 0] = fetch("query", 0)

    share = own_tasks // parts
    embeddings = lax.dynamic_index_in_dim(
        task_embeddings.reshape(parts, share, -1), tensor, 0, keepdims=False
    )
    hidden = jax.nn.silu(
        jnp.dot(embeddings, embedding_weight, preferred_element_type=jnp.float32)
    ).astype(jnp.bfloat16)
    far, came = ring // 2, [0, ring // 2]
    ring_hidden = jnp.concatenate([hidden[None], swap(hidden[None], "task", far)])
    while far > 1:
        far //= 2
        ring_hidden = jnp.concatenate([ring_hidden, swap(ring_hidden, "task", far)])
        came = came + [s ^ far for s in came]
    ring_hidden = jnp.stack([ring_hidden[came.index(s)] for s in ring_shifts])
    group_hidden = jnp.concatenate(
        [ring_hidden] + [swap(ring_hidden, "groups", s) for s in range(1, groups)]
    )
    every_hidden = gather_blocks(group_hidden.reshape(places * share, -1), "tensor")
    every_hidden = every_hidden.reshape(parts, places, share, ring, hidden_rows)
    every_hidden = every_hidden.transpose(3, 1, 0, 2, 4)
    every_hidden = every_hidden.reshape(ring, places * own_tasks, hidden_rows)
    every_hidden = jnp.concatenate(
        [
            lax.dynamic_index_in_dim(every_hidden, lax.axis_index("task") ^ s, 0, keepdims=False)
            for s in ring_shifts
        ],
        axis=1,
    )

    chunks = heads["down"].chunks
    for chunk in range(chunks):
        fetched["down", chunk] = fetch("down", chunk)
    fetched["value", 0] = fetch("value", 0)

    def emit(name, chunk):
        matrix = fetched[name, chunk]
        flat = jnp.dot(
            every_hidden, matrix.reshape(matrix.shape[0], -1), preferred_element_type=jnp.float32
        ).astype(jnp.bfloat16)
        return flat.reshape((places, own_tasks) + matrix.shape[1:])

    def send(made, sent):
        return {s: swap(made[s], PLACES, s) if s else made[s] for s in sent}

    crossing = [s for s in reversed(shifts) if s % ring >= ring // 2]
    late = crossing[-1:]
    early = crossing[:-1] + [s for s in reversed(shifts) if s % ring < ring // 2]
    emitted = {}
    for name, chunk in [("query", 0), ("value", 0)] + [("down", c) for c in range(chunks)]:
        made = emit(name, chunk)
        emitted[name, chunk] = send(made, early)
        emitted[name, chunk].update(send(made, late))

    def ordered(pieces):
        return [pieces[s] for s in shifts]

    token_blocks = tokens.reshape(parts, block_rows, shard_width)
    order = halving_order(parts)
    turned = jnp.concatenate(
        [lax.dynamic_index_in_dim(token_blocks, tensor ^ s, 0, keepdims=False) for s in order]
    )
    base_query = jnp.dot(turned, w_query, preferred_element_type=jnp.float32)
    base_value = jnp.dot(turned, w_value, preferred_element_type=jnp.float32)
    base_query = reduce_blocks(base_query.reshape(parts, block_rows, -1), "tensor")
    base_value = reduce_blocks(base_value.reshape(parts, block_rows, -1), "tensor")

    def own_block(factors, above, below):
        moved = lax.all_to_all(factors, "tensor", split_axis=0, concat_axis=0, tiled=True)
        moved = moved.reshape(parts, block_tasks, rank, -1).transpose(1, 2, 0, 3)
        moved = moved.reshape(block_tasks, rank, -1)
        moved = jnp.pad(moved, ((0, 0), (above, below), (0, 0)))
        return moved.reshape(block_tasks * 2 * rank, -1)

    query_up_factors = heads["query"].join(ordered(emitted["query", 0]), shifts)
    own_query = own_block(query_up_factors, 0, rank)
    value_up_factors = heads["value"].join(ordered(emitted["value", 0]), shifts)
    own_value = own_block(value_up_factors, rank, 0)

    tallies = task_counts.reshape(parts, block_tasks)
    ends = jnp.cumsum(tallies, axis=1)
    begins = ends - tallies
    bounds = jnp.repeat(jnp.stack([begins, ends], axis=1), 2 * rank, axis=2)

    down_factors, low_rank = None, []
    head = heads["down"]
    if head.by_lane:
        for chunk in range(chunks):
            pieces, start = emitted["down", chunk], chunk * head.width
            for half in [early, late] if chunk + 1 == chunks else [early + late]:
                some = [pieces[s] for s in half]
                low_rank = project(
                    some, half, head.stride, start, head.width, tokens, bounds, low_rank,
                    half is late,
                )
                down_factors = head.join(some, half, chunk, down_factors)
    else:
        down_factors = head.join(ordered(emitted["down", 0]), shifts)
        projected = jnp.einsum(
            "bpd,bmd->bpm",
            token_blocks,
            down_factors.reshape(parts, block_tasks * 2 * rank, shard_width),
            preferred_element_type=jnp.float32,
        )
        projected = jnp.where(jax.vmap(lambda b: inside(b, block_rows))(bounds), projected, 0.0)
        projected = projected.reshape(parts, block_rows, block_tasks, 2 * rank).sum(axis=2)
        projected = projected.transpose(0, 2, 1)
        low_rank = [
            lax.dynamic_index_in_dim(projected, tensor ^ s, 0, keepdims=False)
            for s in range(parts)
        ]
    shares = [low_rank[0]] + [swap(low_rank[s], "tensor", s) for s in range(1, parts)]
    query, value = finish(shares, bounds, [base_query, base_value, own_query, own_value], steps=8)
    return query, value, down_factors, query_up_factors, value_up_factors


def solution(mesh):
    return jax.shard_map(
        local,
        mesh=mesh,
        in_specs=(
            P(("groups", "task"), "tensor"),
            P(("groups", "task")),
            P(("groups", "task"), None),
            P(),
            P("task", None, "tensor"),
            P("task", None, "tensor"),
            P("task", None, "tensor"),
            P("tensor", None),
            P("tensor", None),
        ),
        out_specs=(
            P(("groups", "task", "tensor"), None),
            P(("groups", "task", "tensor"), None),
            P(("groups", "task"), None, "tensor"),
            P(("groups", "task"), None, "tensor"),
            P(("groups", "task"), None, "tensor"),
        ),
        check_vma=False,
    )
```

```python
import functools

import jax
import jax.numpy as jnp
from jax import lax
from jax.experimental import pallas as pl
from jax.experimental.pallas import tpu as pltpu
from jax.sharding import PartitionSpec as P


ADAPTER_SCALE = 2.0
LANES = 128
PLACES = ("groups", "task")
SMALL = pltpu.CompilerParams(vmem_limit_bytes=16 * 1024 * 1024)


def swap(x, axes, shift):
    total = lax.axis_size(axes)
    return lax.ppermute(x, axes, [(a, a ^ shift) for a in range(total)])


def place():
    return lax.axis_index("groups") * lax.axis_size("task") + lax.axis_index("task")


def through_vmem(moves, scratch, arrived, left):
    fetches = [
        pltpu.make_async_copy(source, scratch.at[k], arrived.at[k])
        for k, (source, _) in enumerate(moves)
    ]
    stores = [
        pltpu.make_async_copy(scratch.at[k], target, left.at[k])
        for k, (_, target) in enumerate(moves)
    ]
    for fetch in fetches:
        fetch.start()
    for fetch, store in zip(fetches, stores):
        fetch.wait()
        store.start()
    for store in stores:
        store.wait()


def vmem_scratch(count, shape, dtype):
    return [
        pltpu.VMEM((count,) + shape, dtype),
        pltpu.SemaphoreType.DMA((count,)),
        pltpu.SemaphoreType.DMA((count,)),
    ]


def cut_kernel(shifts, stride, start, width, source, *rest):
    moves = []
    for k, shift in enumerate(shifts):
        column = pl.multiple_of((place() ^ shift) * stride + start, LANES)
        moves.append((source.at[:, :, pl.ds(column, width)], rest[k]))
    through_vmem(moves, *rest[len(shifts) :])


def cut(head, shifts, stride, start, width):
    shape = head.shape[:2] + (width,)
    return pl.pallas_call(
        functools.partial(cut_kernel, shifts, stride, start, width),
        in_specs=[pl.BlockSpec(memory_space=pl.ANY)],
        out_specs=[pl.BlockSpec(memory_space=pltpu.HBM)] * len(shifts),
        out_shape=[jax.ShapeDtypeStruct(shape, head.dtype)] * len(shifts),
        scratch_shapes=vmem_scratch(len(shifts), shape, head.dtype),
        compiler_params=SMALL,
        name="cut",
    )(pltpu.with_memory_space_constraint(head, pltpu.HBM))


def cut_row_kernel(shifts, rank, source, *pieces):
    rows = source.shape[0] // rank
    at = lax.broadcasted_iota(jnp.int32, (rows, source.shape[0]), 1)
    at = at - rank * lax.broadcasted_iota(jnp.int32, (rows, source.shape[0]), 0)
    for shift, piece in zip(shifts, pieces):
        pick = jnp.where(at == (place() ^ shift), 1.0, 0.0).astype(source.dtype)
        picked = jnp.dot(pick, source[...], preferred_element_type=jnp.float32)
        piece[...] = picked.astype(piece.dtype)


def cut_row(head, shifts):
    rows, rank, columns = head.shape
    return pl.pallas_call(
        functools.partial(cut_row_kernel, shifts, rank),
        out_shape=[jax.ShapeDtypeStruct((rows, columns), head.dtype)] * len(shifts),
        compiler_params=SMALL,
        name="cut_row",
    )(head.reshape(rows * rank, columns))


def join_kernel(shifts, stride, start, width, *refs):
    whole = refs[-4]
    moves = []
    for k, shift in enumerate(shifts):
        column = pl.multiple_of((place() ^ shift) * stride + start, LANES)
        moves.append((refs[k], whole.at[:, :, pl.ds(column, width)]))
    through_vmem(moves, *refs[-3:])


def join(pieces, shifts, stride, start, width, columns, whole):
    operands = list(pieces) + ([] if whole is None else [whole])
    return pl.pallas_call(
        functools.partial(join_kernel, shifts, stride, start, width),
        in_specs=[pl.BlockSpec(memory_space=pl.ANY)] * len(operands),
        out_specs=pl.BlockSpec(memory_space=pl.ANY),
        out_shape=jax.ShapeDtypeStruct(pieces[0].shape[:2] + (columns,), pieces[0].dtype),
        scratch_shapes=vmem_scratch(len(pieces), pieces[0].shape, pieces[0].dtype),
        input_output_aliases={} if whole is None else {len(pieces): 0},
        compiler_params=SMALL,
        name="join",
    )(*operands)


def stack_kernel(shifts, *refs):
    count = len(shifts)
    moves = [(refs[k], refs[count].at[place() ^ s]) for k, s in enumerate(shifts)]
    through_vmem(moves, *refs[count + 1 :])


def stack(pieces, shifts):
    shape, dtype = pieces[0].shape, pieces[0].dtype
    return pl.pallas_call(
        functools.partial(stack_kernel, shifts),
        in_specs=[pl.BlockSpec(memory_space=pl.ANY)] * len(pieces),
        out_specs=pl.BlockSpec(memory_space=pl.ANY),
        out_shape=jax.ShapeDtypeStruct((len(pieces),) + shape, dtype),
        scratch_shapes=vmem_scratch(len(pieces), shape, dtype),
        compiler_params=SMALL,
        name="stack",
    )(*pieces)


def in_order(pieces, shifts):
    stack = jnp.zeros((len(pieces),) + pieces[0].shape, pieces[0].dtype)
    for piece, shift in zip(pieces, shifts):
        stack = lax.dynamic_update_index_in_dim(stack, piece, place() ^ shift, 0)
    return stack


class Head:
    def __init__(self, head, chunks):
        self.rank, self.columns = head.shape[1:]
        self.head = head
        self.places = lax.axis_size("groups") * lax.axis_size("task")
        self.stride = self.columns // self.places
        self.by_lane = self.stride % (LANES * chunks) == 0
        self.by_row = not self.by_lane and self.rank == self.places
        self.chunks = chunks if self.by_lane else 1
        self.width = self.stride // self.chunks

    def cut(self, chunk, shifts):
        if self.by_lane:
            return cut(self.head, shifts, self.stride, chunk * self.width, self.width)
        if self.by_row:
            return cut_row(self.head, shifts)
        shares = self.head.reshape(-1, self.rank, self.places, self.stride).transpose(2, 0, 1, 3)
        return [lax.dynamic_index_in_dim(shares, place() ^ s, 0, keepdims=False) for s in shifts]

    def join(self, pieces, shifts, chunk=0, whole=None):
        if self.by_lane:
            start = chunk * self.width
            return join(pieces, shifts, self.stride, start, self.width, self.columns, whole)
        if self.by_row:
            whole = stack(pieces, shifts).transpose(1, 0, 2)
        else:
            whole = in_order(pieces, shifts).transpose(1, 2, 0, 3)
        return whole.reshape(whole.shape[0], self.rank, self.columns)


def rank_columns(shape, rank_axis, column_axis, rank):
    of_column = lax.broadcasted_iota(jnp.int32, shape, column_axis) % rank
    return of_column == lax.broadcasted_iota(jnp.int32, shape, rank_axis)


def inside(bounds, rows):
    row = lax.broadcasted_iota(jnp.int32, (rows, bounds.shape[1]), 0)
    return (row >= bounds[0:1]) & (row < bounds[1:2])


def turned(x, square):
    square[...] = jnp.zeros(square.shape, square.dtype)
    square[0 : x.shape[0], 0 : x.shape[1]] = x
    return square[...].T


def terms(x, count):
    parts = []
    for _ in range(count):
        parts.append(x.astype(jnp.bfloat16))
        x = x - parts[-1].astype(jnp.float32)
    return jnp.concatenate(parts)


def project_kernel(shifts, parts, stride, start, width, tokens, bounds, *refs):
    pieces, refs = refs[: len(shifts)], refs[len(shifts) :]
    before, after = refs[:-parts], refs[-parts:]
    rows = tokens.shape[0] // parts
    tasks, rank = pieces[0].shape[0] // parts, pieces[0].shape[1]
    every = []
    for turn in range(parts):
        block = lax.axis_index("tensor") ^ turn
        found = jnp.zeros((rows, tasks * rank), jnp.float32)
        for k, shift in enumerate(shifts):
            column = pl.multiple_of((place() ^ shift) * stride + start, LANES)
            found += lax.dot_general(
                tokens[pl.ds(pl.multiple_of(block * rows, 8), rows), pl.ds(column, width)],
                pieces[k][pl.ds(block * tasks, tasks)].reshape(-1, width),
                (((1,), (1,)), ((), ())),
                preferred_element_type=jnp.float32,
            )
        every.append(jnp.where(inside(bounds[block], rows), found, 0.0))
    pick = rank_columns((tasks * rank, LANES), 1, 0, rank).astype(jnp.bfloat16)
    count = 3
    summed = jnp.dot(
        terms(jnp.concatenate(every), count), pick, preferred_element_type=jnp.float32
    ).reshape(count, parts * rows, LANES)
    low_rank = sum(summed[k] for k in range(count)).T
    for turn in range(parts):
        share = low_rank[0:rank, turn * rows : (turn + 1) * rows]
        after[turn][...] = share + before[turn][...] if before else share


def in_vmem(x):
    return pltpu.with_memory_space_constraint(x, pltpu.VMEM)


def project(pieces, shifts, stride, start, width, tokens, bounds, before, near):
    parts, rank = bounds.shape[0], pieces[0].shape[1]
    rows = tokens.shape[0] // parts
    if near:
        tokens, bounds = in_vmem(tokens), in_vmem(bounds)
        before = [in_vmem(x) for x in before]
    return pl.pallas_call(
        functools.partial(project_kernel, shifts, parts, stride, start, width),
        in_specs=[pl.BlockSpec(memory_space=pltpu.VMEM)] * (2 + len(pieces) + len(before)),
        out_shape=[jax.ShapeDtypeStruct((rank, rows), jnp.float32)] * parts,
        compiler_params=SMALL,
        name="project",
    )(tokens, bounds, *pieces, *before)


def finish_kernel(count, steps, bounds, *refs):
    shares, rest = refs[:count], refs[count:]
    bases, ups, outs, makes, square, sems = rest[0:2], rest[2:4], rest[4:6], rest[6:8], *rest[8:]
    rank, rows = shares[0].shape
    low_rank = shares[0][...]
    for share in shares[1:]:
        low_rank = low_rank + share[...]
    low_rank = turned(low_rank, square)[0:rows]
    own = bounds[lax.axis_index("tensor")]
    pick = rank_columns((LANES, own.shape[1]), 0, 1, rank).astype(jnp.bfloat16)
    spread = jnp.dot(terms(low_rank, 2), pick, preferred_element_type=jnp.float32)
    own = inside(own, rows)
    spread = jnp.where(jnp.concatenate([own, own]), spread, 0.0).astype(jnp.bfloat16)
    copies = []
    for step in range(steps):
        for k, (base, up, out, made) in enumerate(zip(bases, ups, outs, makes)):
            width = base.shape[1] // steps
            columns = pl.ds(step * width, width)
            update = jnp.dot(spread, up[:, columns], preferred_element_type=jnp.float32)
            update = update[0:rows] + update[rows:]
            made[:, columns] = (base[:, columns] + ADAPTER_SCALE * update).astype(made.dtype)
            copies.append(
                pltpu.make_async_copy(made.at[:, columns], out.at[:, columns], sems.at[k, step])
            )
            copies[-1].start()
    for copy in copies:
        copy.wait()


def finish(shares, bounds, operands, steps):
    operands = [in_vmem(x) for x in (bounds, *shares, *operands)]
    shapes = [x.shape for x in operands[-4:-2]]
    return pl.pallas_call(
        functools.partial(finish_kernel, len(shares), steps),
        in_specs=[pl.BlockSpec(memory_space=pltpu.VMEM)] * len(operands),
        out_specs=[pl.BlockSpec(memory_space=pl.ANY)] * 2,
        out_shape=[jax.ShapeDtypeStruct(shape, jnp.bfloat16) for shape in shapes],
        scratch_shapes=[pltpu.VMEM(shape, jnp.bfloat16) for shape in shapes]
        + [pltpu.VMEM((LANES, LANES), jnp.float32), pltpu.SemaphoreType.DMA((2, steps))],
        compiler_params=SMALL,
        name="finish",
    )(*operands)


def halving_order(total):
    bits = total.bit_length() - 1
    return [int(format(o, "b").zfill(bits)[::-1], 2) if bits else 0 for o in range(total)]


def reduce_blocks(partial, axis):
    step = 1
    while True:
        half = partial.shape[0] // 2
        came = swap(partial[half:], axis, step)
        if half == 1:
            return partial[0] + came[0]
        partial = partial[:half] + came
        step *= 2


def gather_blocks(x, axis):
    x = x[None]
    step = 1
    while step < lax.axis_size(axis):
        came = swap(x, axis, step)
        upper = (lax.axis_index(axis) & step) > 0
        x = jnp.concatenate([jnp.where(upper, came, x), jnp.where(upper, x, came)])
        step *= 2
    return x


def local(
    tokens,
    task_counts,
    task_embeddings,
    embedding_weight,
    down_factor_head,
    query_up_head,
    value_up_head,
    w_query,
    w_value,
):
    groups, ring, parts = lax.axis_size("groups"), lax.axis_size("task"), lax.axis_size("tensor")
    places = groups * ring
    tok_rows, shard_width = tokens.shape
    block_rows = tok_rows // parts
    own_tasks = task_counts.shape[0]
    block_tasks = own_tasks // parts
    rank = query_up_head.shape[1]
    hidden_rows = down_factor_head.shape[0]
    tensor = lax.axis_index("tensor")
    ring_shifts = list(range(ring))
    far_first = sorted(ring_shifts[1:], reverse=True)
    shifts = list(range(places))

    heads = {
        "value": Head(value_up_head, 1),
        "query": Head(query_up_head, 1),
        "down": Head(down_factor_head, 2),
    }

    def fetch(name, chunk):
        pieces = heads[name].cut(chunk, far_first + [0])
        got = {s: swap(p, "task", s) if s else p for s, p in zip(far_first + [0], pieces)}
        return jnp.concatenate([got[s] for s in ring_shifts], axis=0)

    fetched = {}
    fetched["query", 0] = fetch("query", 0)

    share = own_tasks // parts
    embeddings = lax.dynamic_index_in_dim(
        task_embeddings.reshape(parts, share, -1), tensor, 0, keepdims=False
    )
    hidden = jax.nn.silu(
        jnp.dot(embeddings, embedding_weight, preferred_element_type=jnp.float32)
    ).astype(jnp.bfloat16)
    far, came = ring // 2, [0, ring // 2]
    ring_hidden = jnp.concatenate([hidden[None], swap(hidden[None], "task", far)])
    while far > 1:
        far //= 2
        ring_hidden = jnp.concatenate([ring_hidden, swap(ring_hidden, "task", far)])
        came = came + [s ^ far for s in came]
    ring_hidden = jnp.stack([ring_hidden[came.index(s)] for s in ring_shifts])
    group_hidden = jnp.concatenate(
        [ring_hidden] + [swap(ring_hidden, "groups", s) for s in range(1, groups)]
    )
    every_hidden = gather_blocks(group_hidden.reshape(places * share, -1), "tensor")
    every_hidden = every_hidden.reshape(parts, places, share, ring, hidden_rows)
    every_hidden = every_hidden.transpose(3, 1, 0, 2, 4)
    every_hidden = every_hidden.reshape(ring, places * own_tasks, hidden_rows)
    every_hidden = jnp.concatenate(
        [
            lax.dynamic_index_in_dim(every_hidden, lax.axis_index("task") ^ s, 0, keepdims=False)
            for s in ring_shifts
        ],
        axis=1,
    )

    chunks = heads["down"].chunks
    for chunk in range(chunks):
        fetched["down", chunk] = fetch("down", chunk)
    fetched["value", 0] = fetch("value", 0)

    def emit(name, chunk):
        matrix = fetched[name, chunk]
        flat = jnp.dot(
            every_hidden, matrix.reshape(matrix.shape[0], -1), preferred_element_type=jnp.float32
        ).astype(jnp.bfloat16)
        return flat.reshape((places, own_tasks) + matrix.shape[1:])

    def send(made, sent):
        return {s: swap(made[s], PLACES, s) if s else made[s] for s in sent}

    crossing = [s for s in shifts if s % ring >= ring // 2]
    crossing = sorted(crossing, key=lambda s: -(s // ring))
    late = crossing[-1:]
    near = [s for s in reversed(shifts) if s % ring < ring // 2]
    early = sorted(near, key=lambda s: s % ring == 0) + crossing[:-1]
    emitted = {}
    for name, chunk in [("query", 0), ("value", 0)] + [("down", c) for c in range(chunks)]:
        made = emit(name, chunk)
        emitted[name, chunk] = send(made, early)
        emitted[name, chunk].update(send(made, late))

    def ordered(pieces):
        return [pieces[s] for s in shifts]

    token_blocks = tokens.reshape(parts, block_rows, shard_width)
    order = halving_order(parts)
    turned = jnp.concatenate(
        [lax.dynamic_index_in_dim(token_blocks, tensor ^ s, 0, keepdims=False) for s in order]
    )
    base_query = jnp.dot(turned, w_query, preferred_element_type=jnp.float32)
    base_value = jnp.dot(turned, w_value, preferred_element_type=jnp.float32)
    base_query = reduce_blocks(base_query.reshape(parts, block_rows, -1), "tensor")
    base_value = reduce_blocks(base_value.reshape(parts, block_rows, -1), "tensor")

    def own_block(factors, above, below):
        moved = lax.all_to_all(factors, "tensor", split_axis=0, concat_axis=0, tiled=True)
        moved = moved.reshape(parts, block_tasks, rank, -1).transpose(1, 2, 0, 3)
        moved = moved.reshape(block_tasks, rank, -1)
        moved = jnp.pad(moved, ((0, 0), (above, below), (0, 0)))
        return moved.reshape(block_tasks * 2 * rank, -1)

    query_up_factors = heads["query"].join(ordered(emitted["query", 0]), shifts)
    own_query = own_block(query_up_factors, 0, rank)
    value_up_factors = heads["value"].join(ordered(emitted["value", 0]), shifts)
    own_value = own_block(value_up_factors, rank, 0)

    tallies = task_counts.reshape(parts, block_tasks)
    ends = jnp.cumsum(tallies, axis=1)
    begins = ends - tallies
    bounds = jnp.repeat(jnp.stack([begins, ends], axis=1), 2 * rank, axis=2)

    down_factors, low_rank = None, []
    head = heads["down"]
    if head.by_lane:
        for chunk in range(chunks):
            pieces, start = emitted["down", chunk], chunk * head.width
            for half in [early, late] if chunk + 1 == chunks else [early + late]:
                some = [pieces[s] for s in half]
                low_rank = project(
                    some, half, head.stride, start, head.width, tokens, bounds, low_rank,
                    half is late,
                )
            down_factors = head.join(
                [pieces[s] for s in early + late], early + late, chunk, down_factors
            )
    else:
        down_factors = head.join(ordered(emitted["down", 0]), shifts)
        projected = jnp.einsum(
            "bpd,bmd->bpm",
            token_blocks,
            down_factors.reshape(parts, block_tasks * 2 * rank, shard_width),
            preferred_element_type=jnp.float32,
        )
        projected = jnp.where(jax.vmap(lambda b: inside(b, block_rows))(bounds), projected, 0.0)
        projected = projected.reshape(parts, block_rows, block_tasks, 2 * rank).sum(axis=2)
        projected = projected.transpose(0, 2, 1)
        low_rank = [
            lax.dynamic_index_in_dim(projected, tensor ^ s, 0, keepdims=False)
            for s in range(parts)
        ]
    shares = [low_rank[0]] + [swap(low_rank[s], "tensor", s) for s in range(1, parts)]
    query, value = finish(shares, bounds, [base_query, base_value, own_query, own_value], steps=4)
    return query, value, down_factors, query_up_factors, value_up_factors


def solution(mesh):
    return jax.shard_map(
        local,
        mesh=mesh,
        in_specs=(
            P(("groups", "task"), "tensor"),
            P(("groups", "task")),
            P(("groups", "task"), None),
            P(),
            P("task", None, "tensor"),
            P("task", None, "tensor"),
            P("task", None, "tensor"),
            P("tensor", None),
            P("tensor", None),
        ),
        out_specs=(
            P(("groups", "task", "tensor"), None),
            P(("groups", "task", "tensor"), None),
            P(("groups", "task"), None, "tensor"),
            P(("groups", "task"), None, "tensor"),
            P(("groups", "task"), None, "tensor"),
        ),
        check_vma=False,
    )
```

```python
import functools

import jax
import jax.numpy as jnp
from jax import lax
from jax.experimental import pallas as pl
from jax.experimental.pallas import tpu as pltpu
from jax.sharding import PartitionSpec as P


ADAPTER_SCALE = 2.0
LANES = 128
PLACES = ("groups", "task")
SMALL = pltpu.CompilerParams(vmem_limit_bytes=16 * 1024 * 1024)


def swap(x, axes, shift):
    total = lax.axis_size(axes)
    return lax.ppermute(x, axes, [(a, a ^ shift) for a in range(total)])


def place():
    return lax.axis_index("groups") * lax.axis_size("task") + lax.axis_index("task")


def through_vmem(moves, scratch, arrived, left):
    fetches = [
        pltpu.make_async_copy(source, scratch.at[k], arrived.at[k])
        for k, (source, _) in enumerate(moves)
    ]
    stores = [
        pltpu.make_async_copy(scratch.at[k], target, left.at[k])
        for k, (_, target) in enumerate(moves)
    ]
    for fetch in fetches:
        fetch.start()
    for fetch, store in zip(fetches, stores):
        fetch.wait()
        store.start()
    for store in stores:
        store.wait()


def vmem_scratch(count, shape, dtype):
    return [
        pltpu.VMEM((count,) + shape, dtype),
        pltpu.SemaphoreType.DMA((count,)),
        pltpu.SemaphoreType.DMA((count,)),
    ]


def cut_kernel(shifts, stride, start, width, source, *rest):
    moves = []
    for k, shift in enumerate(shifts):
        column = pl.multiple_of((place() ^ shift) * stride + start, LANES)
        moves.append((source.at[:, :, pl.ds(column, width)], rest[k]))
    through_vmem(moves, *rest[len(shifts) :])


def cut(head, shifts, stride, start, width):
    shape = head.shape[:2] + (width,)
    return pl.pallas_call(
        functools.partial(cut_kernel, shifts, stride, start, width),
        in_specs=[pl.BlockSpec(memory_space=pl.ANY)],
        out_specs=[pl.BlockSpec(memory_space=pltpu.HBM)] * len(shifts),
        out_shape=[jax.ShapeDtypeStruct(shape, head.dtype)] * len(shifts),
        scratch_shapes=vmem_scratch(len(shifts), shape, head.dtype),
        compiler_params=SMALL,
        name="cut",
    )(pltpu.with_memory_space_constraint(head, pltpu.HBM))


def cut_row_kernel(shifts, rank, source, *pieces):
    rows = source.shape[0] // rank
    at = lax.broadcasted_iota(jnp.int32, (rows, source.shape[0]), 1)
    at = at - rank * lax.broadcasted_iota(jnp.int32, (rows, source.shape[0]), 0)
    for shift, piece in zip(shifts, pieces):
        pick = jnp.where(at == (place() ^ shift), 1.0, 0.0).astype(source.dtype)
        picked = jnp.dot(pick, source[...], preferred_element_type=jnp.float32)
        piece[...] = picked.astype(piece.dtype)


def cut_row(head, shifts):
    rows, rank, columns = head.shape
    return pl.pallas_call(
        functools.partial(cut_row_kernel, shifts, rank),
        out_shape=[jax.ShapeDtypeStruct((rows, columns), head.dtype)] * len(shifts),
        compiler_params=SMALL,
        name="cut_row",
    )(head.reshape(rows * rank, columns))


def join_kernel(shifts, stride, start, width, *refs):
    whole = refs[-4]
    moves = []
    for k, shift in enumerate(shifts):
        column = pl.multiple_of((place() ^ shift) * stride + start, LANES)
        moves.append((refs[k], whole.at[:, :, pl.ds(column, width)]))
    through_vmem(moves, *refs[-3:])


def join(pieces, shifts, stride, start, width, columns, whole):
    operands = list(pieces) + ([] if whole is None else [whole])
    return pl.pallas_call(
        functools.partial(join_kernel, shifts, stride, start, width),
        in_specs=[pl.BlockSpec(memory_space=pl.ANY)] * len(operands),
        out_specs=pl.BlockSpec(memory_space=pl.ANY),
        out_shape=jax.ShapeDtypeStruct(pieces[0].shape[:2] + (columns,), pieces[0].dtype),
        scratch_shapes=vmem_scratch(len(pieces), pieces[0].shape, pieces[0].dtype),
        input_output_aliases={} if whole is None else {len(pieces): 0},
        compiler_params=SMALL,
        name="join",
    )(*operands)


def stack_kernel(shifts, *refs):
    count = len(shifts)
    moves = [(refs[k], refs[count].at[place() ^ s]) for k, s in enumerate(shifts)]
    through_vmem(moves, *refs[count + 1 :])


def stack(pieces, shifts):
    shape, dtype = pieces[0].shape, pieces[0].dtype
    return pl.pallas_call(
        functools.partial(stack_kernel, shifts),
        in_specs=[pl.BlockSpec(memory_space=pl.ANY)] * len(pieces),
        out_specs=pl.BlockSpec(memory_space=pl.ANY),
        out_shape=jax.ShapeDtypeStruct((len(pieces),) + shape, dtype),
        scratch_shapes=vmem_scratch(len(pieces), shape, dtype),
        compiler_params=SMALL,
        name="stack",
    )(*pieces)


def in_order(pieces, shifts):
    stack = jnp.zeros((len(pieces),) + pieces[0].shape, pieces[0].dtype)
    for piece, shift in zip(pieces, shifts):
        stack = lax.dynamic_update_index_in_dim(stack, piece, place() ^ shift, 0)
    return stack


class Head:
    def __init__(self, head, chunks):
        self.rank, self.columns = head.shape[1:]
        self.head = head
        self.places = lax.axis_size("groups") * lax.axis_size("task")
        self.stride = self.columns // self.places
        self.by_lane = self.stride % (LANES * chunks) == 0
        self.by_row = not self.by_lane and self.rank == self.places
        self.chunks = chunks if self.by_lane else 1
        self.width = self.stride // self.chunks

    def cut(self, chunk, shifts):
        if self.by_lane:
            return cut(self.head, shifts, self.stride, chunk * self.width, self.width)
        if self.by_row:
            return cut_row(self.head, shifts)
        shares = self.head.reshape(-1, self.rank, self.places, self.stride).transpose(2, 0, 1, 3)
        return [lax.dynamic_index_in_dim(shares, place() ^ s, 0, keepdims=False) for s in shifts]

    def join(self, pieces, shifts, chunk=0, whole=None):
        if self.by_lane:
            start = chunk * self.width
            return join(pieces, shifts, self.stride, start, self.width, self.columns, whole)
        if self.by_row:
            whole = stack(pieces, shifts).transpose(1, 0, 2)
        else:
            whole = in_order(pieces, shifts).transpose(1, 2, 0, 3)
        return whole.reshape(whole.shape[0], self.rank, self.columns)


def rank_columns(shape, rank_axis, column_axis, rank):
    of_column = lax.broadcasted_iota(jnp.int32, shape, column_axis) % rank
    return of_column == lax.broadcasted_iota(jnp.int32, shape, rank_axis)


def inside(bounds, rows):
    row = lax.broadcasted_iota(jnp.int32, (rows, bounds.shape[1]), 0)
    return (row >= bounds[0:1]) & (row < bounds[1:2])


def turned(x, square):
    square[...] = jnp.zeros(square.shape, square.dtype)
    square[0 : x.shape[0], 0 : x.shape[1]] = x
    return square[...].T


def terms(x, count):
    parts = []
    for _ in range(count):
        parts.append(x.astype(jnp.bfloat16))
        x = x - parts[-1].astype(jnp.float32)
    return jnp.concatenate(parts)


def project_kernel(shifts, parts, stride, start, width, tokens, bounds, *refs):
    pieces, refs = refs[: len(shifts)], refs[len(shifts) :]
    before, after = refs[:-parts], refs[-parts:]
    rows = tokens.shape[0] // parts
    tasks, rank = pieces[0].shape[0] // parts, pieces[0].shape[1]
    every = []
    for turn in range(parts):
        block = lax.axis_index("tensor") ^ turn
        found = jnp.zeros((rows, tasks * rank), jnp.float32)
        for k, shift in enumerate(shifts):
            column = pl.multiple_of((place() ^ shift) * stride + start, LANES)
            found += lax.dot_general(
                tokens[pl.ds(pl.multiple_of(block * rows, 8), rows), pl.ds(column, width)],
                pieces[k][pl.ds(block * tasks, tasks)].reshape(-1, width),
                (((1,), (1,)), ((), ())),
                preferred_element_type=jnp.float32,
            )
        every.append(jnp.where(inside(bounds[block], rows), found, 0.0))
    pick = rank_columns((tasks * rank, LANES), 1, 0, rank).astype(jnp.bfloat16)
    count = 3
    summed = jnp.dot(
        terms(jnp.concatenate(every), count), pick, preferred_element_type=jnp.float32
    ).reshape(count, parts * rows, LANES)
    low_rank = sum(summed[k] for k in range(count)).T
    for turn in range(parts):
        share = low_rank[0:rank, turn * rows : (turn + 1) * rows]
        after[turn][...] = share + before[turn][...] if before else share


def in_vmem(x):
    return pltpu.with_memory_space_constraint(x, pltpu.VMEM)


def project(pieces, shifts, stride, start, width, tokens, bounds, before, near):
    parts, rank = bounds.shape[0], pieces[0].shape[1]
    rows = tokens.shape[0] // parts
    if near:
        tokens, bounds = in_vmem(tokens), in_vmem(bounds)
        before = [in_vmem(x) for x in before]
    return pl.pallas_call(
        functools.partial(project_kernel, shifts, parts, stride, start, width),
        in_specs=[pl.BlockSpec(memory_space=pltpu.VMEM)] * (2 + len(pieces) + len(before)),
        out_shape=[jax.ShapeDtypeStruct((rank, rows), jnp.float32)] * parts,
        compiler_params=SMALL,
        name="project",
    )(tokens, bounds, *pieces, *before)


def finish_kernel(count, steps, bounds, *refs):
    shares, rest = refs[:count], refs[count:]
    bases, ups, outs, makes, square, sems = rest[0:2], rest[2:4], rest[4:6], rest[6:8], *rest[8:]
    rank, rows = shares[0].shape
    low_rank = shares[0][...]
    for share in shares[1:]:
        low_rank = low_rank + share[...]
    low_rank = turned(low_rank, square)[0:rows]
    own = bounds[lax.axis_index("tensor")]
    pick = rank_columns((LANES, own.shape[1]), 0, 1, rank).astype(jnp.bfloat16)
    spread = jnp.dot(terms(low_rank, 2), pick, preferred_element_type=jnp.float32)
    own = inside(own, rows)
    spread = jnp.where(jnp.concatenate([own, own]), spread, 0.0).astype(jnp.bfloat16)
    copies = []
    for step in range(steps):
        for k, (base, up, out, made) in enumerate(zip(bases, ups, outs, makes)):
            width = base.shape[1] // steps
            columns = pl.ds(step * width, width)
            update = jnp.dot(spread, up[:, columns], preferred_element_type=jnp.float32)
            update = update[0:rows] + update[rows:]
            made[:, columns] = (base[:, columns] + ADAPTER_SCALE * update).astype(made.dtype)
            copies.append(
                pltpu.make_async_copy(made.at[:, columns], out.at[:, columns], sems.at[k, step])
            )
            copies[-1].start()
    for copy in copies:
        copy.wait()


def finish(shares, bounds, operands, steps):
    operands = [in_vmem(x) for x in (bounds, *shares, *operands)]
    shapes = [x.shape for x in operands[-4:-2]]
    return pl.pallas_call(
        functools.partial(finish_kernel, len(shares), steps),
        in_specs=[pl.BlockSpec(memory_space=pltpu.VMEM)] * len(operands),
        out_specs=[pl.BlockSpec(memory_space=pl.ANY)] * 2,
        out_shape=[jax.ShapeDtypeStruct(shape, jnp.bfloat16) for shape in shapes],
        scratch_shapes=[pltpu.VMEM(shape, jnp.bfloat16) for shape in shapes]
        + [pltpu.VMEM((LANES, LANES), jnp.float32), pltpu.SemaphoreType.DMA((2, steps))],
        compiler_params=SMALL,
        name="finish",
    )(*operands)


def halving_order(total):
    bits = total.bit_length() - 1
    return [int(format(o, "b").zfill(bits)[::-1], 2) if bits else 0 for o in range(total)]


def reduce_blocks(partial, axis):
    step = 1
    while True:
        half = partial.shape[0] // 2
        came = swap(partial[half:], axis, step)
        if half == 1:
            return partial[0] + came[0]
        partial = partial[:half] + came
        step *= 2


def gather_blocks(x, axis):
    x = x[None]
    step = 1
    while step < lax.axis_size(axis):
        came = swap(x, axis, step)
        upper = (lax.axis_index(axis) & step) > 0
        x = jnp.concatenate([jnp.where(upper, came, x), jnp.where(upper, x, came)])
        step *= 2
    return x


def local(
    tokens,
    task_counts,
    task_embeddings,
    embedding_weight,
    down_factor_head,
    query_up_head,
    value_up_head,
    w_query,
    w_value,
):
    groups, ring, parts = lax.axis_size("groups"), lax.axis_size("task"), lax.axis_size("tensor")
    places = groups * ring
    tok_rows, shard_width = tokens.shape
    block_rows = tok_rows // parts
    own_tasks = task_counts.shape[0]
    block_tasks = own_tasks // parts
    rank = query_up_head.shape[1]
    hidden_rows = down_factor_head.shape[0]
    tensor = lax.axis_index("tensor")
    ring_shifts = list(range(ring))
    far_first = sorted(ring_shifts[1:], reverse=True)
    shifts = list(range(places))

    heads = {
        "value": Head(value_up_head, 1),
        "query": Head(query_up_head, 1),
        "down": Head(down_factor_head, 2),
    }

    def fetch(name, chunk, ahead=()):
        head, got = heads[name], {}
        for s in ahead:
            start = (place() ^ s) * head.stride
            piece = lax.dynamic_slice_in_dim(head.head, start, head.width, axis=2)
            got[s] = swap(piece, "task", s)
        rest = [s for s in far_first + [0] if s not in ahead]
        for s, piece in zip(rest, head.cut(chunk, rest)):
            got[s] = swap(piece, "task", s) if s else piece
        return jnp.concatenate([got[s] for s in ring_shifts], axis=0)

    fetched = {}
    ahead = far_first[:1] if heads["query"].by_lane else []
    fetched["query", 0] = fetch("query", 0, ahead)

    share = own_tasks // parts
    embeddings = lax.dynamic_index_in_dim(
        task_embeddings.reshape(parts, share, -1), tensor, 0, keepdims=False
    )
    hidden = jax.nn.silu(
        jnp.dot(embeddings, embedding_weight, preferred_element_type=jnp.float32)
    ).astype(jnp.bfloat16)
    far, came = ring // 2, [0, ring // 2]
    ring_hidden = jnp.concatenate([hidden[None], swap(hidden[None], "task", far)])
    while far > 1:
        far //= 2
        ring_hidden = jnp.concatenate([ring_hidden, swap(ring_hidden, "task", far)])
        came = came + [s ^ far for s in came]
    ring_hidden = jnp.stack([ring_hidden[came.index(s)] for s in ring_shifts])
    group_hidden = jnp.concatenate(
        [ring_hidden] + [swap(ring_hidden, "groups", s) for s in range(1, groups)]
    )
    every_hidden = gather_blocks(group_hidden.reshape(places * share, -1), "tensor")
    every_hidden = every_hidden.reshape(parts, places, share, ring, hidden_rows)
    every_hidden = every_hidden.transpose(3, 1, 0, 2, 4)
    every_hidden = every_hidden.reshape(ring, places * own_tasks, hidden_rows)
    every_hidden = jnp.concatenate(
        [
            lax.dynamic_index_in_dim(every_hidden, lax.axis_index("task") ^ s, 0, keepdims=False)
            for s in ring_shifts
        ],
        axis=1,
    )

    chunks = heads["down"].chunks
    for chunk in range(chunks):
        fetched["down", chunk] = fetch("down", chunk)
    fetched["value", 0] = fetch("value", 0)

    def emit(name, chunk):
        matrix = fetched[name, chunk]
        flat = jnp.dot(
            every_hidden, matrix.reshape(matrix.shape[0], -1), preferred_element_type=jnp.float32
        ).astype(jnp.bfloat16)
        return flat.reshape((places, own_tasks) + matrix.shape[1:])

    def send(made, sent):
        return {s: swap(made[s], PLACES, s) if s else made[s] for s in sent}

    crossing = [s for s in shifts if s % ring >= ring // 2]
    crossing = sorted(crossing, key=lambda s: (s < ring, s if s < ring else -s))
    late = crossing[-1:]
    near = [s for s in reversed(shifts) if s % ring < ring // 2]
    early = sorted(near, key=lambda s: s % ring == 0) + crossing[:-1]
    emitted = {}
    for name, chunk in [("query", 0), ("value", 0)] + [("down", c) for c in range(chunks)]:
        made = emit(name, chunk)
        emitted[name, chunk] = send(made, early)
        emitted[name, chunk].update(send(made, late))

    def ordered(pieces):
        return [pieces[s] for s in shifts]

    token_blocks = tokens.reshape(parts, block_rows, shard_width)
    order = halving_order(parts)
    turned = jnp.concatenate(
        [lax.dynamic_index_in_dim(token_blocks, tensor ^ s, 0, keepdims=False) for s in order]
    )
    base_query = jnp.dot(turned, w_query, preferred_element_type=jnp.float32)
    base_value = jnp.dot(turned, w_value, preferred_element_type=jnp.float32)
    base_query = reduce_blocks(base_query.reshape(parts, block_rows, -1), "tensor")
    base_value = reduce_blocks(base_value.reshape(parts, block_rows, -1), "tensor")

    def own_block(factors, above, below):
        moved = lax.all_to_all(factors, "tensor", split_axis=0, concat_axis=0, tiled=True)
        moved = moved.reshape(parts, block_tasks, rank, -1).transpose(1, 2, 0, 3)
        moved = moved.reshape(block_tasks, rank, -1)
        moved = jnp.pad(moved, ((0, 0), (above, below), (0, 0)))
        return moved.reshape(block_tasks * 2 * rank, -1)

    query_up_factors = heads["query"].join(ordered(emitted["query", 0]), shifts)
    own_query = own_block(query_up_factors, 0, rank)
    value_up_factors = heads["value"].join(ordered(emitted["value", 0]), shifts)
    own_value = own_block(value_up_factors, rank, 0)

    tallies = task_counts.reshape(parts, block_tasks)
    ends = jnp.cumsum(tallies, axis=1)
    begins = ends - tallies
    bounds = jnp.repeat(jnp.stack([begins, ends], axis=1), 2 * rank, axis=2)

    down_factors, low_rank = None, []
    head = heads["down"]
    if head.by_lane:
        for chunk in range(chunks):
            pieces, start = emitted["down", chunk], chunk * head.width
            for half in [early, late] if chunk + 1 == chunks else [early + late]:
                some = [pieces[s] for s in half]
                low_rank = project(
                    some, half, head.stride, start, head.width, tokens, bounds, low_rank,
                    half is late,
                )
            down_factors = head.join(
                [pieces[s] for s in early + late], early + late, chunk, down_factors
            )
    else:
        down_factors = head.join(ordered(emitted["down", 0]), shifts)
        projected = jnp.einsum(
            "bpd,bmd->bpm",
            token_blocks,
            down_factors.reshape(parts, block_tasks * 2 * rank, shard_width),
            preferred_element_type=jnp.float32,
        )
        projected = jnp.where(jax.vmap(lambda b: inside(b, block_rows))(bounds), projected, 0.0)
        projected = projected.reshape(parts, block_rows, block_tasks, 2 * rank).sum(axis=2)
        projected = projected.transpose(0, 2, 1)
        low_rank = [
            lax.dynamic_index_in_dim(projected, tensor ^ s, 0, keepdims=False)
            for s in range(parts)
        ]
    shares = [low_rank[0]] + [swap(low_rank[s], "tensor", s) for s in range(1, parts)]
    query, value = finish(shares, bounds, [base_query, base_value, own_query, own_value], steps=4)
    return query, value, down_factors, query_up_factors, value_up_factors


def solution(mesh):
    return jax.shard_map(
        local,
        mesh=mesh,
        in_specs=(
            P(("groups", "task"), "tensor"),
            P(("groups", "task")),
            P(("groups", "task"), None),
            P(),
            P("task", None, "tensor"),
            P("task", None, "tensor"),
            P("task", None, "tensor"),
            P("tensor", None),
            P("tensor", None),
        ),
        out_specs=(
            P(("groups", "task", "tensor"), None),
            P(("groups", "task", "tensor"), None),
            P(("groups", "task"), None, "tensor"),
            P(("groups", "task"), None, "tensor"),
            P(("groups", "task"), None, "tensor"),
        ),
        check_vma=False,
    )
```

```python
import functools

import jax
import jax.numpy as jnp
from jax import lax
from jax.experimental import pallas as pl
from jax.experimental.pallas import tpu as pltpu
from jax.sharding import PartitionSpec as P


ADAPTER_SCALE = 2.0
LANES = 128
PLACES = ("groups", "task")
SMALL = pltpu.CompilerParams(vmem_limit_bytes=16 * 1024 * 1024)


def swap(x, axes, shift):
    total = lax.axis_size(axes)
    return lax.ppermute(x, axes, [(a, a ^ shift) for a in range(total)])


def place():
    return lax.axis_index("groups") * lax.axis_size("task") + lax.axis_index("task")


def through_vmem(moves, scratch, arrived, left):
    fetches = [
        pltpu.make_async_copy(source, scratch.at[k], arrived.at[k])
        for k, (source, _) in enumerate(moves)
    ]
    stores = [
        pltpu.make_async_copy(scratch.at[k], target, left.at[k])
        for k, (_, target) in enumerate(moves)
    ]
    for fetch in fetches:
        fetch.start()
    for fetch, store in zip(fetches, stores):
        fetch.wait()
        store.start()
    for store in stores:
        store.wait()


def vmem_scratch(count, shape, dtype):
    return [
        pltpu.VMEM((count,) + shape, dtype),
        pltpu.SemaphoreType.DMA((count,)),
        pltpu.SemaphoreType.DMA((count,)),
    ]


def cut_kernel(shifts, stride, start, width, source, *rest):
    moves = []
    for k, shift in enumerate(shifts):
        column = pl.multiple_of((place() ^ shift) * stride + start, LANES)
        moves.append((source.at[:, :, pl.ds(column, width)], rest[k]))
    through_vmem(moves, *rest[len(shifts) :])


def cut(head, shifts, stride, start, width):
    shape = head.shape[:2] + (width,)
    return pl.pallas_call(
        functools.partial(cut_kernel, shifts, stride, start, width),
        in_specs=[pl.BlockSpec(memory_space=pl.ANY)],
        out_specs=[pl.BlockSpec(memory_space=pltpu.HBM)] * len(shifts),
        out_shape=[jax.ShapeDtypeStruct(shape, head.dtype)] * len(shifts),
        scratch_shapes=vmem_scratch(len(shifts), shape, head.dtype),
        compiler_params=SMALL,
        name="cut",
    )(pltpu.with_memory_space_constraint(head, pltpu.HBM))


def cut_row_kernel(shifts, rank, source, *pieces):
    rows = source.shape[0] // rank
    at = lax.broadcasted_iota(jnp.int32, (rows, source.shape[0]), 1)
    at = at - rank * lax.broadcasted_iota(jnp.int32, (rows, source.shape[0]), 0)
    for shift, piece in zip(shifts, pieces):
        pick = jnp.where(at == (place() ^ shift), 1.0, 0.0).astype(source.dtype)
        picked = jnp.dot(pick, source[...], preferred_element_type=jnp.float32)
        piece[...] = picked.astype(piece.dtype)


def cut_row(head, shifts):
    rows, rank, columns = head.shape
    return pl.pallas_call(
        functools.partial(cut_row_kernel, shifts, rank),
        out_shape=[jax.ShapeDtypeStruct((rows, columns), head.dtype)] * len(shifts),
        compiler_params=SMALL,
        name="cut_row",
    )(head.reshape(rows * rank, columns))


def join_kernel(shifts, stride, start, width, *refs):
    whole = refs[-4]
    moves = []
    for k, shift in enumerate(shifts):
        column = pl.multiple_of((place() ^ shift) * stride + start, LANES)
        moves.append((refs[k], whole.at[:, :, pl.ds(column, width)]))
    through_vmem(moves, *refs[-3:])


def join(pieces, shifts, stride, start, width, columns, whole):
    operands = list(pieces) + ([] if whole is None else [whole])
    return pl.pallas_call(
        functools.partial(join_kernel, shifts, stride, start, width),
        in_specs=[pl.BlockSpec(memory_space=pl.ANY)] * len(operands),
        out_specs=pl.BlockSpec(memory_space=pl.ANY),
        out_shape=jax.ShapeDtypeStruct(pieces[0].shape[:2] + (columns,), pieces[0].dtype),
        scratch_shapes=vmem_scratch(len(pieces), pieces[0].shape, pieces[0].dtype),
        input_output_aliases={} if whole is None else {len(pieces): 0},
        compiler_params=SMALL,
        name="join",
    )(*operands)


def stack_kernel(shifts, *refs):
    count = len(shifts)
    moves = [(refs[k], refs[count].at[place() ^ s]) for k, s in enumerate(shifts)]
    through_vmem(moves, *refs[count + 1 :])


def stack(pieces, shifts):
    shape, dtype = pieces[0].shape, pieces[0].dtype
    return pl.pallas_call(
        functools.partial(stack_kernel, shifts),
        in_specs=[pl.BlockSpec(memory_space=pl.ANY)] * len(pieces),
        out_specs=pl.BlockSpec(memory_space=pl.ANY),
        out_shape=jax.ShapeDtypeStruct((len(pieces),) + shape, dtype),
        scratch_shapes=vmem_scratch(len(pieces), shape, dtype),
        compiler_params=SMALL,
        name="stack",
    )(*pieces)


def in_order(pieces, shifts):
    stack = jnp.zeros((len(pieces),) + pieces[0].shape, pieces[0].dtype)
    for piece, shift in zip(pieces, shifts):
        stack = lax.dynamic_update_index_in_dim(stack, piece, place() ^ shift, 0)
    return stack


class Head:
    def __init__(self, head, chunks):
        self.rank, self.columns = head.shape[1:]
        self.head = head
        self.places = lax.axis_size("groups") * lax.axis_size("task")
        self.stride = self.columns // self.places
        self.by_lane = self.stride % (LANES * chunks) == 0
        self.by_row = not self.by_lane and self.rank == self.places
        self.chunks = chunks if self.by_lane else 1
        self.width = self.stride // self.chunks

    def cut(self, chunk, shifts):
        if self.by_lane:
            return cut(self.head, shifts, self.stride, chunk * self.width, self.width)
        if self.by_row:
            return cut_row(self.head, shifts)
        shares = self.head.reshape(-1, self.rank, self.places, self.stride).transpose(2, 0, 1, 3)
        return [lax.dynamic_index_in_dim(shares, place() ^ s, 0, keepdims=False) for s in shifts]

    def join(self, pieces, shifts, chunk=0, whole=None):
        if self.by_lane:
            start = chunk * self.width
            return join(pieces, shifts, self.stride, start, self.width, self.columns, whole)
        if self.by_row:
            whole = stack(pieces, shifts).transpose(1, 0, 2)
        else:
            whole = in_order(pieces, shifts).transpose(1, 2, 0, 3)
        return whole.reshape(whole.shape[0], self.rank, self.columns)


def rank_columns(shape, rank_axis, column_axis, rank):
    of_column = lax.broadcasted_iota(jnp.int32, shape, column_axis) % rank
    return of_column == lax.broadcasted_iota(jnp.int32, shape, rank_axis)


def inside(bounds, rows):
    row = lax.broadcasted_iota(jnp.int32, (rows, bounds.shape[1]), 0)
    return (row >= bounds[0:1]) & (row < bounds[1:2])


def turned(x, square):
    square[...] = jnp.zeros(square.shape, square.dtype)
    square[0 : x.shape[0], 0 : x.shape[1]] = x
    return square[...].T


def terms(x, count):
    parts = []
    for _ in range(count):
        parts.append(x.astype(jnp.bfloat16))
        x = x - parts[-1].astype(jnp.float32)
    return jnp.concatenate(parts)


def project_kernel(shifts, parts, stride, start, width, tokens, bounds, *refs):
    pieces, refs = refs[: len(shifts)], refs[len(shifts) :]
    before, after = refs[:-parts], refs[-parts:]
    rows = tokens.shape[0] // parts
    tasks, rank = pieces[0].shape[0] // parts, pieces[0].shape[1]
    every = []
    for turn in range(parts):
        block = lax.axis_index("tensor") ^ turn
        found = jnp.zeros((rows, tasks * rank), jnp.float32)
        for k, shift in enumerate(shifts):
            column = pl.multiple_of((place() ^ shift) * stride + start, LANES)
            found += lax.dot_general(
                tokens[pl.ds(pl.multiple_of(block * rows, 8), rows), pl.ds(column, width)],
                pieces[k][pl.ds(block * tasks, tasks)].reshape(-1, width),
                (((1,), (1,)), ((), ())),
                preferred_element_type=jnp.float32,
            )
        every.append(jnp.where(inside(bounds[block], rows), found, 0.0))
    pick = rank_columns((tasks * rank, LANES), 1, 0, rank).astype(jnp.bfloat16)
    count = 3
    summed = jnp.dot(
        terms(jnp.concatenate(every), count), pick, preferred_element_type=jnp.float32
    ).reshape(count, parts * rows, LANES)
    low_rank = sum(summed[k] for k in range(count)).T
    for turn in range(parts):
        share = low_rank[0:rank, turn * rows : (turn + 1) * rows]
        after[turn][...] = share + before[turn][...] if before else share


def in_vmem(x):
    return pltpu.with_memory_space_constraint(x, pltpu.VMEM)


def project(pieces, shifts, stride, start, width, tokens, bounds, before, near):
    parts, rank = bounds.shape[0], pieces[0].shape[1]
    rows = tokens.shape[0] // parts
    if near:
        tokens, bounds = in_vmem(tokens), in_vmem(bounds)
        before = [in_vmem(x) for x in before]
    return pl.pallas_call(
        functools.partial(project_kernel, shifts, parts, stride, start, width),
        in_specs=[pl.BlockSpec(memory_space=pltpu.VMEM)] * (2 + len(pieces) + len(before)),
        out_shape=[jax.ShapeDtypeStruct((rank, rows), jnp.float32)] * parts,
        compiler_params=SMALL,
        name="project",
    )(tokens, bounds, *pieces, *before)


def finish_kernel(count, steps, bounds, *refs):
    shares, rest = refs[:count], refs[count:]
    bases, ups, outs, makes, square, sems = rest[0:2], rest[2:4], rest[4:6], rest[6:8], *rest[8:]
    rank, rows = shares[0].shape
    low_rank = shares[0][...]
    for share in shares[1:]:
        low_rank = low_rank + share[...]
    low_rank = turned(low_rank, square)[0:rows]
    own = bounds[lax.axis_index("tensor")]
    pick = rank_columns((LANES, own.shape[1]), 0, 1, rank).astype(jnp.bfloat16)
    spread = jnp.dot(terms(low_rank, 2), pick, preferred_element_type=jnp.float32)
    own = inside(own, rows)
    spread = jnp.where(jnp.concatenate([own, own]), spread, 0.0).astype(jnp.bfloat16)
    copies = []
    for step in range(steps):
        for k, (base, up, out, made) in enumerate(zip(bases, ups, outs, makes)):
            width = base.shape[1] // steps
            columns = pl.ds(step * width, width)
            update = jnp.dot(spread, up[:, columns], preferred_element_type=jnp.float32)
            update = update[0:rows] + update[rows:]
            made[:, columns] = (base[:, columns] + ADAPTER_SCALE * update).astype(made.dtype)
            copies.append(
                pltpu.make_async_copy(made.at[:, columns], out.at[:, columns], sems.at[k, step])
            )
            copies[-1].start()
    for copy in copies:
        copy.wait()


def finish(shares, bounds, operands, steps):
    operands = [in_vmem(x) for x in (bounds, *shares, *operands)]
    shapes = [x.shape for x in operands[-4:-2]]
    return pl.pallas_call(
        functools.partial(finish_kernel, len(shares), steps),
        in_specs=[pl.BlockSpec(memory_space=pltpu.VMEM)] * len(operands),
        out_specs=[pl.BlockSpec(memory_space=pl.ANY)] * 2,
        out_shape=[jax.ShapeDtypeStruct(shape, jnp.bfloat16) for shape in shapes],
        scratch_shapes=[pltpu.VMEM(shape, jnp.bfloat16) for shape in shapes]
        + [pltpu.VMEM((LANES, LANES), jnp.float32), pltpu.SemaphoreType.DMA((2, steps))],
        compiler_params=SMALL,
        name="finish",
    )(*operands)


def halving_order(total):
    bits = total.bit_length() - 1
    return [int(format(o, "b").zfill(bits)[::-1], 2) if bits else 0 for o in range(total)]


def reduce_blocks(partial, axis):
    step = 1
    while True:
        half = partial.shape[0] // 2
        came = swap(partial[half:], axis, step)
        if half == 1:
            return partial[0] + came[0]
        partial = partial[:half] + came
        step *= 2


def gather_blocks(x, axis):
    x = x[None]
    step = 1
    while step < lax.axis_size(axis):
        came = swap(x, axis, step)
        upper = (lax.axis_index(axis) & step) > 0
        x = jnp.concatenate([jnp.where(upper, came, x), jnp.where(upper, x, came)])
        step *= 2
    return x


def local(
    tokens,
    task_counts,
    task_embeddings,
    embedding_weight,
    down_factor_head,
    query_up_head,
    value_up_head,
    w_query,
    w_value,
):
    groups, ring, parts = lax.axis_size("groups"), lax.axis_size("task"), lax.axis_size("tensor")
    places = groups * ring
    tok_rows, shard_width = tokens.shape
    block_rows = tok_rows // parts
    own_tasks = task_counts.shape[0]
    block_tasks = own_tasks // parts
    rank = query_up_head.shape[1]
    hidden_rows = down_factor_head.shape[0]
    tensor = lax.axis_index("tensor")
    ring_shifts = list(range(ring))
    far_first = sorted(ring_shifts[1:], reverse=True)
    shifts = list(range(places))

    heads = {
        "value": Head(value_up_head, 1),
        "query": Head(query_up_head, 1),
        "down": Head(down_factor_head, 2),
    }

    def fetch(name, chunk, ahead=()):
        head, got = heads[name], {}
        for s in ahead:
            start = (place() ^ s) * head.stride
            piece = lax.dynamic_slice_in_dim(head.head, start, head.width, axis=2)
            got[s] = swap(piece, "task", s)
        rest = [s for s in far_first + [0] if s not in ahead]
        for s, piece in zip(rest, head.cut(chunk, rest)):
            got[s] = swap(piece, "task", s) if s else piece
        return jnp.concatenate([got[s] for s in ring_shifts], axis=0)

    fetched = {}
    ahead = far_first[:1] if heads["query"].by_lane else []
    fetched["query", 0] = fetch("query", 0, ahead)

    share = own_tasks // parts
    embeddings = lax.dynamic_index_in_dim(
        task_embeddings.reshape(parts, share, -1), tensor, 0, keepdims=False
    )
    hidden = jax.nn.silu(
        jnp.dot(embeddings, embedding_weight, preferred_element_type=jnp.float32)
    ).astype(jnp.bfloat16)
    far, came = ring // 2, [0, ring // 2]
    ring_hidden = jnp.concatenate([hidden[None], swap(hidden[None], "task", far)])
    while far > 1:
        far //= 2
        ring_hidden = jnp.concatenate([ring_hidden, swap(ring_hidden, "task", far)])
        came = came + [s ^ far for s in came]
    ring_hidden = jnp.stack([ring_hidden[came.index(s)] for s in ring_shifts])
    group_hidden = jnp.concatenate(
        [ring_hidden] + [swap(ring_hidden, "groups", s) for s in range(1, groups)]
    )
    every_hidden = gather_blocks(group_hidden.reshape(places * share, -1), "tensor")
    every_hidden = every_hidden.reshape(parts, places, share, ring, hidden_rows)
    every_hidden = every_hidden.transpose(3, 1, 0, 2, 4)
    every_hidden = every_hidden.reshape(ring, places * own_tasks, hidden_rows)
    every_hidden = jnp.concatenate(
        [
            lax.dynamic_index_in_dim(every_hidden, lax.axis_index("task") ^ s, 0, keepdims=False)
            for s in ring_shifts
        ],
        axis=1,
    )

    chunks = heads["down"].chunks
    for chunk in range(chunks):
        fetched["down", chunk] = fetch("down", chunk)
    fetched["value", 0] = fetch("value", 0)

    def emit(name, chunk):
        matrix = fetched[name, chunk]
        flat = jnp.dot(
            every_hidden, matrix.reshape(matrix.shape[0], -1), preferred_element_type=jnp.float32
        ).astype(jnp.bfloat16)
        return flat.reshape((places, own_tasks) + matrix.shape[1:])

    def send(made, sent):
        return {s: swap(made[s], PLACES, s) if s else made[s] for s in sent}

    crossing = [s for s in shifts if s % ring >= ring // 2]
    crossing = sorted(crossing, key=lambda s: (s < ring, s if s < ring else -s))
    late = crossing[-1:]
    near = [s for s in reversed(shifts) if s % ring < ring // 2]
    early = sorted(near, key=lambda s: s % ring == 0) + crossing[:-1]
    emitted = {}
    for name, chunk in [("query", 0), ("value", 0)] + [("down", c) for c in range(chunks)]:
        made = emit(name, chunk)
        emitted[name, chunk] = send(made, early)
        emitted[name, chunk].update(send(made, late))

    def ordered(pieces):
        return [pieces[s] for s in shifts]

    token_blocks = tokens.reshape(parts, block_rows, shard_width)
    order = halving_order(parts)
    turned = jnp.concatenate(
        [lax.dynamic_index_in_dim(token_blocks, tensor ^ s, 0, keepdims=False) for s in order]
    )
    base_query = jnp.dot(turned, w_query, preferred_element_type=jnp.float32)
    base_value = jnp.dot(turned, w_value, preferred_element_type=jnp.float32)
    base_query = reduce_blocks(base_query.reshape(parts, block_rows, -1), "tensor")
    base_value = reduce_blocks(base_value.reshape(parts, block_rows, -1), "tensor")

    def own_block(factors, above, below):
        moved = lax.all_to_all(factors, "tensor", split_axis=0, concat_axis=0, tiled=True)
        moved = moved.reshape(parts, block_tasks, rank, -1).transpose(1, 2, 0, 3)
        moved = moved.reshape(block_tasks, rank, -1)
        moved = jnp.pad(moved, ((0, 0), (above, below), (0, 0)))
        return moved.reshape(block_tasks * 2 * rank, -1)

    query_up_factors = heads["query"].join(ordered(emitted["query", 0]), shifts)
    own_query = own_block(query_up_factors, 0, rank)
    value_up_factors = heads["value"].join(ordered(emitted["value", 0]), shifts)
    own_value = own_block(value_up_factors, rank, 0)

    tallies = task_counts.reshape(parts, block_tasks)
    ends = jnp.cumsum(tallies, axis=1)
    begins = ends - tallies
    bounds = jnp.repeat(jnp.stack([begins, ends], axis=1), 2 * rank, axis=2)

    down_factors, low_rank = None, []
    head = heads["down"]
    if head.by_lane:
        for chunk in range(chunks):
            pieces, start = emitted["down", chunk], chunk * head.width
            for half in [early, late] if chunk + 1 == chunks else [early + late]:
                some = [pieces[s] for s in half]
                low_rank = project(
                    some, half, head.stride, start, head.width, tokens, bounds, low_rank,
                    half is late,
                )
            down_factors = head.join(
                [pieces[s] for s in early + late], early + late, chunk, down_factors
            )
    else:
        down_factors = head.join(ordered(emitted["down", 0]), shifts)
        projected = jnp.einsum(
            "bpd,bmd->bpm",
            token_blocks,
            down_factors.reshape(parts, block_tasks * 2 * rank, shard_width),
            preferred_element_type=jnp.float32,
        )
        projected = jnp.where(jax.vmap(lambda b: inside(b, block_rows))(bounds), projected, 0.0)
        projected = projected.reshape(parts, block_rows, block_tasks, 2 * rank).sum(axis=2)
        projected = projected.transpose(0, 2, 1)
        low_rank = [
            lax.dynamic_index_in_dim(projected, tensor ^ s, 0, keepdims=False)
            for s in range(parts)
        ]
    turns = sorted(range(1, parts), key=lambda s: s == 1)
    shares = [low_rank[0]] + [swap(low_rank[s], "tensor", s) for s in turns]
    query, value = finish(shares, bounds, [base_query, base_value, own_query, own_value], steps=2)
    return query, value, down_factors, query_up_factors, value_up_factors


def solution(mesh):
    return jax.shard_map(
        local,
        mesh=mesh,
        in_specs=(
            P(("groups", "task"), "tensor"),
            P(("groups", "task")),
            P(("groups", "task"), None),
            P(),
            P("task", None, "tensor"),
            P("task", None, "tensor"),
            P("task", None, "tensor"),
            P("tensor", None),
            P("tensor", None),
        ),
        out_specs=(
            P(("groups", "task", "tensor"), None),
            P(("groups", "task", "tensor"), None),
            P(("groups", "task"), None, "tensor"),
            P(("groups", "task"), None, "tensor"),
            P(("groups", "task"), None, "tensor"),
        ),
        check_vma=False,
    )
```
